256 devices in a mesh: seq: 32 (over x, z_lo, core), head: 4 (over y), phase: 2 (over z_hi).
Axes of the slice: x: 4, y: 4, z: 8 (z_hi: 2, z_lo: 4; z = z_hi * 4 + z_lo), core: 2. Of those that a mesh axis runs over, the one named last changes fastest.
Arguments:
- queries: bfloat16 [32, 2, 64, 8192], P('seq', None, None, ('head', 'phase')), may hold values from -96 to 96
- keys: bfloat16 [32, 2, 64, 1024], P('seq', None, None, ('head', 'phase')), may hold values from -4 to 4
- values: bfloat16 [32, 2, 64, 1024], P('seq', None, None, ('head', 'phase')), may hold values from -6 to 6
- out_weight: bfloat16 [8192, 16384], P(('head', 'phase'), 'seq'), may hold values from -0.0625 to 0.0625
- block_vis: int32 [32, 32], replicated, may hold values from 0 to 1, as said below
- seg_lengths: int32 [10], replicated, may hold values from 1 to 1024, 4096 in all
Outputs:
- judged: bfloat16 [4096, 16384], P(('head', 'phase'), 'seq')
The draws below stay inside these ranges and needn't reach their ends.
Inputs may be any that keep to these rules, and one draw needn't show every extreme that they name: block_vis[i, i] = 1 and block_vis[i, j] = 0 for j > i. `seg_lengths`: the prompt, the candidate answers and the verdict, in order; they sum to 4096.
All inputs are finite; a program needn't handle non-finite values.
Results may differ from the reference program's by a relative error of at most 0.018.
Values may be sent and summed in bfloat16 or wider, within the bound.
No kernel may reach another device: no remote copies, remote signals or barrier semaphores. Data moves between devices by JAX's collectives and lax.ppermute only.
A program may use at most 64 MiB of HBM per device.

```python
import math
import jax
import jax.numpy as jnp
import numpy as np
from jax import lax

D = 16384
KVH = 8
QPK = 8
HD = 128
BLK = 128
SEGS = 10
SPAN = 64
TOKENS = 4096
NB = 32
HQ = 64
GROUPS = 8
N_SEQ = 32


def draw_pair(key):
    base = jax.random.fold_in(key, 7)
    key_shape = (N_SEQ, 2, SPAN, KVH * HD)
    query_shape = (N_SEQ, 2, SPAN, KVH, QPK, HD)
    key_vals = jnp.clip(jax.random.normal(jax.random.fold_in(base, 1), key_shape, jnp.float32), -4.0, 4.0)
    query_vals = jnp.clip(jax.random.normal(jax.random.fold_in(base, 2), query_shape, jnp.float32), -4.0, 4.0)
    return (query_vals.reshape(N_SEQ, 2, SPAN, KVH * QPK * HD), key_vals)


def draw_queries(key, part):
    query_vals, key_vals = draw_pair(key)
    return query_vals.astype(jnp.bfloat16)


def draw_keys(key, part):
    query_vals, key_vals = draw_pair(key)
    return key_vals.astype(jnp.bfloat16)


def draw_block_vis(key, part):
    coins = jax.random.randint(jax.random.fold_in(key, 3), (NB, NB), 0, 5)
    rows = jnp.arange(NB, dtype=jnp.int32)[:, None]
    cols = jnp.arange(NB, dtype=jnp.int32)[None, :]
    lower = (coins < 3).astype(jnp.int32)
    return jnp.where(cols < rows, lower, jnp.where(cols == rows, 1, 0)).astype(jnp.int32)


def block_levels(own_key, extent, cuts, low, largest):
    loudness, own = 1.0, jax.random.fold_in(own_key, 6)
    for axis_at, blocks in cuts:
        steps = jnp.exp(jax.random.uniform(jax.random.fold_in(own, axis_at), (blocks,), jnp.float32, low / len(cuts), largest / len(cuts)))
        loudness = loudness * jnp.repeat(steps, extent[axis_at] // blocks).reshape([-1 if axis == axis_at else 1 for axis in range(len(extent))])
    return loudness


def length_profile(count, total, bound, skew):
    loads = [(1 << 20) // math.isqrt(standing ** skew) + 1 for standing in range(2, count + 1)]
    rest, given = total - bound - (count - 1), [1] * (count - 1)
    while rest > 0:
        candidates = [i for i in range(count - 1) if given[i] < bound]
        mass, left = sum([loads[i] for i in candidates]), rest
        for i in candidates:
            extra = min(bound - given[i], max(1, left * loads[i] // mass), rest)
            given[i] = given[i] + extra
            rest = rest - extra
    return np.array([bound] + given)


def uneven(own_key, number_of, total, limit, slope):
    if number_of == 2:
        one = jax.random.randint(own_key, (), max(1, total - limit), min(limit, total - 1) + 1)
        return jnp.stack([one, total - one])
    lengths = jnp.asarray(length_profile(number_of, total, limit, slope), jnp.int32)
    pairs = (number_of - 1) // 2
    giver, taker = lengths[1:1 + 2 * pairs:2], lengths[2:2 + 2 * pairs:2]
    margin = jnp.minimum(giver - 1, limit - taker)
    passed = jax.random.randint(jax.random.fold_in(own_key, 1), (pairs,), 0, 1 << 20) % (margin + 1)
    lengths = lengths.at[1:1 + 2 * pairs:2].set(giver - passed).at[2:2 + 2 * pairs:2].set(taker + passed)
    return lengths[jax.random.permutation(jax.random.fold_in(own_key, 2), number_of)]


def noise(own_key, extent, scale, reach, split=(), held_as=jnp.bfloat16):
    entries = jax.random.normal(own_key, extent, jnp.float32) * scale
    if len(split) > 0:
        entries = block_levels(own_key, extent, split, -0.22, 0.18) * entries
    return jnp.clip(entries, min=-reach, max=reach).astype(held_as)


def setup_inputs(seed: int = 0) -> dict:
    key_of = jax.random.split(jax.random.key(seed), 7)
    queries = draw_queries(jax.random.fold_in(key_of[6], 71), 0)
    keys = draw_keys(jax.random.fold_in(key_of[6], 71), 0)
    values = noise(key_of[2], (N_SEQ, 2, SPAN, KVH * HD), 1.0, 6.0, ((0, 32), (3, 8)))
    out_weight = noise(key_of[3], (HQ * HD, D), (HQ * HD) ** -0.5, 0.0625, ((0, 8), (1, 32)))
    block_vis = draw_block_vis(jax.random.fold_in(key_of[6], 71), 0)
    seg_lengths = uneven(key_of[5], SEGS, TOKENS, TOKENS // 4, 1).astype(jnp.int32)
    return {"queries": queries, "keys": keys, "values": values, "out_weight": out_weight, "block_vis": block_vis, "seg_lengths": seg_lengths}


def in_order(stacked):
    first_half = stacked[:, 0]
    second_half = jnp.flip(stacked[:, 1], 0)
    joined = jnp.concatenate([first_half, second_half], 0)
    return joined.reshape(-1, stacked.shape[-1])


def segment_of(places, starts):
    return jnp.sum((starts[None, 1:] <= places[:, None]).astype(jnp.int32), axis=1)


def reference(queries, keys, values, out_weight, block_vis, seg_lengths):
    query_rows = in_order(queries)
    key_rows = in_order(keys)
    value_rows = in_order(values)
    places = jnp.arange(TOKENS, dtype=jnp.int32)
    starts = jnp.cumsum(seg_lengths) - seg_lengths
    segment = segment_of(places, starts)
    blocks = places // BLK
    visible = block_vis[blocks][:, blocks] == 1
    causal = places[None, :] <= places[:, None]
    seg_ok = (segment[None, :] == 0) | (segment[None, :] == segment[:, None]) | (segment[:, None] == SEGS - 1)
    allowed = visible & causal & seg_ok
    scale = 1.0 / (HD ** 0.5)

    def one_head(head_id):
        kv_head = head_id // QPK
        query_head = lax.dynamic_slice_in_dim(query_rows, head_id * HD, HD, 1).astype(jnp.float32)
        key_head = lax.dynamic_slice_in_dim(key_rows, kv_head * HD, HD, 1).astype(jnp.float32)
        value_head = lax.dynamic_slice_in_dim(value_rows, kv_head * HD, HD, 1)
        scores = jnp.dot(query_head, key_head.T, precision=lax.Precision.HIGHEST, preferred_element_type=jnp.float32) * scale
        peak = jnp.max(jnp.where(allowed, scores, jnp.float32(-1e30)), axis=1, keepdims=True)
        weight = jnp.where(allowed, jnp.exp(scores - peak), jnp.float32(0.0))
        total = jnp.sum(weight, axis=1, keepdims=True)
        mixed = jnp.dot(weight.astype(jnp.bfloat16), value_head, preferred_element_type=jnp.float32)
        return (mixed / total).astype(jnp.bfloat16)

    heads = lax.map(one_head, jnp.arange(HQ, dtype=jnp.int32))
    head_out = jnp.transpose(heads, (1, 0, 2)).reshape(TOKENS, HQ * HD)
    width = HQ * HD // GROUPS

    def add_group(group_id, running):
        rows = lax.dynamic_slice_in_dim(head_out, group_id * width, width, 1)
        weight_rows = lax.dynamic_slice_in_dim(out_weight, group_id * width, width, 0)
        partial_value = jnp.dot(rows, weight_rows, preferred_element_type=jnp.float32).astype(jnp.bfloat16)
        partial_value = lax.optimization_barrier(partial_value)
        return running + partial_value.astype(jnp.float32)

    summed = lax.fori_loop(0, GROUPS, add_group, jnp.zeros((TOKENS, D), jnp.float32))
    return summed.astype(jnp.bfloat16)
```

```python
import functools
import math

import jax
import jax.numpy as jnp
from jax import lax
from jax.experimental import pallas as pl
from jax.experimental.pallas import tpu as pltpu
from jax.sharding import PartitionSpec as P

HD = 128
BLK = 128
SEGS = 10
SPAN = 64
NX, NZ, NC = 4, 4, 2
NY = 4
HEADS = 8
NEG = -1e30
HIDDEN = 1 << 20
TILES = 17


def places_of_seq(shift_x=0, flip_z=0, flip_core=0):
    pairs = []
    for x in range(NX):
        for z in range(NZ):
            for c in range(NC):
                src = (x * NZ + z) * NC + c
                dst = (((x - shift_x) % NX) * NZ + (z ^ flip_z)) * NC + (c ^ flip_core)
                pairs.append((src, dst))
    return pairs


def from_seq(a, **kw):
    return lax.ppermute(a, "seq", places_of_seq(**kw))


def gather_z(a):
    return jnp.stack([a] + [from_seq(a, flip_z=k) for k in (1, 2, 3)], 0)


def gather_x(a):
    return jnp.stack([a] + [from_seq(a, shift_x=k) for k in (1, 2, 3)], 0)


def attention_kernel(
    sc, q_ref, kva, kvb, kcode, kpos, qseg, qlim, qpos, send_ref, keep_ref, sbuf, qs, mx, acc, tot
):
    gs, my_x, my_zh, keep_member = sc[0], sc[1], sc[2], sc[3]
    rows = HEADS * SPAN
    for m in range(2):
        for h in range(HEADS):
            qs[m, h * SPAN:(h + 1) * SPAN, :] = q_ref[m, :, h * HD:(h + 1) * HD]
    mx[...] = jnp.full_like(mx, NEG)
    acc[...] = jnp.zeros_like(acc)
    tot[...] = jnp.zeros_like(tot)

    def tile_of(t):
        if t < 8:
            return 1, 0, t
        u = t - 8
        early = u <= gs
        mq = jnp.where(early, 0, 1)
        mk = jnp.where(early, 0, 1)
        g = jnp.where(early, u, u - 1)
        g_rel = (((g >> 1) - my_x) & 3) * 2 + ((g & 1) ^ my_zh)
        return mq, mk, g_rel

    def rows_of(kv, mk, g):
        return jnp.concatenate(
            [kva[2 * g, kv, mk], kva[2 * g + 1, kv, mk], kvb[2 * g, kv, mk], kvb[2 * g + 1, kv, mk]], 0
        )

    for t in range(TILES):
        mq, mk, g = tile_of(t)
        s = lax.dot_general(
            qs[mq], rows_of(0, mk, g), (((1,), (1,)), ((), ())), preferred_element_type=jnp.float32
        )
        code = kcode[(mq * 2 + mk) * 8 + g]
        ok = ((code == qseg[mq]) | (code <= qlim[mq])) & (kpos[mk * 8 + g] <= qpos[mq])
        s = jnp.where(ok[None], s.reshape(HEADS, SPAN, 256), NEG).reshape(rows, 256)
        sbuf[t] = s
        mx[mq] = jnp.maximum(mx[mq], jnp.maximum(s[:, :HD], s[:, HD:]))
    for m in range(2):
        mx[m] = jnp.broadcast_to(jnp.max(mx[m], axis=1, keepdims=True), (rows, HD))
    factor = math.log2(math.e) / math.sqrt(HD)
    for t in range(TILES):
        mq, mk, g = tile_of(t)
        peak = mx[mq]
        s = sbuf[t]
        w = jnp.exp2((s - jnp.concatenate([peak, peak], 1)) * factor)
        tot[mq] += w[:, :HD] + w[:, HD:]
        acc[mq] += jnp.dot(
            w.astype(jnp.bfloat16), rows_of(1, mk, g), preferred_element_type=jnp.float32
        )
    for m in range(2):
        total = jnp.sum(tot[m], axis=1, keepdims=True)
        out = (acc[m] / total).astype(jnp.bfloat16)

        @pl.when(keep_member == m)
        def _():
            for h in range(HEADS):
                keep_ref[:, h * HD:(h + 1) * HD] = out[h * SPAN:(h + 1) * SPAN]

        @pl.when(keep_member != m)
        def _():
            for h in range(HEADS):
                send_ref[:, h * HD:(h + 1) * HD] = out[h * SPAN:(h + 1) * SPAN]


def project_kernel(slots, a_ref, woo, wpo, woc, wpc, c_ref):
    a = a_ref[0]
    own = a[:, 0].reshape(NZ * SPAN, HEADS * HD)
    other = a[:, 1].reshape(NZ * SPAN, HEADS * HD)

    def mix(w_own, w_other):
        return (
            jnp.dot(own, w_own[...], preferred_element_type=jnp.float32)
            + jnp.dot(other, w_other[...], preferred_element_type=jnp.float32)
        ).astype(jnp.bfloat16)

    c_ref[0, 0] = mix(woo, wpo)
    c_ref[0, 1] = mix(woc, wpc)


def place_kernel(spots, p0, u1, u2, u3, other, o_ref):
    i = pl.program_id(0)

    @pl.when(i < NZ)
    def _():
        o_ref[...] = (
            p0[0, 0].astype(jnp.float32)
            + u1[0].astype(jnp.float32)
            + u2[0].astype(jnp.float32)
            + u3[0].astype(jnp.float32)
        ).astype(jnp.bfloat16)

    @pl.when(i >= NZ)
    def _():
        o_ref[...] = other[...]


def per_device(queries, keys, values, out_weight, block_vis, seg_lengths):
    seq = lax.axis_index("seq")
    phase = lax.axis_index("phase")
    head = lax.axis_index("head")
    my_x, my_z, my_c = seq // 8, (seq // 2) % 4, seq % 2

    kv = jnp.stack([keys.reshape(2, SPAN, HD), values.reshape(2, SPAN, HD)], 0)
    kv_z = gather_z(kv)
    kv_z, weight = lax.optimization_barrier((kv_z, out_weight))
    kva = gather_x(kv_z).reshape(NX * NZ, 2, 2, SPAN, HD)
    kvb = from_seq(kva, flip_core=1)

    weight_p = lax.ppermute(weight, "phase", [(0, 1), (1, 0)])
    weight_oc = from_seq(weight, flip_core=1)
    weight_pc = from_seq(weight_p, flip_core=1)

    tri = jnp.arange(SEGS)[None, :] < jnp.arange(SEGS)[:, None]
    starts = jnp.sum(jnp.where(tri, seg_lengths[None, :], 0), axis=1)

    def segment(pos):
        return jnp.sum((starts[1:] <= pos[..., None]).astype(jnp.int32), axis=-1)

    two = jnp.arange(2, dtype=jnp.int32)
    my_spans = jnp.where(two == 0, seq, 63 - seq)
    q_pos = my_spans[:, None] * SPAN + jnp.arange(SPAN, dtype=jnp.int32)
    q_seg = segment(q_pos)
    q_lim = jnp.where(q_seg == SEGS - 1, SEGS - 1, 0)
    g = jnp.arange(8, dtype=jnp.int32)
    key_x = (my_x + g // 2) & 3
    pair = jnp.arange(2, dtype=jnp.int32)
    key_z = my_z ^ ((g % 2)[:, None] * 2 + pair)
    key_s = key_x[:, None, None] * 8 + key_z[:, None, :] * 2 + (my_c ^ pair)[None, :, None]
    key_span = jnp.where(two[:, None, None, None] == 0, key_s[None], 63 - key_s[None])
    key_span = key_span.reshape(2, 8, 4)
    k_pos = (key_span[..., None] * SPAN + jnp.arange(SPAN, dtype=jnp.int32)).reshape(2, 8, 256)
    k_seg = segment(k_pos)
    blocks = jnp.arange(block_vis.shape[0], dtype=jnp.int32)
    vis_rows = jnp.sum(
        jnp.where(((my_spans // 2)[:, None] == blocks)[..., None], block_vis[None], 0), axis=1
    )
    seen = jnp.sum(
        jnp.where((key_span // 2)[None, ..., None] == blocks, vis_rows[:, None, None, None, :], 0),
        axis=-1,
    )
    seen = jnp.repeat(seen, SPAN, axis=-1).reshape(2, 2, 8, 256)
    k_code = jnp.where(seen == 1, k_seg[None], HIDDEN).reshape(32, 1, 256)
    k_pos = k_pos.reshape(16, 1, 256)
    wide = lambda v: jnp.broadcast_to(v[..., None], (2, SPAN, 256))
    scalars = jnp.stack([seq // 4, my_x, my_z // 2, (my_x + phase) % 2])

    rows = HEADS * SPAN
    vmem = pl.BlockSpec(memory_space=pltpu.VMEM)
    half = jax.ShapeDtypeStruct((SPAN, HEADS * HD), jnp.bfloat16)
    send, keep = pl.pallas_call(
        attention_kernel,
        name="attention",
        out_shape=(half, half),
        in_specs=[pl.BlockSpec(memory_space=pltpu.SMEM)] + [vmem] * 8,
        out_specs=(vmem, vmem),
        scratch_shapes=[
            pltpu.VMEM((TILES, rows, 256), jnp.float32),
            pltpu.VMEM((2, rows, HD), jnp.bfloat16),
            pltpu.VMEM((2, rows, HD), jnp.float32),
            pltpu.VMEM((2, rows, HD), jnp.float32),
            pltpu.VMEM((2, rows, HD), jnp.float32),
        ],
        compiler_params=pltpu.CompilerParams(vmem_limit_bytes=40 << 20),
    )(scalars, queries.reshape(2, SPAN, HEADS * HD), kva, kvb, k_code, k_pos, wide(q_seg), wide(q_lim), wide(q_pos))

    got = lax.ppermute(send, "phase", [(0, 1), (1, 0)])
    mine = jnp.stack([keep, got], 0)
    gathered = gather_x(gather_z(mine))

    y_of = (head + jnp.arange(NY, dtype=jnp.int32)) % NY
    block = 2 * y_of + phase
    x_of = jnp.where(block < 4, block, 7 - block)
    slots = (x_of - my_x) & 3
    w_spec = pl.BlockSpec((HEADS * HD, 512), lambda k, s: (0, 0))
    partial = pl.pallas_call(
        project_kernel,
        name="project",
        out_shape=jax.ShapeDtypeStruct((NY, 2, NZ * SPAN, 512), jnp.bfloat16),
        grid_spec=pltpu.PrefetchScalarGridSpec(
            num_scalar_prefetch=1,
            grid=(NY,),
            in_specs=[
                pl.BlockSpec((1, NZ, 2, SPAN, HEADS * HD), lambda k, s: (s[k], 0, 0, 0, 0)),
                w_spec, w_spec, w_spec, w_spec,
            ],
            out_specs=pl.BlockSpec((1, 2, NZ * SPAN, 512), lambda k, s: (k, 0, 0, 0)),
        ),
        compiler_params=pltpu.CompilerParams(vmem_limit_bytes=40 << 20),
    )(slots, gathered, weight, weight_p, weight_oc, weight_pc)

    def up(k):
        return lax.ppermute(partial[k], "head", [(y, (y + k) % NY) for y in range(NY)])

    u1, u2, u3 = up(1), up(2), up(3)
    f32 = jnp.float32
    for_other = (
        partial[0, 1].astype(f32) + u1[1].astype(f32) + u2[1].astype(f32) + u3[1].astype(f32)
    ).astype(jnp.bfloat16)
    from_other = from_seq(for_other, flip_core=1)

    my_block = 2 * head + phase
    z_of = my_z ^ jnp.arange(NZ, dtype=jnp.int32)
    place = jnp.concatenate([2 * z_of + my_c, 2 * z_of + (1 - my_c)])
    spots = jnp.where(my_block < 4, place, 7 - place)
    near = lambda i, s: (0, jnp.minimum(i, NZ - 1), 0)
    return pl.pallas_call(
        place_kernel,
        name="place",
        out_shape=jax.ShapeDtypeStruct((8 * SPAN, 512), jnp.bfloat16),
        grid_spec=pltpu.PrefetchScalarGridSpec(
            num_scalar_prefetch=1,
            grid=(2 * NZ,),
            in_specs=[
                pl.BlockSpec((1, 1, SPAN, 512), lambda i, s: (0, 0, jnp.minimum(i, NZ - 1), 0)),
                pl.BlockSpec((1, SPAN, 512), near),
                pl.BlockSpec((1, SPAN, 512), near),
                pl.BlockSpec((1, SPAN, 512), near),
                pl.BlockSpec((SPAN, 512), lambda i, s: (jnp.maximum(i - NZ, 0), 0)),
            ],
            out_specs=pl.BlockSpec((SPAN, 512), lambda i, s: (s[i], 0)),
        ),
    )(spots, partial, u1, u2, u3, from_other)


def solution(mesh):
    return jax.shard_map(
        per_device,
        mesh=mesh,
        in_specs=(
            P("seq", None, None, ("head", "phase")),
            P("seq", None, None, ("head", "phase")),
            P("seq", None, None, ("head", "phase")),
            P(("head", "phase"), "seq"),
            P(),
            P(),
        ),
        out_specs=P(("head", "phase"), "seq"),
        check_vma=False,
    )
```

```python
import functools
import math

import jax
import jax.numpy as jnp
from jax import lax
from jax.experimental import pallas as pl
from jax.experimental.pallas import tpu as pltpu
from jax.sharding import PartitionSpec as P

HD = 128
BLK = 128
SEGS = 10
SPAN = 64
HALF = 32
NX, NZ, NC = 4, 4, 2
NY = 4
HEADS = 8
NEG = -1e30
HIDDEN = 1 << 20
TILES = 17


def places_of_seq(shift_x=0, flip_z=0, flip_core=0):
    pairs = []
    for x in range(NX):
        for z in range(NZ):
            for c in range(NC):
                src = (x * NZ + z) * NC + c
                dst = (((x - shift_x) % NX) * NZ + (z ^ flip_z)) * NC + (c ^ flip_core)
                pairs.append((src, dst))
    return pairs


def from_seq(a, **kw):
    return lax.ppermute(a, "seq", places_of_seq(**kw))


def gather_z(a):
    return jnp.stack([a] + [from_seq(a, flip_z=k) for k in (1, 2, 3)], 0)


def over_x(a):
    return [a] + [from_seq(a, shift_x=k) for k in (1, 2, 3)]


def attention_kernel(
    sc, q_ref, kva, kvb, kcode, kpos, qseg, qlim, qpos, send_ref, keep_ref, sbuf, qs, mx, acc, tot
):
    gs, my_x, my_zh, keep_member = sc[0], sc[1], sc[2], sc[3]
    rows = HEADS * SPAN
    for m in range(2):
        for h in range(HEADS):
            qs[m, h * SPAN:(h + 1) * SPAN, :] = q_ref[m, :, h * HD:(h + 1) * HD]
    mx[...] = jnp.full_like(mx, NEG)
    acc[...] = jnp.zeros_like(acc)
    tot[...] = jnp.zeros_like(tot)

    def tile_of(t):
        if t < 8:
            return 1, 0, t
        u = t - 8
        early = u <= gs
        mq = jnp.where(early, 0, 1)
        mk = jnp.where(early, 0, 1)
        g = jnp.where(early, u, u - 1)
        g_rel = (((g >> 1) - my_x) & 3) * 2 + ((g & 1) ^ my_zh)
        return mq, mk, g_rel

    def rows_of(kv, mk, g):
        return jnp.concatenate(
            [kva[2 * g, kv, mk], kva[2 * g + 1, kv, mk], kvb[2 * g, kv, mk], kvb[2 * g + 1, kv, mk]], 0
        )

    for t in range(TILES):
        mq, mk, g = tile_of(t)
        s = lax.dot_general(
            qs[mq], rows_of(0, mk, g), (((1,), (1,)), ((), ())), preferred_element_type=jnp.float32
        )
        code = kcode[(mq * 2 + mk) * 8 + g]
        ok = ((code == qseg[mq]) | (code <= qlim[mq])) & (kpos[mk * 8 + g] <= qpos[mq])
        s = jnp.where(ok[None], s.reshape(HEADS, SPAN, 256), NEG).reshape(rows, 256)
        sbuf[t] = s
        mx[mq] = jnp.maximum(mx[mq], jnp.maximum(s[:, :HD], s[:, HD:]))
    for m in range(2):
        mx[m] = jnp.broadcast_to(jnp.max(mx[m], axis=1, keepdims=True), (rows, HD))
    factor = math.log2(math.e) / math.sqrt(HD)
    for t in range(TILES):
        mq, mk, g = tile_of(t)
        peak = mx[mq]
        s = sbuf[t]
        w = jnp.exp2((s - jnp.concatenate([peak, peak], 1)) * factor)
        tot[mq] += w[:, :HD] + w[:, HD:]
        acc[mq] += jnp.dot(
            w.astype(jnp.bfloat16), rows_of(1, mk, g), preferred_element_type=jnp.float32
        )
    for m in range(2):
        total = jnp.sum(tot[m], axis=1, keepdims=True)
        out = (acc[m] / total).astype(jnp.bfloat16)

        @pl.when(keep_member == m)
        def _():
            for h in range(HEADS):
                keep_ref[:, h * HD:(h + 1) * HD] = out[h * SPAN:(h + 1) * SPAN]

        @pl.when(keep_member != m)
        def _():
            for h in range(HEADS):
                send_ref[:, h * HD:(h + 1) * HD] = out[h * SPAN:(h + 1) * SPAN]


def project_kernel(where, *refs):
    keeps, gots, (woo, wpo, woc, wpc), c_ref = refs[0:NX], refs[NX:2 * NX], refs[2 * NX:2 * NX + 4], refs[-1]
    step = pl.program_id(0)

    def fill(w_own, w_other):
        for j in range(NX):
            own = keeps[j][...].reshape(NZ * HALF, HEADS * HD)
            other = gots[j][...].reshape(NZ * HALF, HEADS * HD)
            c_ref[where[j], 0] = (
                jnp.dot(own, w_own[...], preferred_element_type=jnp.float32)
                + jnp.dot(other, w_other[...], preferred_element_type=jnp.float32)
            ).astype(jnp.bfloat16)

    @pl.when(step < 2)
    def _():
        fill(woo, wpo)

    @pl.when(step >= 2)
    def _():
        fill(woc, wpc)


def place_kernel(spots, *refs):
    o_ref = refs[-1]
    for t in range(2):
        p0, u1, u2, u3, other = refs[5 * t:5 * t + 5]
        mine = (
            p0[0, 0].astype(jnp.float32)
            + u1[0].astype(jnp.float32)
            + u2[0].astype(jnp.float32)
            + u3[0].astype(jnp.float32)
        ).astype(jnp.bfloat16)
        theirs = other[...]
        for k in range(NZ):
            part = slice(k * HALF, (k + 1) * HALF)
            row = pl.multiple_of(spots[k] * SPAN + t * HALF, HALF)
            o_ref[pl.ds(row, HALF), :] = mine[part]
            row = pl.multiple_of(spots[NZ + k] * SPAN + t * HALF, HALF)
            o_ref[pl.ds(row, HALF), :] = theirs[part]


def per_device(queries, keys, values, out_weight, block_vis, seg_lengths):
    seq = lax.axis_index("seq")
    phase = lax.axis_index("phase")
    head = lax.axis_index("head")
    my_x, my_z, my_c = seq // 8, (seq // 2) % 4, seq % 2

    kv = jnp.stack([keys.reshape(2, SPAN, HD), values.reshape(2, SPAN, HD)], 0)
    kv_z = gather_z(kv)
    kv_x, weight_oc = lax.optimization_barrier((over_x(kv_z), from_seq(out_weight, flip_core=1)))
    kva = jnp.stack(kv_x, 0).reshape(NX * NZ, 2, 2, SPAN, HD)
    kvb = from_seq(kva, flip_core=1)

    tri = jnp.arange(SEGS)[None, :] < jnp.arange(SEGS)[:, None]
    starts = jnp.sum(jnp.where(tri, seg_lengths[None, :], 0), axis=1)

    def segment(pos):
        return jnp.sum((starts[1:] <= pos[..., None]).astype(jnp.int32), axis=-1)

    two = jnp.arange(2, dtype=jnp.int32)
    my_spans = jnp.where(two == 0, seq, 63 - seq)
    q_pos = my_spans[:, None] * SPAN + jnp.arange(SPAN, dtype=jnp.int32)
    q_seg = segment(q_pos)
    q_lim = jnp.where(q_seg == SEGS - 1, SEGS - 1, 0)
    g = jnp.arange(8, dtype=jnp.int32)
    key_x = (my_x + g // 2) & 3
    pair = jnp.arange(2, dtype=jnp.int32)
    key_z = my_z ^ ((g % 2)[:, None] * 2 + pair)
    key_s = key_x[:, None, None] * 8 + key_z[:, None, :] * 2 + (my_c ^ pair)[None, :, None]
    key_span = jnp.where(two[:, None, None, None] == 0, key_s[None], 63 - key_s[None])
    key_span = key_span.reshape(2, 8, 4)
    k_pos = (key_span[..., None] * SPAN + jnp.arange(SPAN, dtype=jnp.int32)).reshape(2, 8, 256)
    k_seg = segment(k_pos)
    blocks = jnp.arange(block_vis.shape[0], dtype=jnp.int32)
    vis_rows = jnp.sum(
        jnp.where(((my_spans // 2)[:, None] == blocks)[..., None], block_vis[None], 0), axis=1
    )
    seen = jnp.sum(
        jnp.where((key_span // 2)[None, ..., None] == blocks, vis_rows[:, None, None, None, :], 0),
        axis=-1,
    )
    seen = jnp.repeat(seen, SPAN, axis=-1).reshape(2, 2, 8, 256)
    k_code = jnp.where(seen == 1, k_seg[None], HIDDEN).reshape(32, 1, 256)
    k_pos = k_pos.reshape(16, 1, 256)
    wide = lambda v: jnp.broadcast_to(v[..., None], (2, SPAN, 256))
    scalars = jnp.stack([seq // 4, my_x, my_z // 2, (my_x + phase) % 2])

    rows = HEADS * SPAN
    vmem = pl.BlockSpec(memory_space=pltpu.VMEM)
    half = jax.ShapeDtypeStruct((SPAN, HEADS * HD), jnp.bfloat16)
    send, keep = pl.pallas_call(
        attention_kernel,
        name="attention",
        out_shape=(half, half),
        in_specs=[pl.BlockSpec(memory_space=pltpu.SMEM)] + [vmem] * 8,
        out_specs=(vmem, vmem),
        scratch_shapes=[
            pltpu.VMEM((TILES, rows, 256), jnp.float32),
            pltpu.VMEM((2, rows, HD), jnp.bfloat16),
            pltpu.VMEM((2, rows, HD), jnp.float32),
            pltpu.VMEM((2, rows, HD), jnp.float32),
            pltpu.VMEM((2, rows, HD), jnp.float32),
        ],
        compiler_params=pltpu.CompilerParams(vmem_limit_bytes=24 << 20),
    )(scalars, queries.reshape(2, SPAN, HEADS * HD), kva, kvb, k_code, k_pos, wide(q_seg), wide(q_lim), wide(q_pos))

    got = lax.ppermute(send, "phase", [(0, 1), (1, 0)])
    keep_z, got = lax.optimization_barrier((gather_z(keep), got))
    keep_x = over_x(keep_z)
    got_z = gather_z(got)

    got_z, weight = lax.optimization_barrier((got_z, out_weight))
    weight_p = lax.ppermute(weight, "phase", [(0, 1), (1, 0)])
    got_t = [got_z[:, :HALF], got_z[:, HALF:]]
    keep_x, got_t[0] = lax.optimization_barrier((keep_x, got_t[0]))
    got_x = over_x(got_t[0])
    got_x, got_t[1], weight_p = lax.optimization_barrier((got_x, got_t[1], weight_p))
    weight_pc = from_seq(weight_p, flip_core=1)
    got_x = [got_x, over_x(got_t[1])]

    steps = jnp.arange(NY, dtype=jnp.int32)
    x_of = (my_x + steps) & 3
    block = jnp.where((x_of + phase) % 2 == 0, x_of, 7 - x_of)
    where = (block // 2 - head) & 3
    my_block = 2 * head + phase
    z_of = my_z ^ steps
    place = jnp.concatenate([2 * z_of + my_c, 2 * z_of + (1 - my_c)])
    spots = jnp.where(my_block < 4, place, 7 - place)
    f32 = jnp.float32
    pieces = []
    for t in range(2):
        first = lambda i, s: (0, jnp.minimum(i, 1))
        last = lambda i, s: (0, jnp.maximum(i - 2, 0))
        wide_k = HEADS * HD
        partial = pl.pallas_call(
            project_kernel,
            name="project",
            out_shape=jax.ShapeDtypeStruct((NY, 2, NZ * HALF, 512), jnp.bfloat16),
            grid_spec=pltpu.PrefetchScalarGridSpec(
                num_scalar_prefetch=1,
                grid=(4,),
                in_specs=[pl.BlockSpec((NZ, HALF, wide_k), lambda i, s, t=t: (0, t, 0))] * NX
                + [pl.BlockSpec((NZ, HALF, wide_k), lambda i, s: (0, 0, 0))] * NX
                + [pl.BlockSpec((wide_k, 256), first)] * 2
                + [pl.BlockSpec((wide_k, 256), last)] * 2,
                out_specs=pl.BlockSpec((NY, 1, NZ * HALF, 256), lambda i, s: (0, i // 2, 0, i % 2)),
            ),
            compiler_params=pltpu.CompilerParams(vmem_limit_bytes=16 << 20),
        )(where, *keep_x, *got_x[t], weight, weight_p, weight_oc, weight_pc)
        ups = [
            lax.ppermute(partial[k], "head", [(y, (y + k) % NY) for y in range(NY)]) for k in (1, 2, 3)
        ]
        for_other = sum([u[1].astype(f32) for u in ups], partial[0, 1].astype(f32))
        from_other = from_seq(for_other.astype(jnp.bfloat16), flip_core=1)
        pieces += [partial, *ups, from_other]

    in_specs = []
    for t in range(2):
        in_specs += [pl.BlockSpec((1, 1, NZ * HALF, 512), lambda i, s: (0, 0, 0, 0))]
        in_specs += [pl.BlockSpec((1, NZ * HALF, 512), lambda i, s: (0, 0, 0))] * 3
        in_specs += [pl.BlockSpec((NZ * HALF, 512), lambda i, s: (0, 0))]
    return pl.pallas_call(
        place_kernel,
        name="place",
        out_shape=jax.ShapeDtypeStruct((8 * SPAN, 512), jnp.bfloat16),
        grid_spec=pltpu.PrefetchScalarGridSpec(
            num_scalar_prefetch=1,
            grid=(1,),
            in_specs=in_specs,
            out_specs=pl.BlockSpec((8 * SPAN, 512), lambda i, s: (0, 0)),
        ),
    )(spots, *pieces)


def solution(mesh):
    return jax.shard_map(
        per_device,
        mesh=mesh,
        in_specs=(
            P("seq", None, None, ("head", "phase")),
            P("seq", None, None, ("head", "phase")),
            P("seq", None, None, ("head", "phase")),
            P(("head", "phase"), "seq"),
            P(),
            P(),
        ),
        out_specs=P(("head", "phase"), "seq"),
        check_vma=False,
    )
```

```python
import functools
import math

import jax
import jax.numpy as jnp
from jax import lax
from jax.experimental import pallas as pl
from jax.experimental.pallas import tpu as pltpu
from jax.sharding import PartitionSpec as P

HD = 128
BLK = 128
SEGS = 10
SPAN = 64
HALF = 32
NX, NZ, NC = 4, 4, 2
NY = 4
HEADS = 8
NEG = -1e30
HIDDEN = 1 << 20
TILES = 17


def places_of_seq(shift_x=0, flip_z=0, flip_core=0):
    pairs = []
    for x in range(NX):
        for z in range(NZ):
            for c in range(NC):
                src = (x * NZ + z) * NC + c
                dst = (((x - shift_x) % NX) * NZ + (z ^ flip_z)) * NC + (c ^ flip_core)
                pairs.append((src, dst))
    return pairs


def from_seq(a, **kw):
    return lax.ppermute(a, "seq", places_of_seq(**kw))


def gather_z(a):
    return jnp.stack([a] + [from_seq(a, flip_z=k) for k in (1, 2, 3)], 0)


def on_chip(a):
    return pltpu.with_memory_space_constraint(a, pltpu.VMEM)


def off_chip(a):
    return pltpu.with_memory_space_constraint(a, pltpu.HBM)


def over_x(a):
    return [a] + [from_seq(a, shift_x=k) for k in (1, 2, 3)]


def attention_kernel(
    sc, q_ref, kva, kvb, kcode, kpos, qseg, qlim, qpos, send_ref, keep_ref, sbuf, qs, mx, acc, tot
):
    gs, my_x, my_zh, keep_member = sc[0], sc[1], sc[2], sc[3]
    rows = HEADS * SPAN
    for m in range(2):
        for h in range(HEADS):
            qs[m, h * SPAN:(h + 1) * SPAN, :] = q_ref[m, :, h * HD:(h + 1) * HD]
    mx[...] = jnp.full_like(mx, NEG)
    acc[...] = jnp.zeros_like(acc)
    tot[...] = jnp.zeros_like(tot)

    def tile_of(t):
        if t < 8:
            return 1, 0, t
        u = t - 8
        early = u <= gs
        mq = jnp.where(early, 0, 1)
        mk = jnp.where(early, 0, 1)
        g = jnp.where(early, u, u - 1)
        g_rel = (((g >> 1) - my_x) & 3) * 2 + ((g & 1) ^ my_zh)
        return mq, mk, g_rel

    def rows_of(kv, mk, g):
        return jnp.concatenate(
            [kva[2 * g, kv, mk], kva[2 * g + 1, kv, mk], kvb[2 * g, kv, mk], kvb[2 * g + 1, kv, mk]], 0
        )

    for t in range(TILES):
        mq, mk, g = tile_of(t)
        s = lax.dot_general(
            qs[mq], rows_of(0, mk, g), (((1,), (1,)), ((), ())), preferred_element_type=jnp.float32
        )
        code = kcode[(mq * 2 + mk) * 8 + g]
        ok = ((code == qseg[mq]) | (code <= qlim[mq])) & (kpos[mk * 8 + g] <= qpos[mq])
        s = jnp.where(ok[None], s.reshape(HEADS, SPAN, 256), NEG).reshape(rows, 256)
        sbuf[t] = s
        mx[mq] = jnp.maximum(mx[mq], jnp.maximum(s[:, :HD], s[:, HD:]))
    for m in range(2):
        mx[m] = jnp.broadcast_to(jnp.max(mx[m], axis=1, keepdims=True), (rows, HD))
    factor = math.log2(math.e) / math.sqrt(HD)
    for t in range(TILES):
        mq, mk, g = tile_of(t)
        peak = mx[mq]
        s = sbuf[t]
        w = jnp.exp2((s - jnp.concatenate([peak, peak], 1)) * factor)
        tot[mq] += w[:, :HD] + w[:, HD:]
        acc[mq] += jnp.dot(
            w.astype(jnp.bfloat16), rows_of(1, mk, g), preferred_element_type=jnp.float32
        )
    for m in range(2):
        total = jnp.sum(tot[m], axis=1, keepdims=True)
        out = (acc[m] / total).astype(jnp.bfloat16)

        @pl.when(keep_member == m)
        def _():
            for h in range(HEADS):
                keep_ref[:, h * HD:(h + 1) * HD] = out[h * SPAN:(h + 1) * SPAN]

        @pl.when(keep_member != m)
        def _():
            for h in range(HEADS):
                send_ref[:, h * HD:(h + 1) * HD] = out[h * SPAN:(h + 1) * SPAN]


def project_kernel(where, *refs):
    a_in, w_in, outs, (a_own, a_other, sems) = refs[:8], refs[8:16], refs[16:20], refs[20:]
    copies = []
    for j in range(2 * NX):
        to = (a_own if j < NX else a_other).at[where[j % NX]]
        copies.append(pltpu.make_async_copy(a_in[j], to, sems.at[j]))
        copies[-1].start()
    for copy in copies:
        copy.wait()
    wide = HEADS * HD
    own = a_own[...].reshape(NX * NZ * HALF, wide)
    other = a_other[...].reshape(NX * NZ * HALF, wide)
    rows = NZ * HALF
    for half in range(2):
        w_own, *w_other = w_in[4 * half:4 * half + 4]
        c = jnp.dot(own, w_own[...], preferred_element_type=jnp.float32)
        row = 0
        for w in w_other:
            c += jnp.dot(other[:, row:row + w.shape[0]], w[...], preferred_element_type=jnp.float32)
            row += w.shape[0]
        c = c.astype(jnp.bfloat16)
        for k in range(NY):
            outs[k][half] = c[k * rows:(k + 1) * rows]


def place_kernel(spots, *refs):
    o_ref = refs[-1]
    for t in range(2):
        p0, u1, u2, u3, other = refs[5 * t:5 * t + 5]
        mine = (
            p0[0].astype(jnp.float32)
            + u1[0].astype(jnp.float32)
            + u2[0].astype(jnp.float32)
            + u3[0].astype(jnp.float32)
        ).astype(jnp.bfloat16)
        theirs = other[...]
        for k in range(NZ):
            part = slice(k * HALF, (k + 1) * HALF)
            row = pl.multiple_of(spots[k] * SPAN + t * HALF, HALF)
            o_ref[pl.ds(row, HALF), :] = mine[part]
            row = pl.multiple_of(spots[NZ + k] * SPAN + t * HALF, HALF)
            o_ref[pl.ds(row, HALF), :] = theirs[part]


def per_device(queries, keys, values, out_weight, block_vis, seg_lengths):
    seq = lax.axis_index("seq")
    phase = lax.axis_index("phase")
    head = lax.axis_index("head")
    my_x, my_z, my_c = seq // 8, (seq // 2) % 4, seq % 2

    kv = jnp.stack([keys.reshape(2, SPAN, HD), values.reshape(2, SPAN, HD)], 0)
    kv_z = gather_z(kv)
    swap = [(0, 1), (1, 0)]
    kv_z, weight = lax.optimization_barrier((kv_z, out_weight))
    kv_x = over_x(kv_z)
    weight_p = [lax.ppermute(weight[:256], "phase", swap)]
    kv_x, weight_p[0], weight, weight_oc = lax.optimization_barrier(
        (kv_x, weight_p[0], weight, from_seq(out_weight, flip_core=1))
    )
    weight_p += [lax.ppermute(weight[256:512], "phase", swap)]
    kva = jnp.stack(kv_x, 0).reshape(NX * NZ, 2, 2, SPAN, HD)
    kvb = from_seq(kva, flip_core=1)

    tri = jnp.arange(SEGS)[None, :] < jnp.arange(SEGS)[:, None]
    starts = jnp.sum(jnp.where(tri, seg_lengths[None, :], 0), axis=1)

    def segment(pos):
        return jnp.sum((starts[1:] <= pos[..., None]).astype(jnp.int32), axis=-1)

    two = jnp.arange(2, dtype=jnp.int32)
    my_spans = jnp.where(two == 0, seq, 63 - seq)
    q_pos = my_spans[:, None] * SPAN + jnp.arange(SPAN, dtype=jnp.int32)
    q_seg = segment(q_pos)
    q_lim = jnp.where(q_seg == SEGS - 1, SEGS - 1, 0)
    g = jnp.arange(8, dtype=jnp.int32)
    key_x = (my_x + g // 2) & 3
    pair = jnp.arange(2, dtype=jnp.int32)
    key_z = my_z ^ ((g % 2)[:, None] * 2 + pair)
    key_s = key_x[:, None, None] * 8 + key_z[:, None, :] * 2 + (my_c ^ pair)[None, :, None]
    key_span = jnp.where(two[:, None, None, None] == 0, key_s[None], 63 - key_s[None])
    key_span = key_span.reshape(2, 8, 4)
    k_pos = (key_span[..., None] * SPAN + jnp.arange(SPAN, dtype=jnp.int32)).reshape(2, 8, 256)
    k_seg = segment(k_pos)
    blocks = jnp.arange(block_vis.shape[0], dtype=jnp.int32)
    vis_rows = jnp.sum(
        jnp.where(((my_spans // 2)[:, None] == blocks)[..., None], block_vis[None], 0), axis=1
    )
    seen = jnp.sum(
        jnp.where((key_span // 2)[None, ..., None] == blocks, vis_rows[:, None, None, None, :], 0),
        axis=-1,
    )
    seen = jnp.repeat(seen, SPAN, axis=-1).reshape(2, 2, 8, 256)
    k_code = jnp.where(seen == 1, k_seg[None], HIDDEN).reshape(32, 1, 256)
    k_pos = k_pos.reshape(16, 1, 256)
    wide = lambda v: jnp.broadcast_to(v[..., None], (2, SPAN, 256))
    scalars = jnp.stack([seq // 4, my_x, my_z // 2, (my_x + phase) % 2])

    rows = HEADS * SPAN
    vmem = pl.BlockSpec(memory_space=pltpu.VMEM)
    half = jax.ShapeDtypeStruct((SPAN, HEADS * HD), jnp.bfloat16)
    send, keep = pl.pallas_call(
        attention_kernel,
        name="attention",
        out_shape=(half, half),
        in_specs=[pl.BlockSpec(memory_space=pltpu.SMEM)] + [vmem] * 8,
        out_specs=(vmem, vmem),
        scratch_shapes=[
            pltpu.VMEM((TILES, rows, 256), jnp.float32),
            pltpu.VMEM((2, rows, HD), jnp.bfloat16),
            pltpu.VMEM((2, rows, HD), jnp.float32),
            pltpu.VMEM((2, rows, HD), jnp.float32),
            pltpu.VMEM((2, rows, HD), jnp.float32),
        ],
        compiler_params=pltpu.CompilerParams(vmem_limit_bytes=24 << 20),
    )(scalars, queries.reshape(2, SPAN, HEADS * HD), kva, kvb, k_code, k_pos, wide(q_seg), wide(q_lim), wide(q_pos))

    keep, send, weight_p[1] = lax.optimization_barrier((keep, send, weight_p[1]))
    keep_z = gather_z(keep[:HALF])
    keep_z, keep_late, send = lax.optimization_barrier((keep_z, keep[HALF:], send))
    keep_x = [over_x(keep_z)]
    got = lax.ppermute(send, "phase", swap)
    keep_z = gather_z(keep_late)
    keep_z, got = lax.optimization_barrier((keep_z, got))
    keep_x += [over_x(keep_z)]
    got_z = gather_z(got)
    keep_x, got_z, weight, weight_p = lax.optimization_barrier((keep_x, got_z, weight, weight_p))
    weight_p += [lax.ppermute(weight[512:], "phase", swap)]
    got_t = [got_z[:, :HALF], got_z[:, HALF:]]
    got_x = [over_x(got_t[0])]
    weight_pc = [from_seq(w, flip_core=1) for w in weight_p[:2]]
    got_x[0], got_t[1], weight_p[2] = lax.optimization_barrier((got_x[0], got_t[1], weight_p[2]))
    got_x += [over_x(got_t[1])]
    weight_pc += [from_seq(weight_p[2], flip_core=1)]

    steps = jnp.arange(NY, dtype=jnp.int32)
    x_of = (my_x + steps) & 3
    block = jnp.where((x_of + phase) % 2 == 0, x_of, 7 - x_of)
    where = (block // 2 - head) & 3
    my_block = 2 * head + phase
    z_of = my_z ^ steps
    place = jnp.concatenate([2 * z_of + my_c, 2 * z_of + (1 - my_c)])
    spots = jnp.where(my_block < 4, place, 7 - place)
    f32 = jnp.float32
    pieces = []
    for t in range(2):
        piece = jax.ShapeDtypeStruct((2, NZ * HALF, 512), jnp.bfloat16)
        wide_k = HEADS * HD
        partial = pl.pallas_call(
            project_kernel,
            name="project",
            out_shape=(piece,) * NY,
            in_specs=[pl.BlockSpec(memory_space=pltpu.SMEM)] + [pl.BlockSpec(memory_space=pltpu.HBM)] * 8 + [vmem] * 8,
            out_specs=(vmem,) * NY,
            scratch_shapes=[
                pltpu.VMEM((NX, NZ, HALF, wide_k), jnp.bfloat16),
                pltpu.VMEM((NX, NZ, HALF, wide_k), jnp.bfloat16),
                pltpu.SemaphoreType.DMA((2 * NX,)),
            ],
            compiler_params=pltpu.CompilerParams(vmem_limit_bytes=16 << 20),
        )(where, *[off_chip(v) for v in (*keep_x[t], *got_x[t])],
          *[on_chip(v) for v in (out_weight, *weight_p, weight_oc, *weight_pc)])
        ups = [
            lax.ppermute(partial[k], "head", [(y, (y + k) % NY) for y in range(NY)]) for k in (1, 2, 3)
        ]
        for_other = sum([u[1].astype(f32) for u in ups], partial[0][1].astype(f32))
        from_other = from_seq(for_other.astype(jnp.bfloat16), flip_core=1)
        pieces += [partial[0], *ups, from_other]

    in_specs = []
    for t in range(2):
        in_specs += [pl.BlockSpec((1, NZ * HALF, 512), lambda i, s: (0, 0, 0))]
        in_specs += [pl.BlockSpec((1, NZ * HALF, 512), lambda i, s: (0, 0, 0))] * 3
        in_specs += [pl.BlockSpec((NZ * HALF, 512), lambda i, s: (0, 0))]
    return pl.pallas_call(
        place_kernel,
        name="place",
        out_shape=jax.ShapeDtypeStruct((8 * SPAN, 512), jnp.bfloat16),
        grid_spec=pltpu.PrefetchScalarGridSpec(
            num_scalar_prefetch=1,
            grid=(1,),
            in_specs=in_specs,
            out_specs=pl.BlockSpec((8 * SPAN, 512), lambda i, s: (0, 0)),
        ),
    )(spots, *[on_chip(v) for v in pieces])


def solution(mesh):
    return jax.shard_map(
        per_device,
        mesh=mesh,
        in_specs=(
            P("seq", None, None, ("head", "phase")),
            P("seq", None, None, ("head", "phase")),
            P("seq", None, None, ("head", "phase")),
            P(("head", "phase"), "seq"),
            P(),
            P(),
        ),
        out_specs=P(("head", "phase"), "seq"),
        check_vma=False,
    )
```

```python
import functools
import math

import jax
import jax.numpy as jnp
from jax import lax
from jax.experimental import pallas as pl
from jax.experimental.pallas import tpu as pltpu
from jax.sharding import PartitionSpec as P

HD = 128
BLK = 128
SEGS = 10
SPAN = 64
NX, NZ, NC = 4, 4, 2
NY = 4
HEADS = 8
NEG = -1e30
HIDDEN = 1 << 20
TILES = 17


def places_of_seq(shift_x=0, flip_z=0, flip_core=0):
    pairs = []
    for x in range(NX):
        for z in range(NZ):
            for c in range(NC):
                src = (x * NZ + z) * NC + c
                dst = (((x - shift_x) % NX) * NZ + (z ^ flip_z)) * NC + (c ^ flip_core)
                pairs.append((src, dst))
    return pairs


def from_seq(a, **kw):
    return lax.ppermute(a, "seq", places_of_seq(**kw))


def gather_z(a):
    return jnp.stack([a] + [from_seq(a, flip_z=k) for k in (1, 2, 3)], 0)


def off_chip(a):
    return pltpu.with_memory_space_constraint(a, pltpu.HBM)


def over_x(a):
    return [a] + [from_seq(a, shift_x=k) for k in (1, 2, 3)]


def attention_kernel(
    sc, q_ref, kva, kvb, kcode, kpos, qseg, qlim, qpos, send_ref, keep_ref, sbuf, qs, mx, acc, tot
):
    gs, my_x, my_zh, keep_member = sc[0], sc[1], sc[2], sc[3]
    rows = HEADS * SPAN
    for m in range(2):
        for h in range(HEADS):
            qs[m, h * SPAN:(h + 1) * SPAN, :] = q_ref[m, :, h * HD:(h + 1) * HD]
    mx[...] = jnp.full_like(mx, NEG)
    acc[...] = jnp.zeros_like(acc)
    tot[...] = jnp.zeros_like(tot)

    def tile_of(t):
        if t < 8:
            return 1, 0, t
        u = t - 8
        early = u <= gs
        mq = jnp.where(early, 0, 1)
        mk = jnp.where(early, 0, 1)
        g = jnp.where(early, u, u - 1)
        g_rel = (((g >> 1) - my_x) & 3) * 2 + ((g & 1) ^ my_zh)
        return mq, mk, g_rel

    def rows_of(kv, mk, g):
        return jnp.concatenate(
            [kva[2 * g, kv, mk], kva[2 * g + 1, kv, mk], kvb[2 * g, kv, mk], kvb[2 * g + 1, kv, mk]], 0
        )

    for t in range(TILES):
        mq, mk, g = tile_of(t)
        s = lax.dot_general(
            qs[mq], rows_of(0, mk, g), (((1,), (1,)), ((), ())), preferred_element_type=jnp.float32
        )
        code = kcode[(mq * 2 + mk) * 8 + g]
        ok = ((code == qseg[mq]) | (code <= qlim[mq])) & (kpos[mk * 8 + g] <= qpos[mq])
        s = jnp.where(ok[None], s.reshape(HEADS, SPAN, 256), NEG).reshape(rows, 256)
        sbuf[t] = s
        mx[mq] = jnp.maximum(mx[mq], jnp.maximum(s[:, :HD], s[:, HD:]))
    for m in range(2):
        mx[m] = jnp.broadcast_to(jnp.max(mx[m], axis=1, keepdims=True), (rows, HD))
    factor = math.log2(math.e) / math.sqrt(HD)
    for t in range(TILES):
        mq, mk, g = tile_of(t)
        peak = mx[mq]
        s = sbuf[t]
        w = jnp.exp2((s - jnp.concatenate([peak, peak], 1)) * factor)
        tot[mq] += w[:, :HD] + w[:, HD:]
        acc[mq] += jnp.dot(
            w.astype(jnp.bfloat16), rows_of(1, mk, g), preferred_element_type=jnp.float32
        )
    for m in range(2):
        total = jnp.sum(tot[m], axis=1, keepdims=True)
        out = (acc[m] / total).astype(jnp.bfloat16)

        @pl.when(keep_member == m)
        def _():
            for h in range(HEADS):
                keep_ref[:, h * HD:(h + 1) * HD] = out[h * SPAN:(h + 1) * SPAN]

        @pl.when(keep_member != m)
        def _():
            for h in range(HEADS):
                send_ref[:, h * HD:(h + 1) * HD] = out[h * SPAN:(h + 1) * SPAN]


def project_kernel(where, *refs):
    a_in, w_in, outs, (a_own, a_other, sems) = refs[:8], refs[8:10], refs[10:14], refs[14:]
    copies = []
    for j in range(2 * NX):
        to = (a_own if j < NX else a_other).at[where[j % NX]]
        copies.append(pltpu.make_async_copy(a_in[j], to, sems.at[j]))
        copies[-1].start()
    for copy in copies:
        copy.wait()
    wide = HEADS * HD
    phase = where[NX]
    rows = NZ * SPAN
    for k in range(NY):
        own = a_own[k].reshape(rows, wide)
        other = a_other[k].reshape(rows, wide)
        for half in range(2):
            w = w_in[half]
            c = jnp.dot(own, w[phase], preferred_element_type=jnp.float32)
            c += jnp.dot(other, w[1 - phase], preferred_element_type=jnp.float32)
            outs[k][half] = c.astype(jnp.bfloat16)


def place_kernel(spots, p0, u1, u2, u3, other, o_ref):
    mine = (
        p0[0].astype(jnp.float32)
        + u1[0].astype(jnp.float32)
        + u2[0].astype(jnp.float32)
        + u3[0].astype(jnp.float32)
    ).astype(jnp.bfloat16)
    theirs = other[...]
    for k in range(NZ):
        part = slice(k * SPAN, (k + 1) * SPAN)
        o_ref[pl.ds(pl.multiple_of(spots[k] * SPAN, SPAN), SPAN), :] = mine[part]
        o_ref[pl.ds(pl.multiple_of(spots[NZ + k] * SPAN, SPAN), SPAN), :] = theirs[part]


def per_device(queries, keys, values, out_weight, block_vis, seg_lengths):
    seq = lax.axis_index("seq")
    phase = lax.axis_index("phase")
    head = lax.axis_index("head")
    my_x, my_z, my_c = seq // 8, (seq // 2) % 4, seq % 2

    kv = jnp.stack([keys.reshape(2, SPAN, HD), values.reshape(2, SPAN, HD)], 0)
    kv_z = gather_z(kv)
    swap = [(0, 1), (1, 0)]
    weights = lax.all_gather(out_weight, "phase", axis=0)
    kv_x = over_x(kv_z)
    kva = jnp.stack(kv_x, 0).reshape(NX * NZ, 2, 2, SPAN, HD)
    kvb = from_seq(kva, flip_core=1)

    tri = jnp.arange(SEGS)[None, :] < jnp.arange(SEGS)[:, None]
    starts = jnp.sum(jnp.where(tri, seg_lengths[None, :], 0), axis=1)

    def segment(pos):
        return jnp.sum((starts[1:] <= pos[..., None]).astype(jnp.int32), axis=-1)

    two = jnp.arange(2, dtype=jnp.int32)
    my_spans = jnp.where(two == 0, seq, 63 - seq)
    q_pos = my_spans[:, None] * SPAN + jnp.arange(SPAN, dtype=jnp.int32)
    q_seg = segment(q_pos)
    q_lim = jnp.where(q_seg == SEGS - 1, SEGS - 1, 0)
    g = jnp.arange(8, dtype=jnp.int32)
    key_x = (my_x + g // 2) & 3
    pair = jnp.arange(2, dtype=jnp.int32)
    key_z = my_z ^ ((g % 2)[:, None] * 2 + pair)
    key_s = key_x[:, None, None] * 8 + key_z[:, None, :] * 2 + (my_c ^ pair)[None, :, None]
    key_span = jnp.where(two[:, None, None, None] == 0, key_s[None], 63 - key_s[None])
    key_span = key_span.reshape(2, 8, 4)
    k_pos = (key_span[..., None] * SPAN + jnp.arange(SPAN, dtype=jnp.int32)).reshape(2, 8, 256)
    k_seg = segment(k_pos)
    blocks = jnp.arange(block_vis.shape[0], dtype=jnp.int32)
    vis_rows = jnp.sum(
        jnp.where(((my_spans // 2)[:, None] == blocks)[..., None], block_vis[None], 0), axis=1
    )
    seen = jnp.sum(
        jnp.where((key_span // 2)[None, ..., None] == blocks, vis_rows[:, None, None, None, :], 0),
        axis=-1,
    )
    seen = jnp.repeat(seen, SPAN, axis=-1).reshape(2, 2, 8, 256)
    k_code = jnp.where(seen == 1, k_seg[None], HIDDEN).reshape(32, 1, 256)
    k_pos = k_pos.reshape(16, 1, 256)
    wide = lambda v: jnp.broadcast_to(v[..., None], (2, SPAN, 256))
    scalars = jnp.stack([seq // 4, my_x, my_z // 2, (my_x + phase) % 2])

    rows = HEADS * SPAN
    vmem = pl.BlockSpec(memory_space=pltpu.VMEM)
    half = jax.ShapeDtypeStruct((SPAN, HEADS * HD), jnp.bfloat16)
    send, keep = pl.pallas_call(
        attention_kernel,
        name="attention",
        out_shape=(half, half),
        in_specs=[pl.BlockSpec(memory_space=pltpu.SMEM)] + [vmem] * 8,
        out_specs=(vmem, vmem),
        scratch_shapes=[
            pltpu.VMEM((TILES, rows, 256), jnp.float32),
            pltpu.VMEM((2, rows, HD), jnp.bfloat16),
            pltpu.VMEM((2, rows, HD), jnp.float32),
            pltpu.VMEM((2, rows, HD), jnp.float32),
            pltpu.VMEM((2, rows, HD), jnp.float32),
        ],
        compiler_params=pltpu.CompilerParams(vmem_limit_bytes=24 << 20),
    )(scalars, queries.reshape(2, SPAN, HEADS * HD), kva, kvb, k_code, k_pos, wide(q_seg), wide(q_lim), wide(q_pos))

    got = lax.ppermute(send, "phase", swap)
    keep_z, got = lax.optimization_barrier((gather_z(keep), got))
    keep_x = over_x(keep_z)
    got_z = gather_z(got)
    keep_x, got_z, weights = lax.optimization_barrier((keep_x, got_z, weights))
    got_x = over_x(got_z)
    weights_other = from_seq(weights, flip_core=1)

    steps = jnp.arange(NY, dtype=jnp.int32)
    x_of = (my_x + steps) & 3
    block = jnp.where((x_of + phase) % 2 == 0, x_of, 7 - x_of)
    where = jnp.concatenate([(block // 2 - head) & 3, phase[None]])
    my_block = 2 * head + phase
    z_of = my_z ^ steps
    place = jnp.concatenate([2 * z_of + my_c, 2 * z_of + (1 - my_c)])
    spots = jnp.where(my_block < 4, place, 7 - place)
    f32 = jnp.float32
    piece = jax.ShapeDtypeStruct((2, NZ * SPAN, 512), jnp.bfloat16)
    wide_k = HEADS * HD
    partial = pl.pallas_call(
        project_kernel,
        name="project",
        out_shape=(piece,) * NY,
        in_specs=[pl.BlockSpec(memory_space=pltpu.SMEM)]
        + [pl.BlockSpec(memory_space=pltpu.HBM)] * 8
        + [vmem] * 2,
        out_specs=(vmem,) * NY,
        scratch_shapes=[
            pltpu.VMEM((NX, NZ, SPAN, wide_k), jnp.bfloat16),
            pltpu.VMEM((NX, NZ, SPAN, wide_k), jnp.bfloat16),
            pltpu.SemaphoreType.DMA((2 * NX,)),
        ],
        compiler_params=pltpu.CompilerParams(vmem_limit_bytes=24 << 20),
    )(where, *[off_chip(v) for v in (*keep_x, *got_x)], weights, weights_other)
    ups = [lax.ppermute(partial[k], "head", [(y, (y + k) % NY) for y in range(NY)]) for k in (1, 2, 3)]
    for_other = sum([u[1].astype(f32) for u in ups], partial[0][1].astype(f32))
    from_other = from_seq(for_other.astype(jnp.bfloat16), flip_core=1)
    return pl.pallas_call(
        place_kernel,
        name="place",
        out_shape=jax.ShapeDtypeStruct((8 * SPAN, 512), jnp.bfloat16),
        in_specs=[pl.BlockSpec(memory_space=pltpu.SMEM)] + [vmem] * 5,
        out_specs=vmem,
        compiler_params=pltpu.CompilerParams(vmem_limit_bytes=16 << 20),
    )(spots, partial[0], *ups, from_other)


def solution(mesh):
    return jax.shard_map(
        per_device,
        mesh=mesh,
        in_specs=(
            P("seq", None, None, ("head", "phase")),
            P("seq", None, None, ("head", "phase")),
            P("seq", None, None, ("head", "phase")),
            P(("head", "phase"), "seq"),
            P(),
            P(),
        ),
        out_specs=P(("head", "phase"), "seq"),
        check_vma=False,
    )
```

```python
import math

import jax
import jax.numpy as jnp
from jax import lax
from jax.experimental import pallas as pl
from jax.experimental.pallas import tpu as pltpu
from jax.sharding import PartitionSpec as P

HD = 128
SEGS = 10
SPAN = 64
ROWS = 32
PART = 16
NX, NZ, NC = 4, 4, 2
NY = 4
HEADS = 8
WIDE = HEADS * HD
NEG = -1e30
HIDDEN = 1 << 20
BOTH = 8
SINGLE = 18


def places_of_seq(shift_x=0, flip_z=0, flip_core=0):
    pairs = []
    for x in range(NX):
        for z in range(NZ):
            for c in range(NC):
                src = (x * NZ + z) * NC + c
                dst = (((x - shift_x) % NX) * NZ + (z ^ flip_z)) * NC + (c ^ flip_core)
                pairs.append((src, dst))
    return pairs


def from_seq(a, **kw):
    return lax.ppermute(a, "seq", places_of_seq(**kw))


def up_head(a, k):
    return lax.ppermute(a, "head", [(y, (y + k) % NY) for y in range(NY)])


def gather_z(a):
    return jnp.stack([a] + [from_seq(a, flip_z=k) for k in (1, 2, 3)], 0)


def over_x(a):
    return [a] + [from_seq(a, shift_x=k) for k in (1, 2, 3)]


def on_chip(a):
    return pltpu.with_memory_space_constraint(a, pltpu.VMEM)


def off_chip(a):
    return pltpu.with_memory_space_constraint(a, pltpu.HBM)


def attention_kernel(
    sc, q_own, q_far, kva, kvb, kcode, kpos, qseg, qlim, qpos, *rest
):
    outs, (both, single, qs, mx, acc, tot, done) = rest[:NY], rest[NY:]
    tile_lo, tile_hi, my_x, my_zh, half, head = sc[0], sc[1], sc[2], sc[3], sc[4], sc[5]
    rows = HEADS * ROWS
    start = pl.multiple_of(half * ROWS, ROWS)

    for m in range(2):
        near = q_own[m, pl.ds(start, ROWS), :]
        far = q_far[m, pl.ds(start, ROWS), :]
        low = jnp.where(half == 0, near, far)
        high = jnp.where(half == 0, far, near)
        for h in range(HEADS):
            cols = slice(h * HD, (h + 1) * HD)
            qs[3 * m, h * ROWS:(h + 1) * ROWS, :] = low[:, cols]
            qs[1 + m, h * ROWS:(h + 1) * ROWS, :] = high[:, cols]
    mx[...] = jnp.full_like(mx, NEG)
    acc[...] = jnp.zeros_like(acc)
    tot[...] = jnp.zeros_like(tot)

    def tile_of(t):
        pair, u = t // 9, t % 9
        early = u <= (tile_lo if pair == 0 else tile_hi)
        group = jnp.where(early, pair, 3 - pair)
        mk = jnp.where(early, 0, 1)
        g = jnp.where(early, u, u - 1)
        g_rel = (((g >> 1) - my_x) & 3) * 2 + ((g & 1) ^ my_zh)
        return group, mk, g_rel

    def rows_of(kv, mk, g):
        return jnp.concatenate(
            [kva[2 * g, kv, mk], kva[2 * g + 1, kv, mk], kvb[2 * g, kv, mk], kvb[2 * g + 1, kv, mk]], 0
        )

    def masked(s, group, mk, g):
        code = kcode[(group * 2 + mk) * 8 + g]
        ok = ((code == qseg[group]) | (code <= qlim[group])) & (kpos[mk * 8 + g] <= qpos[group])
        return jnp.where(ok[None], s.reshape(HEADS, ROWS, 256), NEG).reshape(rows, 256)

    def dot_keys(q, keys):
        return lax.dot_general(q, keys, (((1,), (1,)), ((), ())), preferred_element_type=jnp.float32)

    for t in range(BOTH):
        s = dot_keys(qs[2:4].reshape(2 * rows, HD), rows_of(0, 0, t))
        for i in range(2):
            part = masked(s[i * rows:(i + 1) * rows], 2 + i, 0, t)
            both[t, i] = part
            mx[2 + i] = jnp.maximum(mx[2 + i], jnp.maximum(part[:, :HD], part[:, HD:]))
    for t in range(SINGLE):
        group, mk, g = tile_of(t)
        s = masked(dot_keys(qs[group], rows_of(0, mk, g)), group, mk, g)
        single[t] = s
        mx[group] = jnp.maximum(mx[group], jnp.maximum(s[:, :HD], s[:, HD:]))
    for i in range(4):
        mx[i] = jnp.broadcast_to(jnp.max(mx[i], axis=1, keepdims=True), (rows, HD))
    factor = math.log2(math.e) / math.sqrt(HD)

    def weigh(s, peak):
        return jnp.exp2((s - jnp.concatenate([peak, peak], 1)) * factor)

    for t in range(BOTH):
        parts = []
        for i in range(2):
            w = weigh(both[t, i], mx[2 + i])
            tot[2 + i] += w[:, :HD] + w[:, HD:]
            parts.append(w.astype(jnp.bfloat16))
        mixed = jnp.dot(jnp.concatenate(parts, 0), rows_of(1, 0, t), preferred_element_type=jnp.float32)
        for i in range(2):
            acc[2 + i] += mixed[i * rows:(i + 1) * rows]
    for t in range(SINGLE):
        group, mk, g = tile_of(t)
        w = weigh(single[t], mx[group])
        tot[group] += w[:, :HD] + w[:, HD:]
        acc[group] += jnp.dot(w.astype(jnp.bfloat16), rows_of(1, mk, g), preferred_element_type=jnp.float32)
    for i in range(4):
        total = jnp.sum(tot[i], axis=1, keepdims=True)
        out = (acc[i] / total).astype(jnp.bfloat16)
        for h in range(HEADS):
            done[i, :, h * HD:(h + 1) * HD] = out[h * ROWS:(h + 1) * ROWS]
    for k in range(NY):
        outs[k][...] = done[(head + k) & 3].reshape(2, PART, WIDE)


def project_kernel(where, *refs):
    a_in, w_in, (mine, theirs), (a_all, sems) = refs[:NX], refs[NX:NX + 8], refs[NX + 8:NX + 10], refs[NX + 10:]
    copies = []
    for j in range(NX):
        copies.append(pltpu.make_async_copy(a_in[j], a_all.at[where[j]], sems.at[j]))
        copies[-1].start()
    for copy in copies:
        copy.wait()
    count = NZ * PART
    lhs = [a_all[:, :, k].reshape(NX * count, WIDE) for k in range(NY)]
    for side in range(2):
        c = jnp.dot(lhs[0], w_in[4 * side][...], preferred_element_type=jnp.float32)
        for k in range(1, NY):
            c += jnp.dot(lhs[k], w_in[4 * side + k][...], preferred_element_type=jnp.float32)
        c = c.astype(jnp.bfloat16)
        mine[side] = c[:2 * count]
        theirs[side] = c[2 * count:]


def place_kernel(spots, *refs):
    o_ref = refs[-1]
    for t in range(2):
        near, got, other = refs[3 * t:3 * t + 3]
        own = (near[0].astype(jnp.float32) + got[0].astype(jnp.float32)).astype(jnp.bfloat16)
        theirs = other[...]
        for h in range(2):
            for k in range(NZ):
                part = slice((h * NZ + k) * PART, (h * NZ + k + 1) * PART)
                inside = h * ROWS + t * PART
                row = pl.multiple_of(spots[k] * SPAN + inside, PART)
                o_ref[pl.ds(row, PART), :] = own[part]
                row = pl.multiple_of(spots[NZ + k] * SPAN + inside, PART)
                o_ref[pl.ds(row, PART), :] = theirs[part]


def per_device(queries, keys, values, out_weight, block_vis, seg_lengths):
    seq = lax.axis_index("seq")
    phase = lax.axis_index("phase")
    head = lax.axis_index("head")
    my_x, my_z, my_c = seq // 8, (seq // 2) % 4, seq % 2
    f32 = jnp.float32

    q_own = queries.reshape(2, SPAN, WIDE)
    q_far = from_seq(q_own, shift_x=2)
    half = my_x // 2

    kv = jnp.stack([keys.reshape(2, SPAN, HD), values.reshape(2, SPAN, HD)], 0)
    kv_x = over_x(gather_z(kv))
    kv_x, weight_oc, q_far = lax.optimization_barrier((kv_x, from_seq(out_weight, flip_core=1), q_far))
    kva = jnp.stack(kv_x, 0).reshape(NX * NZ, 2, 2, SPAN, HD)
    kvb = from_seq(kva, flip_core=1)
    weight_1, weight_3 = up_head(out_weight, 1), up_head(out_weight, 3)
    kva, kvb, weight_1, weight_3 = lax.optimization_barrier((kva, kvb, weight_1, weight_3))

    tri = jnp.arange(SEGS)[None, :] < jnp.arange(SEGS)[:, None]
    starts = jnp.sum(jnp.where(tri, seg_lengths[None, :], 0), axis=1)

    def segment(pos):
        return jnp.sum((starts[1:] <= pos[..., None]).astype(jnp.int32), axis=-1)

    two = jnp.arange(2, dtype=jnp.int32)
    four = jnp.arange(4, dtype=jnp.int32)
    low = seq & 15
    high = low + 16
    q_span = jnp.where(four == 0, low, jnp.where(four == 1, high, jnp.where(four == 2, 63 - high, 63 - low)))
    q_pos = q_span[:, None] * SPAN + half * ROWS + jnp.arange(ROWS, dtype=jnp.int32)
    q_seg = segment(q_pos)
    q_lim = jnp.where(q_seg == SEGS - 1, SEGS - 1, 0)
    g = jnp.arange(8, dtype=jnp.int32)
    key_x = (my_x + g // 2) & 3
    key_z = my_z ^ ((g % 2)[:, None] * 2 + two)
    key_s = key_x[:, None, None] * 8 + key_z[:, None, :] * 2 + (my_c ^ two)[None, :, None]
    key_span = jnp.where(two[:, None, None, None] == 0, key_s[None], 63 - key_s[None])
    key_span = key_span.reshape(2, 8, 4)
    k_pos = (key_span[..., None] * SPAN + jnp.arange(SPAN, dtype=jnp.int32)).reshape(2, 8, 256)
    k_seg = segment(k_pos)
    blocks = jnp.arange(block_vis.shape[0], dtype=jnp.int32)
    vis_rows = jnp.sum(
        jnp.where(((q_span // 2)[:, None] == blocks)[..., None], block_vis[None], 0), axis=1
    )
    seen = jnp.sum(
        jnp.where((key_span // 2)[None, ..., None] == blocks, vis_rows[:, None, None, None, :], 0),
        axis=-1,
    )
    seen = jnp.repeat(seen, SPAN, axis=-1).reshape(4, 2, 8, 256)
    k_code = jnp.where(seen == 1, k_seg[None], HIDDEN).reshape(64, 1, 256)
    k_pos = k_pos.reshape(16, 1, 256)
    wide = lambda v: jnp.broadcast_to(v[..., None], (4, ROWS, 256))
    scalars = jnp.stack([low // 4, high // 4, my_x, my_z // 2, half, head])

    rows = HEADS * ROWS
    smem = pl.BlockSpec(memory_space=pltpu.SMEM)
    vmem = pl.BlockSpec(memory_space=pltpu.VMEM)
    hbm = pl.BlockSpec(memory_space=pltpu.HBM)
    heads_out = pl.pallas_call(
        attention_kernel,
        name="attention",
        out_shape=(jax.ShapeDtypeStruct((2, PART, WIDE), jnp.bfloat16),) * NY,
        in_specs=[smem] + [vmem] * 9,
        out_specs=(vmem,) * NY,
        scratch_shapes=[
            pltpu.VMEM((BOTH, 2, rows, 256), f32),
            pltpu.VMEM((SINGLE, rows, 256), f32),
            pltpu.VMEM((4, rows, HD), jnp.bfloat16),
            pltpu.VMEM((4, rows, HD), f32),
            pltpu.VMEM((4, rows, HD), f32),
            pltpu.VMEM((4, rows, HD), f32),
            pltpu.VMEM((4, ROWS, WIDE), jnp.bfloat16),
        ],
        compiler_params=pltpu.CompilerParams(vmem_limit_bytes=24 << 20),
    )(scalars, q_own, q_far, kva, kvb, k_code, k_pos, wide(q_seg), wide(q_lim), wide(q_pos))

    heads_in = [heads_out[0]] + [up_head(heads_out[k], k) for k in (1, 2, 3)]
    part = [jnp.stack([v[t] for v in heads_in], 0) for t in range(2)]
    part[0], part[1], weight = lax.optimization_barrier((part[0], part[1], out_weight))
    weight_2 = up_head(weight, 2)
    part_z, late = lax.optimization_barrier((gather_z(part[0]), part[1]))
    part_x = over_x(part_z)
    late_z = gather_z(late)
    part_x, late_z, weight_1, weight_2, weight_3 = lax.optimization_barrier(
        (part_x, late_z, weight_1, weight_2, weight_3)
    )
    part_x = [part_x, over_x(late_z)]
    weights = [out_weight, weight_1, weight_2, weight_3]
    weights += [weight_oc] + [from_seq(w, flip_core=1) for w in weights[1:]]

    x_of = (my_x + four) & 3
    ends = (x_of & 1) ^ (head // 2)
    where = jnp.where(ends == phase, 0, 2) + x_of // 2
    z_of = my_z ^ four
    place = jnp.concatenate([2 * z_of + my_c, 2 * z_of + (1 - my_c)])
    spots = jnp.where(head < 2, place, 7 - place)
    piece = jax.ShapeDtypeStruct((2, 2 * NZ * PART, 512), jnp.bfloat16)
    pieces = []
    for t in range(2):
        mine, theirs = pl.pallas_call(
            project_kernel,
            name="project",
            out_shape=(piece, piece),
            in_specs=[smem] + [hbm] * NX + [vmem] * 8,
            out_specs=(vmem, vmem),
            scratch_shapes=[
                pltpu.VMEM((NX, NZ, NY, PART, WIDE), jnp.bfloat16),
                pltpu.SemaphoreType.DMA((NX,)),
            ],
            compiler_params=pltpu.CompilerParams(vmem_limit_bytes=24 << 20),
        )(where, *[off_chip(v) for v in part_x[t]], *[on_chip(w) for w in weights])
        got = lax.ppermute(theirs, "phase", [(0, 1), (1, 0)])
        for_other = (mine[1].astype(f32) + got[1].astype(f32)).astype(jnp.bfloat16)
        pieces += [mine, got, from_seq(for_other, flip_core=1)]
    return pl.pallas_call(
        place_kernel,
        name="place",
        out_shape=jax.ShapeDtypeStruct((8 * SPAN, 512), jnp.bfloat16),
        in_specs=[smem] + [vmem] * 6,
        out_specs=vmem,
        compiler_params=pltpu.CompilerParams(vmem_limit_bytes=16 << 20),
    )(spots, *pieces)


def solution(mesh):
    return jax.shard_map(
        per_device,
        mesh=mesh,
        in_specs=(
            P("seq", None, None, ("head", "phase")),
            P("seq", None, None, ("head", "phase")),
            P("seq", None, None, ("head", "phase")),
            P(("head", "phase"), "seq"),
            P(),
            P(),
        ),
        out_specs=P(("head", "phase"), "seq"),
        check_vma=False,
    )
```

```python
import math

import jax
import jax.numpy as jnp
from jax import lax
from jax.experimental import pallas as pl
from jax.experimental.pallas import tpu as pltpu
from jax.sharding import PartitionSpec as P

HD = 128
SEGS = 10
SPAN = 64
ROWS = 32
PART = 16
NX, NZ, NC = 4, 4, 2
NY = 4
HEADS = 8
WIDE = HEADS * HD
NEG = -1e30
HIDDEN = 1 << 20
BOTH = 8
SINGLE = 18


def places_of_seq(shift_x=0, flip_z=0, flip_core=0):
    pairs = []
    for x in range(NX):
        for z in range(NZ):
            for c in range(NC):
                src = (x * NZ + z) * NC + c
                dst = (((x - shift_x) % NX) * NZ + (z ^ flip_z)) * NC + (c ^ flip_core)
                pairs.append((src, dst))
    return pairs


def from_seq(a, **kw):
    return lax.ppermute(a, "seq", places_of_seq(**kw))


def up_head(a, k):
    return lax.ppermute(a, "head", [(y, (y + k) % NY) for y in range(NY)])


def gather_z(a):
    return jnp.stack([a] + [from_seq(a, flip_z=k) for k in (1, 2, 3)], 0)


def over_x(a):
    return [a] + [from_seq(a, shift_x=k) for k in (1, 2, 3)]


def on_chip(a):
    return pltpu.with_memory_space_constraint(a, pltpu.VMEM)


def off_chip(a):
    return pltpu.with_memory_space_constraint(a, pltpu.HBM)


def attention_kernel(
    sc, q_own, q_far, kva, kvb, kcode, kpos, qseg, qlim, qpos, *rest
):
    outs, (both, single, qs, mx, acc, tot, done) = rest[:NY], rest[NY:]
    tile_lo, tile_hi, my_x, my_zh, half, head = sc[0], sc[1], sc[2], sc[3], sc[4], sc[5]
    rows = HEADS * ROWS
    start = pl.multiple_of(half * ROWS, ROWS)

    for m in range(2):
        near = q_own[m, pl.ds(start, ROWS), :]
        far = q_far[m, pl.ds(start, ROWS), :]
        low = jnp.where(half == 0, near, far)
        high = jnp.where(half == 0, far, near)
        for h in range(HEADS):
            cols = slice(h * HD, (h + 1) * HD)
            qs[3 * m, h * ROWS:(h + 1) * ROWS, :] = low[:, cols]
            qs[1 + m, h * ROWS:(h + 1) * ROWS, :] = high[:, cols]
    mx[...] = jnp.full_like(mx, NEG)
    acc[...] = jnp.zeros_like(acc)
    tot[...] = jnp.zeros_like(tot)

    def tile_of(t):
        pair, u = t // 9, t % 9
        early = u <= (tile_lo if pair == 0 else tile_hi)
        group = jnp.where(early, pair, 3 - pair)
        mk = jnp.where(early, 0, 1)
        g = jnp.where(early, u, u - 1)
        g_rel = (((g >> 1) - my_x) & 3) * 2 + ((g & 1) ^ my_zh)
        return group, mk, g_rel

    def rows_of(kv, mk, g):
        return jnp.concatenate(
            [kva[2 * g, kv, mk], kva[2 * g + 1, kv, mk], kvb[2 * g, kv, mk], kvb[2 * g + 1, kv, mk]], 0
        )

    def masked(s, group, mk, g):
        code = kcode[(group * 2 + mk) * 8 + g]
        ok = ((code == qseg[group]) | (code <= qlim[group])) & (kpos[mk * 8 + g] <= qpos[group])
        return jnp.where(ok[None], s.reshape(HEADS, ROWS, 256), NEG).reshape(rows, 256)

    def dot_keys(q, keys):
        return lax.dot_general(q, keys, (((1,), (1,)), ((), ())), preferred_element_type=jnp.float32)

    for t in range(BOTH):
        s = dot_keys(qs[2:4].reshape(2 * rows, HD), rows_of(0, 0, t))
        for i in range(2):
            part = masked(s[i * rows:(i + 1) * rows], 2 + i, 0, t)
            both[t, i] = part
            mx[2 + i] = jnp.maximum(mx[2 + i], jnp.maximum(part[:, :HD], part[:, HD:]))
    for t in range(SINGLE):
        group, mk, g = tile_of(t)
        s = masked(dot_keys(qs[group], rows_of(0, mk, g)), group, mk, g)
        single[t] = s
        mx[group] = jnp.maximum(mx[group], jnp.maximum(s[:, :HD], s[:, HD:]))
    for i in range(4):
        mx[i] = jnp.broadcast_to(jnp.max(mx[i], axis=1, keepdims=True), (rows, HD))
    factor = math.log2(math.e) / math.sqrt(HD)

    def weigh(s, peak):
        return jnp.exp2((s - jnp.concatenate([peak, peak], 1)) * factor)

    for t in range(BOTH):
        parts = []
        for i in range(2):
            w = weigh(both[t, i], mx[2 + i])
            tot[2 + i] += w[:, :HD] + w[:, HD:]
            parts.append(w.astype(jnp.bfloat16))
        mixed = jnp.dot(jnp.concatenate(parts, 0), rows_of(1, 0, t), preferred_element_type=jnp.float32)
        for i in range(2):
            acc[2 + i] += mixed[i * rows:(i + 1) * rows]
    for t in range(SINGLE):
        group, mk, g = tile_of(t)
        w = weigh(single[t], mx[group])
        tot[group] += w[:, :HD] + w[:, HD:]
        acc[group] += jnp.dot(w.astype(jnp.bfloat16), rows_of(1, mk, g), preferred_element_type=jnp.float32)
    for i in range(4):
        total = jnp.sum(tot[i], axis=1, keepdims=True)
        out = (acc[i] / total).astype(jnp.bfloat16)
        for h in range(HEADS):
            done[i, :, h * HD:(h + 1) * HD] = out[h * ROWS:(h + 1) * ROWS]
    for k in range(NY):
        outs[k][...] = done[(head + k) & 3].reshape(2, PART, WIDE)


def project_kernel(where, *refs):
    a_in, w_in, (mine, theirs), (a_all, sems) = refs[:NX], refs[NX:NX + 4], refs[NX + 4:NX + 6], refs[NX + 6:]
    copies = []
    for k in range(NY):
        for j in range(NX):
            copy = pltpu.make_async_copy(a_in[j].at[:, k], a_all.at[k, where[j]], sems.at[k * NX + j])
            copy.start()
            copies.append(copy)
    count = NZ * PART
    c = [None, None]
    for k in range(NY):
        for copy in copies[k * NX:(k + 1) * NX]:
            copy.wait()
        lhs = a_all[k].reshape(NX * count, WIDE)
        for side in range(2):
            for i in range(2):
                w = w_in[2 * side + i][(where[NX] - k) & 3]
                cols = slice(i * WIDE // 2, (i + 1) * WIDE // 2)
                part = jnp.dot(lhs[:, cols], w, preferred_element_type=jnp.float32)
                c[side] = part if k + i == 0 else c[side] + part
    for side in range(2):
        out = c[side].astype(jnp.bfloat16)
        mine[side] = out[:2 * count]
        theirs[side] = out[2 * count:]


def place_kernel(spots, *refs):
    o_ref = refs[-1]
    for t in range(2):
        near, got, other = refs[3 * t:3 * t + 3]
        own = (near[0].astype(jnp.float32) + got[0].astype(jnp.float32)).astype(jnp.bfloat16)
        theirs = other[...]
        for h in range(2):
            for k in range(NZ):
                part = slice((h * NZ + k) * PART, (h * NZ + k + 1) * PART)
                inside = h * ROWS + t * PART
                row = pl.multiple_of(spots[k] * SPAN + inside, PART)
                o_ref[pl.ds(row, PART), :] = own[part]
                row = pl.multiple_of(spots[NZ + k] * SPAN + inside, PART)
                o_ref[pl.ds(row, PART), :] = theirs[part]


def per_device(queries, keys, values, out_weight, block_vis, seg_lengths):
    seq = lax.axis_index("seq")
    phase = lax.axis_index("phase")
    head = lax.axis_index("head")
    my_x, my_z, my_c = seq // 8, (seq // 2) % 4, seq % 2
    f32 = jnp.float32

    q_own = queries.reshape(2, SPAN, WIDE)
    q_far = from_seq(q_own, shift_x=2)
    half = my_x // 2

    kv = jnp.stack([keys.reshape(2, SPAN, HD), values.reshape(2, SPAN, HD)], 0)
    kv_x = over_x(gather_z(kv))
    kv_x, q_far = lax.optimization_barrier((kv_x, q_far))
    kva = jnp.stack(kv_x, 0).reshape(NX * NZ, 2, 2, SPAN, HD)
    kvb = from_seq(kva, flip_core=1)

    weights = [lax.all_gather(out_weight[:WIDE // 2], "head", axis=0)]

    tri = jnp.arange(SEGS)[None, :] < jnp.arange(SEGS)[:, None]
    starts = jnp.sum(jnp.where(tri, seg_lengths[None, :], 0), axis=1)

    def segment(pos):
        return jnp.sum((starts[1:] <= pos[..., None]).astype(jnp.int32), axis=-1)

    two = jnp.arange(2, dtype=jnp.int32)
    four = jnp.arange(4, dtype=jnp.int32)
    low = seq & 15
    high = low + 16
    q_span = jnp.where(four == 0, low, jnp.where(four == 1, high, jnp.where(four == 2, 63 - high, 63 - low)))
    q_pos = q_span[:, None] * SPAN + half * ROWS + jnp.arange(ROWS, dtype=jnp.int32)
    q_seg = segment(q_pos)
    q_lim = jnp.where(q_seg == SEGS - 1, SEGS - 1, 0)
    g = jnp.arange(8, dtype=jnp.int32)
    key_x = (my_x + g // 2) & 3
    key_z = my_z ^ ((g % 2)[:, None] * 2 + two)
    key_s = key_x[:, None, None] * 8 + key_z[:, None, :] * 2 + (my_c ^ two)[None, :, None]
    key_span = jnp.where(two[:, None, None, None] == 0, key_s[None], 63 - key_s[None])
    key_span = key_span.reshape(2, 8, 4)
    k_pos = (key_span[..., None] * SPAN + jnp.arange(SPAN, dtype=jnp.int32)).reshape(2, 8, 256)
    k_seg = segment(k_pos)
    blocks = jnp.arange(block_vis.shape[0], dtype=jnp.int32)
    vis_rows = jnp.sum(
        jnp.where(((q_span // 2)[:, None] == blocks)[..., None], block_vis[None], 0), axis=1
    )
    seen = jnp.sum(
        jnp.where((key_span // 2)[None, ..., None] == blocks, vis_rows[:, None, None, None, :], 0),
        axis=-1,
    )
    seen = jnp.repeat(seen, SPAN, axis=-1).reshape(4, 2, 8, 256)
    k_code = jnp.where(seen == 1, k_seg[None], HIDDEN).reshape(64, 1, 256)
    k_pos = k_pos.reshape(16, 1, 256)
    wide = lambda v: jnp.broadcast_to(v[..., None], (4, ROWS, 256))
    scalars = jnp.stack([low // 4, high // 4, my_x, my_z // 2, half, head])

    rows = HEADS * ROWS
    smem = pl.BlockSpec(memory_space=pltpu.SMEM)
    vmem = pl.BlockSpec(memory_space=pltpu.VMEM)
    hbm = pl.BlockSpec(memory_space=pltpu.HBM)
    heads_out = pl.pallas_call(
        attention_kernel,
        name="attention",
        out_shape=(jax.ShapeDtypeStruct((2, PART, WIDE), jnp.bfloat16),) * NY,
        in_specs=[smem] + [vmem] * 9,
        out_specs=(vmem,) * NY,
        scratch_shapes=[
            pltpu.VMEM((BOTH, 2, rows, 256), f32),
            pltpu.VMEM((SINGLE, rows, 256), f32),
            pltpu.VMEM((4, rows, HD), jnp.bfloat16),
            pltpu.VMEM((4, rows, HD), f32),
            pltpu.VMEM((4, rows, HD), f32),
            pltpu.VMEM((4, rows, HD), f32),
            pltpu.VMEM((4, ROWS, WIDE), jnp.bfloat16),
        ],
        compiler_params=pltpu.CompilerParams(vmem_limit_bytes=24 << 20),
    )(scalars, q_own, q_far, kva, kvb, k_code, k_pos, wide(q_seg), wide(q_lim), wide(q_pos))

    heads_in = [heads_out[0]] + [up_head(heads_out[k], k) for k in (1, 2, 3)]
    part = [jnp.stack([v[t] for v in heads_in], 0) for t in range(2)]
    part[0], part[1], weight = lax.optimization_barrier((part[0], part[1], out_weight[WIDE // 2:]))
    weights += [lax.all_gather(weight, "head", axis=0)]
    part_z, late, weights[0] = lax.optimization_barrier((gather_z(part[0]), part[1], weights[0]))
    weights_other = [from_seq(weights[0], flip_core=1)]
    part_x = over_x(part_z)
    late_z = gather_z(late)
    part_x, late_z, weights[1] = lax.optimization_barrier((part_x, late_z, weights[1]))
    part_x = [part_x, over_x(late_z)]
    weights_other += [from_seq(weights[1], flip_core=1)]

    x_of = (my_x + four) & 3
    ends = (x_of & 1) ^ (head // 2)
    where = jnp.concatenate([jnp.where(ends == phase, 0, 2) + x_of // 2, head[None]])
    z_of = my_z ^ four
    place = jnp.concatenate([2 * z_of + my_c, 2 * z_of + (1 - my_c)])
    spots = jnp.where(head < 2, place, 7 - place)
    piece = jax.ShapeDtypeStruct((2, 2 * NZ * PART, 512), jnp.bfloat16)
    pieces = []
    for t in range(2):
        mine, theirs = pl.pallas_call(
            project_kernel,
            name="project",
            out_shape=(piece, piece),
            in_specs=[smem] + [hbm] * NX + [vmem] * 4,
            out_specs=(vmem, vmem),
            scratch_shapes=[
                pltpu.VMEM((NY, NX, NZ, PART, WIDE), jnp.bfloat16),
                pltpu.SemaphoreType.DMA((NX * NY,)),
            ],
            compiler_params=pltpu.CompilerParams(vmem_limit_bytes=24 << 20),
        )(where, *[off_chip(v) for v in part_x[t]], *[on_chip(w) for w in weights + weights_other])
        got = lax.ppermute(theirs, "phase", [(0, 1), (1, 0)])
        for_other = (mine[1].astype(f32) + got[1].astype(f32)).astype(jnp.bfloat16)
        pieces += [mine, got, from_seq(for_other, flip_core=1)]
    return pl.pallas_call(
        place_kernel,
        name="place",
        out_shape=jax.ShapeDtypeStruct((8 * SPAN, 512), jnp.bfloat16),
        in_specs=[smem] + [vmem] * 6,
        out_specs=vmem,
        compiler_params=pltpu.CompilerParams(vmem_limit_bytes=16 << 20),
    )(spots, *pieces)


def solution(mesh):
    return jax.shard_map(
        per_device,
        mesh=mesh,
        in_specs=(
            P("seq", None, None, ("head", "phase")),
            P("seq", None, None, ("head", "phase")),
            P("seq", None, None, ("head", "phase")),
            P(("head", "phase"), "seq"),
            P(),
            P(),
        ),
        out_specs=P(("head", "phase"), "seq"),
        check_vma=False,
    )
```

```python
import math

import jax
import jax.numpy as jnp
from jax import lax
from jax.experimental import pallas as pl
from jax.experimental.pallas import tpu as pltpu
from jax.sharding import PartitionSpec as P

HD = 128
SEGS = 10
SPAN = 64
ROWS = 32
PART = 16
NX, NZ, NC = 4, 4, 2
NY = 4
HEADS = 8
WIDE = HEADS * HD
NEG = -1e30
HIDDEN = 1 << 20
BOTH = 8
SINGLE = 18


def places_of_seq(shift_x=0, flip_z=0, flip_core=0):
    pairs = []
    for x in range(NX):
        for z in range(NZ):
            for c in range(NC):
                src = (x * NZ + z) * NC + c
                dst = (((x - shift_x) % NX) * NZ + (z ^ flip_z)) * NC + (c ^ flip_core)
                pairs.append((src, dst))
    return pairs


def from_seq(a, **kw):
    return lax.ppermute(a, "seq", places_of_seq(**kw))


def swap_head(a, k):
    return lax.ppermute(a, "head", [(y, y ^ k) for y in range(NY)])


def gather_z(a):
    return jnp.stack([a] + [from_seq(a, flip_z=k) for k in (1, 2, 3)], 0)


def over_x(a):
    return [a] + [from_seq(a, shift_x=k) for k in (1, 2, 3)]


def on_chip(a):
    return pltpu.with_memory_space_constraint(a, pltpu.VMEM)


def off_chip(a):
    return pltpu.with_memory_space_constraint(a, pltpu.HBM)


def attention_kernel(
    sc, q_own, q_far, kva, kvb, kcode, kpos, qseg, qlim, qpos, *rest
):
    outs, (both, single, qs, mx, acc, tot, done) = rest[:NY], rest[NY:]
    tile_lo, tile_hi, my_x, my_zh, half, head = sc[0], sc[1], sc[2], sc[3], sc[4], sc[5]
    rows = HEADS * ROWS
    start = pl.multiple_of(half * ROWS, ROWS)

    for m in range(2):
        near = q_own[m, pl.ds(start, ROWS), :]
        far = q_far[m, pl.ds(start, ROWS), :]
        low = jnp.where(half == 0, near, far)
        high = jnp.where(half == 0, far, near)
        for h in range(HEADS):
            cols = slice(h * HD, (h + 1) * HD)
            qs[3 * m, h * ROWS:(h + 1) * ROWS, :] = low[:, cols]
            qs[1 + m, h * ROWS:(h + 1) * ROWS, :] = high[:, cols]
    mx[...] = jnp.full_like(mx, NEG)
    acc[...] = jnp.zeros_like(acc)
    tot[...] = jnp.zeros_like(tot)

    def tile_of(t):
        pair, u = t // 9, t % 9
        early = u <= (tile_lo if pair == 0 else tile_hi)
        group = jnp.where(early, pair, 3 - pair)
        mk = jnp.where(early, 0, 1)
        g = jnp.where(early, u, u - 1)
        g_rel = (((g >> 1) - my_x) & 3) * 2 + ((g & 1) ^ my_zh)
        return group, mk, g_rel

    def rows_of(kv, mk, g):
        return jnp.concatenate(
            [kva[2 * g, kv, mk], kva[2 * g + 1, kv, mk], kvb[2 * g, kv, mk], kvb[2 * g + 1, kv, mk]], 0
        )

    def masked(s, group, mk, g):
        code = kcode[(group * 2 + mk) * 8 + g]
        ok = ((code == qseg[group]) | (code <= qlim[group])) & (kpos[mk * 8 + g] <= qpos[group])
        return jnp.where(ok[None], s.reshape(HEADS, ROWS, 256), NEG).reshape(rows, 256)

    def dot_keys(q, keys):
        return lax.dot_general(q, keys, (((1,), (1,)), ((), ())), preferred_element_type=jnp.float32)

    for t in range(BOTH):
        s = dot_keys(qs[2:4].reshape(2 * rows, HD), rows_of(0, 0, t))
        for i in range(2):
            part = masked(s[i * rows:(i + 1) * rows], 2 + i, 0, t)
            both[t, i] = part
            mx[2 + i] = jnp.maximum(mx[2 + i], jnp.maximum(part[:, :HD], part[:, HD:]))
    for t in range(SINGLE):
        group, mk, g = tile_of(t)
        s = masked(dot_keys(qs[group], rows_of(0, mk, g)), group, mk, g)
        single[t] = s
        mx[group] = jnp.maximum(mx[group], jnp.maximum(s[:, :HD], s[:, HD:]))
    for i in range(4):
        mx[i] = jnp.broadcast_to(jnp.max(mx[i], axis=1, keepdims=True), (rows, HD))
    factor = math.log2(math.e) / math.sqrt(HD)

    def weigh(s, peak):
        return jnp.exp2((s - jnp.concatenate([peak, peak], 1)) * factor)

    for t in range(BOTH):
        parts = []
        for i in range(2):
            w = weigh(both[t, i], mx[2 + i])
            tot[2 + i] += w[:, :HD] + w[:, HD:]
            parts.append(w.astype(jnp.bfloat16))
        mixed = jnp.dot(jnp.concatenate(parts, 0), rows_of(1, 0, t), preferred_element_type=jnp.float32)
        for i in range(2):
            acc[2 + i] += mixed[i * rows:(i + 1) * rows]
    for t in range(SINGLE):
        group, mk, g = tile_of(t)
        w = weigh(single[t], mx[group])
        tot[group] += w[:, :HD] + w[:, HD:]
        acc[group] += jnp.dot(w.astype(jnp.bfloat16), rows_of(1, mk, g), preferred_element_type=jnp.float32)
    for i in range(4):
        total = jnp.sum(tot[i], axis=1, keepdims=True)
        out = (acc[i] / total).astype(jnp.bfloat16)
        for h in range(HEADS):
            done[i, :, h * HD:(h + 1) * HD] = out[h * ROWS:(h + 1) * ROWS]
    for k in range(NY):
        outs[k][...] = done[head ^ k].reshape(2, PART, WIDE)


def project_kernel(where, *refs):
    a_in, w_in, (mine, theirs), (a_all, sems) = refs[:5], refs[5:9], refs[9:11], refs[11:]
    copies = []
    for k in range(NY):
        for j, slot in enumerate((0, 1, 3, 2, 2)):
            to = a_all.at[k, where[slot]]
            if slot == 2:
                to = to.at[pl.ds(2 * (j - 3), 2)]
            copy = pltpu.make_async_copy(a_in[j].at[:, k], to, sems.at[5 * k + j])
            copy.start()
            copies.append(copy)
    count = NZ * PART
    c = [None, None]
    for k in range(NY):
        for copy in copies[5 * k:5 * k + 5]:
            copy.wait()
        lhs = a_all[k].reshape(NX * count, WIDE)
        for side in range(2):
            part = jnp.dot(lhs, w_in[2 * side + k // 2][k % 2], preferred_element_type=jnp.float32)
            c[side] = part if k == 0 else c[side] + part
    for side in range(2):
        out = c[side].astype(jnp.bfloat16)
        mine[side] = out[:2 * count]
        theirs[side] = out[2 * count:]


def place_kernel(spots, *refs):
    o_ref = refs[-1]
    for t in range(2):
        near, got, other = refs[3 * t:3 * t + 3]
        own = (near[0].astype(jnp.float32) + got[0].astype(jnp.float32)).astype(jnp.bfloat16)
        theirs = other[...]
        for h in range(2):
            for k in range(NZ):
                part = slice((h * NZ + k) * PART, (h * NZ + k + 1) * PART)
                inside = h * ROWS + t * PART
                row = pl.multiple_of(spots[k] * SPAN + inside, PART)
                o_ref[pl.ds(row, PART), :] = own[part]
                row = pl.multiple_of(spots[NZ + k] * SPAN + inside, PART)
                o_ref[pl.ds(row, PART), :] = theirs[part]


def per_device(queries, keys, values, out_weight, block_vis, seg_lengths):
    seq = lax.axis_index("seq")
    phase = lax.axis_index("phase")
    head = lax.axis_index("head")
    my_x, my_z, my_c = seq // 8, (seq // 2) % 4, seq % 2
    f32 = jnp.float32

    q_own = queries.reshape(2, SPAN, WIDE)
    q_far = from_seq(q_own, shift_x=2)
    half = my_x // 2

    kv = jnp.stack([keys.reshape(2, SPAN, HD), values.reshape(2, SPAN, HD)], 0)
    kv_x = over_x(gather_z(kv))
    kv_x, q_far, weight = lax.optimization_barrier((kv_x, q_far, swap_head(out_weight, 1)))
    weights = [jnp.stack([out_weight, weight], 0)]
    kva = jnp.stack(kv_x, 0).reshape(NX * NZ, 2, 2, SPAN, HD)
    kvb = from_seq(kva, flip_core=1)

    tri = jnp.arange(SEGS)[None, :] < jnp.arange(SEGS)[:, None]
    starts = jnp.sum(jnp.where(tri, seg_lengths[None, :], 0), axis=1)

    def segment(pos):
        return jnp.sum((starts[1:] <= pos[..., None]).astype(jnp.int32), axis=-1)

    two = jnp.arange(2, dtype=jnp.int32)
    four = jnp.arange(4, dtype=jnp.int32)
    low = seq & 15
    high = low + 16
    q_span = jnp.where(four == 0, low, jnp.where(four == 1, high, jnp.where(four == 2, 63 - high, 63 - low)))
    q_pos = q_span[:, None] * SPAN + half * ROWS + jnp.arange(ROWS, dtype=jnp.int32)
    q_seg = segment(q_pos)
    q_lim = jnp.where(q_seg == SEGS - 1, SEGS - 1, 0)
    g = jnp.arange(8, dtype=jnp.int32)
    key_x = (my_x + g // 2) & 3
    key_z = my_z ^ ((g % 2)[:, None] * 2 + two)
    key_s = key_x[:, None, None] * 8 + key_z[:, None, :] * 2 + (my_c ^ two)[None, :, None]
    key_span = jnp.where(two[:, None, None, None] == 0, key_s[None], 63 - key_s[None])
    key_span = key_span.reshape(2, 8, 4)
    k_pos = (key_span[..., None] * SPAN + jnp.arange(SPAN, dtype=jnp.int32)).reshape(2, 8, 256)
    k_seg = segment(k_pos)
    blocks = jnp.arange(block_vis.shape[0], dtype=jnp.int32)
    vis_rows = jnp.sum(
        jnp.where(((q_span // 2)[:, None] == blocks)[..., None], block_vis[None], 0), axis=1
    )
    seen = jnp.sum(
        jnp.where((key_span // 2)[None, ..., None] == blocks, vis_rows[:, None, None, None, :], 0),
        axis=-1,
    )
    seen = jnp.repeat(seen, SPAN, axis=-1).reshape(4, 2, 8, 256)
    k_code = jnp.where(seen == 1, k_seg[None], HIDDEN).reshape(64, 1, 256)
    k_pos = k_pos.reshape(16, 1, 256)
    wide = lambda v: jnp.broadcast_to(v[..., None], (4, ROWS, 256))
    scalars = jnp.stack([low // 4, high // 4, my_x, my_z // 2, half, head])

    rows = HEADS * ROWS
    smem = pl.BlockSpec(memory_space=pltpu.SMEM)
    vmem = pl.BlockSpec(memory_space=pltpu.VMEM)
    hbm = pl.BlockSpec(memory_space=pltpu.HBM)
    heads_out = pl.pallas_call(
        attention_kernel,
        name="attention",
        out_shape=(jax.ShapeDtypeStruct((2, PART, WIDE), jnp.bfloat16),) * NY,
        in_specs=[smem] + [vmem] * 9,
        out_specs=(vmem,) * NY,
        scratch_shapes=[
            pltpu.VMEM((BOTH, 2, rows, 256), f32),
            pltpu.VMEM((SINGLE, rows, 256), f32),
            pltpu.VMEM((4, rows, HD), jnp.bfloat16),
            pltpu.VMEM((4, rows, HD), f32),
            pltpu.VMEM((4, rows, HD), f32),
            pltpu.VMEM((4, rows, HD), f32),
            pltpu.VMEM((4, ROWS, WIDE), jnp.bfloat16),
        ],
        compiler_params=pltpu.CompilerParams(vmem_limit_bytes=24 << 20),
    )(scalars, q_own, q_far, kva, kvb, k_code, k_pos, wide(q_seg), wide(q_lim), wide(q_pos))

    heads_in = [heads_out[0]] + [swap_head(heads_out[k], k) for k in (1, 2, 3)]
    part = [jnp.stack([v[t] for v in heads_in], 0) for t in range(2)]
    part[0], part[1], weights[0] = lax.optimization_barrier((part[0], part[1], weights[0]))
    weights += [swap_head(weights[0], 2)]
    part_z, late, weights[0] = lax.optimization_barrier((gather_z(part[0]), part[1], weights[0]))
    weights_other = [from_seq(weights[0], flip_core=1)]

    right, left = from_seq(part_z, shift_x=1), from_seq(part_z, shift_x=3)
    late_z = gather_z(late)
    right, left, late_z = lax.optimization_barrier((right, left, late_z))
    early_x = [part_z, right, left, from_seq(right[:2], shift_x=1), from_seq(left[2:], shift_x=3)]
    right, left = from_seq(late_z, shift_x=1), from_seq(late_z, shift_x=3)
    early_x, right, left, weights[1] = lax.optimization_barrier((early_x, right, left, weights[1]))
    part_x = [early_x, [late_z, right, left, from_seq(right[:2], shift_x=1), from_seq(left[2:], shift_x=3)]]
    weights_other += [from_seq(weights[1], flip_core=1)]

    x_of = (my_x + four) & 3
    ends = (x_of & 1) ^ (head // 2)
    where = jnp.where(ends == phase, 0, 2) + x_of // 2
    z_of = my_z ^ four
    place = jnp.concatenate([2 * z_of + my_c, 2 * z_of + (1 - my_c)])
    spots = jnp.where(head < 2, place, 7 - place)
    piece = jax.ShapeDtypeStruct((2, 2 * NZ * PART, 512), jnp.bfloat16)
    pieces = []
    for t in range(2):
        mine, theirs = pl.pallas_call(
            project_kernel,
            name="project",
            out_shape=(piece, piece),
            in_specs=[smem] + [hbm] * 5 + [vmem] * 4,
            out_specs=(vmem, vmem),
            scratch_shapes=[
                pltpu.VMEM((NY, NX, NZ, PART, WIDE), jnp.bfloat16),
                pltpu.SemaphoreType.DMA((5 * NY,)),
            ],
            compiler_params=pltpu.CompilerParams(vmem_limit_bytes=24 << 20),
        )(where, *[off_chip(v) for v in part_x[t]], *[on_chip(w) for w in weights + weights_other])
        got = lax.ppermute(theirs, "phase", [(0, 1), (1, 0)])
        for_other = (mine[1].astype(f32) + got[1].astype(f32)).astype(jnp.bfloat16)
        pieces += [mine, got, from_seq(for_other, flip_core=1)]
    return pl.pallas_call(
        place_kernel,
        name="place",
        out_shape=jax.ShapeDtypeStruct((8 * SPAN, 512), jnp.bfloat16),
        in_specs=[smem] + [vmem] * 6,
        out_specs=vmem,
        compiler_params=pltpu.CompilerParams(vmem_limit_bytes=16 << 20),
    )(spots, *pieces)


def solution(mesh):
    return jax.shard_map(
        per_device,
        mesh=mesh,
        in_specs=(
            P("seq", None, None, ("head", "phase")),
            P("seq", None, None, ("head", "phase")),
            P("seq", None, None, ("head", "phase")),
            P(("head", "phase"), "seq"),
            P(),
            P(),
        ),
        out_specs=P(("head", "phase"), "seq"),
        check_vma=False,
    )
```

```python
import math

import jax
import jax.numpy as jnp
from jax import lax
from jax.experimental import pallas as pl
from jax.experimental.pallas import tpu as pltpu
from jax.sharding import PartitionSpec as P

HD = 128
SEGS = 10
SPAN = 64
ROWS = 32
PART = 16
NX, NZ, NC = 4, 4, 2
NY = 4
HEADS = 8
WIDE = HEADS * HD
NEG = -1e30
HIDDEN = 1 << 20
BOTH = 8
SINGLE = 18


def places_of_seq(shift_x=0, flip_z=0, flip_core=0):
    pairs = []
    for x in range(NX):
        for z in range(NZ):
            for c in range(NC):
                src = (x * NZ + z) * NC + c
                dst = (((x - shift_x) % NX) * NZ + (z ^ flip_z)) * NC + (c ^ flip_core)
                pairs.append((src, dst))
    return pairs


def from_seq(a, **kw):
    return lax.ppermute(a, "seq", places_of_seq(**kw))


def swap_head(a, k):
    return lax.ppermute(a, "head", [(y, y ^ k) for y in range(NY)])


def gather_z(a):
    return jnp.stack([a] + [from_seq(a, flip_z=k) for k in (1, 2, 3)], 0)


def over_x(a):
    return [a] + [from_seq(a, shift_x=k) for k in (1, 2, 3)]


def on_chip(a):
    return pltpu.with_memory_space_constraint(a, pltpu.VMEM)


def off_chip(a):
    return pltpu.with_memory_space_constraint(a, pltpu.HBM)


def attention_kernel(
    sc, q_own, q_far, kva, kvb, kcode, kpos, qseg, qlim, qpos, *rest
):
    outs, (both, single, qs, mx, acc, tot, done) = rest[:NY], rest[NY:]
    tile_lo, tile_hi, my_x, my_zh, half, head = sc[0], sc[1], sc[2], sc[3], sc[4], sc[5]
    rows = HEADS * ROWS
    start = pl.multiple_of(half * ROWS, ROWS)

    for m in range(2):
        near = q_own[m, pl.ds(start, ROWS), :]
        far = q_far[m, pl.ds(start, ROWS), :]
        low = jnp.where(half == 0, near, far)
        high = jnp.where(half == 0, far, near)
        for h in range(HEADS):
            cols = slice(h * HD, (h + 1) * HD)
            qs[3 * m, h * ROWS:(h + 1) * ROWS, :] = low[:, cols]
            qs[1 + m, h * ROWS:(h + 1) * ROWS, :] = high[:, cols]
    mx[...] = jnp.full_like(mx, NEG)
    acc[...] = jnp.zeros_like(acc)
    tot[...] = jnp.zeros_like(tot)

    def tile_of(t):
        pair, u = t // 9, t % 9
        early = u <= (tile_lo if pair == 0 else tile_hi)
        group = jnp.where(early, pair, 3 - pair)
        mk = jnp.where(early, 0, 1)
        g = jnp.where(early, u, u - 1)
        g_rel = (((g >> 1) - my_x) & 3) * 2 + ((g & 1) ^ my_zh)
        return group, mk, g_rel

    def rows_of(kv, mk, g):
        return jnp.concatenate(
            [kva[2 * g, kv, mk], kva[2 * g + 1, kv, mk], kvb[2 * g, kv, mk], kvb[2 * g + 1, kv, mk]], 0
        )

    def masked(s, group, mk, g):
        code = kcode[(group * 2 + mk) * 8 + g]
        ok = ((code == qseg[group]) | (code <= qlim[group])) & (kpos[mk * 8 + g] <= qpos[group])
        return jnp.where(ok[None], s.reshape(HEADS, ROWS, 256), NEG).reshape(rows, 256)

    def dot_keys(q, keys):
        return lax.dot_general(q, keys, (((1,), (1,)), ((), ())), preferred_element_type=jnp.float32)

    for t in range(BOTH):
        s = dot_keys(qs[2:4].reshape(2 * rows, HD), rows_of(0, 0, t))
        for i in range(2):
            part = masked(s[i * rows:(i + 1) * rows], 2 + i, 0, t)
            both[t, i] = part
            mx[2 + i] = jnp.maximum(mx[2 + i], jnp.maximum(part[:, :HD], part[:, HD:]))
    for t in range(SINGLE):
        group, mk, g = tile_of(t)
        s = masked(dot_keys(qs[group], rows_of(0, mk, g)), group, mk, g)
        single[t] = s
        mx[group] = jnp.maximum(mx[group], jnp.maximum(s[:, :HD], s[:, HD:]))
    for i in range(4):
        mx[i] = jnp.broadcast_to(jnp.max(mx[i], axis=1, keepdims=True), (rows, HD))
    factor = math.log2(math.e) / math.sqrt(HD)

    def weigh(s, peak):
        return jnp.exp2((s - jnp.concatenate([peak, peak], 1)) * factor)

    for t in range(BOTH):
        parts = []
        for i in range(2):
            w = weigh(both[t, i], mx[2 + i])
            tot[2 + i] += w[:, :HD] + w[:, HD:]
            parts.append(w.astype(jnp.bfloat16))
        mixed = jnp.dot(jnp.concatenate(parts, 0), rows_of(1, 0, t), preferred_element_type=jnp.float32)
        for i in range(2):
            acc[2 + i] += mixed[i * rows:(i + 1) * rows]
    for t in range(SINGLE):
        group, mk, g = tile_of(t)
        w = weigh(single[t], mx[group])
        tot[group] += w[:, :HD] + w[:, HD:]
        acc[group] += jnp.dot(w.astype(jnp.bfloat16), rows_of(1, mk, g), preferred_element_type=jnp.float32)
    for i in range(4):
        total = jnp.sum(tot[i], axis=1, keepdims=True)
        out = (acc[i] / total).astype(jnp.bfloat16)
        for h in range(HEADS):
            done[i, :, h * HD:(h + 1) * HD] = out[h * ROWS:(h + 1) * ROWS]
    for k in range(NY):
        outs[k][...] = done[head ^ k].reshape(2, PART, WIDE)


def project_kernel(where, *refs):
    a_in, w_in, (mine, theirs), (a_all, sems) = refs[:5], refs[5:9], refs[9:11], refs[11:]
    copies = []
    for k in range(NY):
        for j, slot in enumerate((0, 1, 3, 2, 2)):
            to = a_all.at[k, where[slot]]
            if slot == 2:
                to = to.at[pl.ds(2 * (j - 3), 2)]
            copy = pltpu.make_async_copy(a_in[j].at[:, k], to, sems.at[5 * k + j])
            copy.start()
            copies.append(copy)
    count = NZ * PART
    c = [None, None]
    for k in range(NY):
        for copy in copies[5 * k:5 * k + 5]:
            copy.wait()
        lhs = a_all[k].reshape(NX * count, WIDE)
        for side in range(2):
            for i in range(2):
                cols = slice(i * WIDE // 2, (i + 1) * WIDE // 2)
                w = w_in[2 * side + k // 2][k % 2, cols]
                part = jnp.dot(lhs[:, cols], w, preferred_element_type=jnp.float32)
                c[side] = part if k + i == 0 else c[side] + part
    for side in range(2):
        out = c[side].astype(jnp.bfloat16)
        mine[side] = out[:2 * count]
        theirs[side] = out[2 * count:]


def place_kernel(spots, *refs):
    o_ref = refs[-1]
    for t in range(2):
        near, got, other = refs[3 * t:3 * t + 3]
        own = (near[0].astype(jnp.float32) + got[0].astype(jnp.float32)).astype(jnp.bfloat16)
        theirs = other[...]
        for h in range(2):
            for k in range(NZ):
                part = slice((h * NZ + k) * PART, (h * NZ + k + 1) * PART)
                inside = h * ROWS + t * PART
                row = pl.multiple_of(spots[k] * SPAN + inside, PART)
                o_ref[pl.ds(row, PART), :] = own[part]
                row = pl.multiple_of(spots[NZ + k] * SPAN + inside, PART)
                o_ref[pl.ds(row, PART), :] = theirs[part]


def per_device(queries, keys, values, out_weight, block_vis, seg_lengths):
    seq = lax.axis_index("seq")
    phase = lax.axis_index("phase")
    head = lax.axis_index("head")
    my_x, my_z, my_c = seq // 8, (seq // 2) % 4, seq % 2
    f32 = jnp.float32

    q_own = queries.reshape(2, SPAN, WIDE)
    q_far = from_seq(q_own, shift_x=2)
    half = my_x // 2

    kv = jnp.stack([keys.reshape(2, SPAN, HD), values.reshape(2, SPAN, HD)], 0)
    kv_x = over_x(gather_z(kv))
    kv_x, q_far = lax.optimization_barrier((kv_x, q_far))
    kva = jnp.stack(kv_x, 0).reshape(NX * NZ, 2, 2, SPAN, HD)
    kvb = from_seq(kva, flip_core=1)
    kva, kvb, weight = lax.optimization_barrier((kva, kvb, swap_head(out_weight, 1)))

    tri = jnp.arange(SEGS)[None, :] < jnp.arange(SEGS)[:, None]
    starts = jnp.sum(jnp.where(tri, seg_lengths[None, :], 0), axis=1)

    def segment(pos):
        return jnp.sum((starts[1:] <= pos[..., None]).astype(jnp.int32), axis=-1)

    two = jnp.arange(2, dtype=jnp.int32)
    four = jnp.arange(4, dtype=jnp.int32)
    low = seq & 15
    high = low + 16
    q_span = jnp.where(four == 0, low, jnp.where(four == 1, high, jnp.where(four == 2, 63 - high, 63 - low)))
    q_pos = q_span[:, None] * SPAN + half * ROWS + jnp.arange(ROWS, dtype=jnp.int32)
    q_seg = segment(q_pos)
    q_lim = jnp.where(q_seg == SEGS - 1, SEGS - 1, 0)
    g = jnp.arange(8, dtype=jnp.int32)
    key_x = (my_x + g // 2) & 3
    key_z = my_z ^ ((g % 2)[:, None] * 2 + two)
    key_s = key_x[:, None, None] * 8 + key_z[:, None, :] * 2 + (my_c ^ two)[None, :, None]
    key_span = jnp.where(two[:, None, None, None] == 0, key_s[None], 63 - key_s[None])
    key_span = key_span.reshape(2, 8, 4)
    k_pos = (key_span[..., None] * SPAN + jnp.arange(SPAN, dtype=jnp.int32)).reshape(2, 8, 256)
    k_seg = segment(k_pos)
    blocks = jnp.arange(block_vis.shape[0], dtype=jnp.int32)
    vis_rows = jnp.sum(
        jnp.where(((q_span // 2)[:, None] == blocks)[..., None], block_vis[None], 0), axis=1
    )
    seen = jnp.sum(
        jnp.where((key_span // 2)[None, ..., None] == blocks, vis_rows[:, None, None, None, :], 0),
        axis=-1,
    )
    seen = jnp.repeat(seen, SPAN, axis=-1).reshape(4, 2, 8, 256)
    k_code = jnp.where(seen == 1, k_seg[None], HIDDEN).reshape(64, 1, 256)
    k_pos = k_pos.reshape(16, 1, 256)
    wide = lambda v: jnp.broadcast_to(v[..., None], (4, ROWS, 256))
    scalars = jnp.stack([low // 4, high // 4, my_x, my_z // 2, half, head])

    rows = HEADS * ROWS
    smem = pl.BlockSpec(memory_space=pltpu.SMEM)
    vmem = pl.BlockSpec(memory_space=pltpu.VMEM)
    hbm = pl.BlockSpec(memory_space=pltpu.HBM)
    heads_out = pl.pallas_call(
        attention_kernel,
        name="attention",
        out_shape=(jax.ShapeDtypeStruct((2, PART, WIDE), jnp.bfloat16),) * NY,
        in_specs=[smem] + [vmem] * 9,
        out_specs=(vmem,) * NY,
        scratch_shapes=[
            pltpu.VMEM((BOTH, 2, rows, 256), f32),
            pltpu.VMEM((SINGLE, rows, 256), f32),
            pltpu.VMEM((4, rows, HD), jnp.bfloat16),
            pltpu.VMEM((4, rows, HD), f32),
            pltpu.VMEM((4, rows, HD), f32),
            pltpu.VMEM((4, rows, HD), f32),
            pltpu.VMEM((4, ROWS, WIDE), jnp.bfloat16),
        ],
        compiler_params=pltpu.CompilerParams(vmem_limit_bytes=24 << 20),
    )(scalars, q_own, q_far, kva, kvb, k_code, k_pos, wide(q_seg), wide(q_lim), wide(q_pos))

    *heads_out, weight = lax.optimization_barrier((*heads_out, weight))
    weights = [jnp.stack([out_weight, weight], 0)]

    heads_in = [heads_out[0]] + [swap_head(heads_out[k], k) for k in (1, 2, 3)]
    part = [jnp.stack([v[t] for v in heads_in], 0) for t in range(2)]
    part[0], part[1], weights[0] = lax.optimization_barrier((part[0], part[1], weights[0]))
    weights += [swap_head(weights[0], 2)]
    part_z, late, weights[0] = lax.optimization_barrier((gather_z(part[0]), part[1], weights[0]))
    weights_other = [from_seq(weights[0], flip_core=1)]

    right, left = from_seq(part_z, shift_x=1), from_seq(part_z, shift_x=3)
    late_z = gather_z(late)
    right, left, late_z = lax.optimization_barrier((right, left, late_z))
    early_x = [part_z, right, left, from_seq(right[:2], shift_x=1), from_seq(left[2:], shift_x=3)]
    right, left = from_seq(late_z, shift_x=1), from_seq(late_z, shift_x=3)
    early_x, right, left, weights[1] = lax.optimization_barrier((early_x, right, left, weights[1]))
    part_x = [early_x, [late_z, right, left, from_seq(right[:2], shift_x=1), from_seq(left[2:], shift_x=3)]]
    weights_other += [from_seq(weights[1], flip_core=1)]

    x_of = (my_x + four) & 3
    ends = (x_of & 1) ^ (head // 2)
    where = jnp.where(ends == phase, 0, 2) + x_of // 2
    z_of = my_z ^ four
    place = jnp.concatenate([2 * z_of + my_c, 2 * z_of + (1 - my_c)])
    spots = jnp.where(head < 2, place, 7 - place)
    piece = jax.ShapeDtypeStruct((2, 2 * NZ * PART, 512), jnp.bfloat16)
    pieces = []
    for t in range(2):
        mine, theirs = pl.pallas_call(
            project_kernel,
            name="project",
            out_shape=(piece, piece),
            in_specs=[smem] + [hbm] * 5 + [vmem] * 4,
            out_specs=(vmem, vmem),
            scratch_shapes=[
                pltpu.VMEM((NY, NX, NZ, PART, WIDE), jnp.bfloat16),
                pltpu.SemaphoreType.DMA((5 * NY,)),
            ],
            compiler_params=pltpu.CompilerParams(vmem_limit_bytes=24 << 20),
        )(where, *[off_chip(v) for v in part_x[t]], *[on_chip(w) for w in weights + weights_other])
        got = lax.ppermute(theirs, "phase", [(0, 1), (1, 0)])
        for_other = (mine[1].astype(f32) + got[1].astype(f32)).astype(jnp.bfloat16)
        pieces += [mine, got, from_seq(for_other, flip_core=1)]
    return pl.pallas_call(
        place_kernel,
        name="place",
        out_shape=jax.ShapeDtypeStruct((8 * SPAN, 512), jnp.bfloat16),
        in_specs=[smem] + [vmem] * 6,
        out_specs=vmem,
        compiler_params=pltpu.CompilerParams(vmem_limit_bytes=16 << 20),
    )(spots, *pieces)


def solution(mesh):
    return jax.shard_map(
        per_device,
        mesh=mesh,
        in_specs=(
            P("seq", None, None, ("head", "phase")),
            P("seq", None, None, ("head", "phase")),
            P("seq", None, None, ("head", "phase")),
            P(("head", "phase"), "seq"),
            P(),
            P(),
        ),
        out_specs=P(("head", "phase"), "seq"),
        check_vma=False,
    )
```

```python
import math

import jax
import jax.numpy as jnp
from jax import lax
from jax.experimental import pallas as pl
from jax.experimental.pallas import tpu as pltpu
from jax.sharding import PartitionSpec as P

HD = 128
SEGS = 10
SPAN = 64
ROWS = 32
PART = 16
NX, NZ, NC = 4, 4, 2
NY = 4
HEADS = 8
WIDE = HEADS * HD
NEG = -1e30
HIDDEN = 1 << 20
BOTH = 8
SINGLE = 18


def places_of_seq(shift_x=0, flip_z=0, flip_core=0):
    pairs = []
    for x in range(NX):
        for z in range(NZ):
            for c in range(NC):
                src = (x * NZ + z) * NC + c
                dst = (((x - shift_x) % NX) * NZ + (z ^ flip_z)) * NC + (c ^ flip_core)
                pairs.append((src, dst))
    return pairs


def from_seq(a, **kw):
    return lax.ppermute(a, "seq", places_of_seq(**kw))


def swap_head(a, k):
    return lax.ppermute(a, "head", [(y, y ^ k) for y in range(NY)])


def gather_z(a):
    return jnp.stack([a] + [from_seq(a, flip_z=k) for k in (1, 2, 3)], 0)


def over_x(a):
    return [a] + [from_seq(a, shift_x=k) for k in (1, 2, 3)]


def on_chip(a):
    return pltpu.with_memory_space_constraint(a, pltpu.VMEM)


def off_chip(a):
    return pltpu.with_memory_space_constraint(a, pltpu.HBM)


def attention_kernel(
    sc, q_own, q_far, kva, kvb, kcode, kpos, qseg, qlim, qpos, *rest
):
    outs, (both, single, qs, mx, acc, tot, done) = rest[:NY], rest[NY:]
    tile_lo, tile_hi, my_x, my_zh, half, head = sc[0], sc[1], sc[2], sc[3], sc[4], sc[5]
    rows = HEADS * ROWS
    start = pl.multiple_of(half * ROWS, ROWS)

    for m in range(2):
        near = q_own[m, pl.ds(start, ROWS), :]
        far = q_far[m, pl.ds(start, ROWS), :]
        low = jnp.where(half == 0, near, far)
        high = jnp.where(half == 0, far, near)
        for h in range(HEADS):
            cols = slice(h * HD, (h + 1) * HD)
            qs[3 * m, h * ROWS:(h + 1) * ROWS, :] = low[:, cols]
            qs[1 + m, h * ROWS:(h + 1) * ROWS, :] = high[:, cols]
    mx[...] = jnp.full_like(mx, NEG)
    acc[...] = jnp.zeros_like(acc)
    tot[...] = jnp.zeros_like(tot)

    def tile_of(t):
        pair, u = t // 9, t % 9
        early = u <= (tile_lo if pair == 0 else tile_hi)
        group = jnp.where(early, pair, 3 - pair)
        mk = jnp.where(early, 0, 1)
        g = jnp.where(early, u, u - 1)
        g_rel = (((g >> 1) - my_x) & 3) * 2 + ((g & 1) ^ my_zh)
        return group, mk, g_rel

    def rows_of(kv, mk, g):
        return jnp.concatenate(
            [kva[2 * g, kv, mk], kva[2 * g + 1, kv, mk], kvb[2 * g, kv, mk], kvb[2 * g + 1, kv, mk]], 0
        )

    def masked(s, group, mk, g):
        code = kcode[(group * 2 + mk) * 8 + g]
        ok = ((code == qseg[group]) | (code <= qlim[group])) & (kpos[mk * 8 + g] <= qpos[group])
        return jnp.where(ok[None], s.reshape(HEADS, ROWS, 256), NEG).reshape(rows, 256)

    def dot_keys(q, keys):
        return lax.dot_general(q, keys, (((1,), (1,)), ((), ())), preferred_element_type=jnp.float32)

    for t in range(BOTH):
        s = dot_keys(qs[2:4].reshape(2 * rows, HD), rows_of(0, 0, t))
        for i in range(2):
            part = masked(s[i * rows:(i + 1) * rows], 2 + i, 0, t)
            both[t, i] = part
            mx[2 + i] = jnp.maximum(mx[2 + i], jnp.maximum(part[:, :HD], part[:, HD:]))
    for t in range(SINGLE):
        group, mk, g = tile_of(t)
        s = masked(dot_keys(qs[group], rows_of(0, mk, g)), group, mk, g)
        single[t] = s
        mx[group] = jnp.maximum(mx[group], jnp.maximum(s[:, :HD], s[:, HD:]))
    for i in range(4):
        mx[i] = jnp.broadcast_to(jnp.max(mx[i], axis=1, keepdims=True), (rows, HD))
    factor = math.log2(math.e) / math.sqrt(HD)

    def weigh(s, peak):
        return jnp.exp2((s - jnp.concatenate([peak, peak], 1)) * factor)

    for t in range(BOTH):
        parts = []
        for i in range(2):
            w = weigh(both[t, i], mx[2 + i])
            tot[2 + i] += w[:, :HD] + w[:, HD:]
            parts.append(w.astype(jnp.bfloat16))
        mixed = jnp.dot(jnp.concatenate(parts, 0), rows_of(1, 0, t), preferred_element_type=jnp.float32)
        for i in range(2):
            acc[2 + i] += mixed[i * rows:(i + 1) * rows]
    for t in range(SINGLE):
        group, mk, g = tile_of(t)
        w = weigh(single[t], mx[group])
        tot[group] += w[:, :HD] + w[:, HD:]
        acc[group] += jnp.dot(w.astype(jnp.bfloat16), rows_of(1, mk, g), preferred_element_type=jnp.float32)
    for i in range(4):
        total = jnp.sum(tot[i], axis=1, keepdims=True)
        out = (acc[i] / total).astype(jnp.bfloat16)
        for h in range(HEADS):
            done[i, :, h * HD:(h + 1) * HD] = out[h * ROWS:(h + 1) * ROWS]
    for k in range(NY):
        outs[k][...] = done[head ^ k].reshape(2, PART, WIDE)


def project_kernel(where, *refs):
    a_in, w_in, (mine, theirs), (a_all, sems) = refs[:5], refs[5:9], refs[9:11], refs[11:]
    copies = []
    for k in range(NY):
        for j, slot in enumerate((0, 1, 3, 2, 2)):
            to = a_all.at[k, where[slot]]
            if slot == 2:
                to = to.at[pl.ds(2 * (j - 3), 2)]
            copy = pltpu.make_async_copy(a_in[j].at[:, k], to, sems.at[5 * k + j])
            copy.start()
            copies.append(copy)
    count = NZ * PART
    c = [None, None]
    for k in range(NY):
        for copy in copies[5 * k:5 * k + 5]:
            copy.wait()
        lhs = a_all[k].reshape(NX * count, WIDE)
        for side in range(2):
            for i in range(2):
                cols = slice(i * WIDE // 2, (i + 1) * WIDE // 2)
                w = w_in[2 * side + k // 2][k % 2, cols]
                part = jnp.dot(lhs[:, cols], w, preferred_element_type=jnp.float32)
                c[side] = part if k + i == 0 else c[side] + part
    for side in range(2):
        out = c[side].astype(jnp.bfloat16)
        mine[side] = out[:2 * count]
        theirs[side] = out[2 * count:]


def place_kernel(spots, *refs):
    o_ref = refs[-1]
    for t in range(2):
        near, got, other = refs[3 * t:3 * t + 3]
        own = (near[0].astype(jnp.float32) + got[0].astype(jnp.float32)).astype(jnp.bfloat16)
        theirs = other[...]
        for h in range(2):
            for k in range(NZ):
                part = slice((h * NZ + k) * PART, (h * NZ + k + 1) * PART)
                inside = h * ROWS + t * PART
                row = pl.multiple_of(spots[k] * SPAN + inside, PART)
                o_ref[pl.ds(row, PART), :] = own[part]
                row = pl.multiple_of(spots[NZ + k] * SPAN + inside, PART)
                o_ref[pl.ds(row, PART), :] = theirs[part]


def per_device(queries, keys, values, out_weight, block_vis, seg_lengths):
    seq = lax.axis_index("seq")
    phase = lax.axis_index("phase")
    head = lax.axis_index("head")
    my_x, my_z, my_c = seq // 8, (seq // 2) % 4, seq % 2
    f32 = jnp.float32

    q_own = queries.reshape(2, SPAN, WIDE)
    q_far = from_seq(q_own, shift_x=2)
    half = my_x // 2

    kv = jnp.stack([keys.reshape(2, SPAN, HD), values.reshape(2, SPAN, HD)], 0)
    kv_x = over_x(gather_z(kv))
    kv_x, q_far = lax.optimization_barrier((kv_x, q_far))
    kva = jnp.stack(kv_x, 0).reshape(NX * NZ, 2, 2, SPAN, HD)
    kvb = from_seq(kva, flip_core=1)
    kva, kvb, weight = lax.optimization_barrier((kva, kvb, swap_head(out_weight, 1)))

    tri = jnp.arange(SEGS)[None, :] < jnp.arange(SEGS)[:, None]
    starts = jnp.sum(jnp.where(tri, seg_lengths[None, :], 0), axis=1)

    def segment(pos):
        return jnp.sum((starts[1:] <= pos[..., None]).astype(jnp.int32), axis=-1)

    two = jnp.arange(2, dtype=jnp.int32)
    four = jnp.arange(4, dtype=jnp.int32)
    low = seq & 15
    high = low + 16
    q_span = jnp.where(four == 0, low, jnp.where(four == 1, high, jnp.where(four == 2, 63 - high, 63 - low)))
    q_pos = q_span[:, None] * SPAN + half * ROWS + jnp.arange(ROWS, dtype=jnp.int32)
    q_seg = segment(q_pos)
    q_lim = jnp.where(q_seg == SEGS - 1, SEGS - 1, 0)
    g = jnp.arange(8, dtype=jnp.int32)
    key_x = (my_x + g // 2) & 3
    key_z = my_z ^ ((g % 2)[:, None] * 2 + two)
    key_s = key_x[:, None, None] * 8 + key_z[:, None, :] * 2 + (my_c ^ two)[None, :, None]
    key_span = jnp.where(two[:, None, None, None] == 0, key_s[None], 63 - key_s[None])
    key_span = key_span.reshape(2, 8, 4)
    k_pos = (key_span[..., None] * SPAN + jnp.arange(SPAN, dtype=jnp.int32)).reshape(2, 8, 256)
    k_seg = segment(k_pos)
    blocks = jnp.arange(block_vis.shape[0], dtype=jnp.int32)
    vis_rows = jnp.sum(
        jnp.where(((q_span // 2)[:, None] == blocks)[..., None], block_vis[None], 0), axis=1
    )
    seen = jnp.sum(
        jnp.where((key_span // 2)[None, ..., None] == blocks, vis_rows[:, None, None, None, :], 0),
        axis=-1,
    )
    seen = jnp.repeat(seen, SPAN, axis=-1).reshape(4, 2, 8, 256)
    k_code = jnp.where(seen == 1, k_seg[None], HIDDEN).reshape(64, 1, 256)
    k_pos = k_pos.reshape(16, 1, 256)
    wide = lambda v: jnp.broadcast_to(v[..., None], (4, ROWS, 256))
    scalars = jnp.stack([low // 4, high // 4, my_x, my_z // 2, half, head])

    rows = HEADS * ROWS
    smem = pl.BlockSpec(memory_space=pltpu.SMEM)
    vmem = pl.BlockSpec(memory_space=pltpu.VMEM)
    hbm = pl.BlockSpec(memory_space=pltpu.HBM)
    heads_out = pl.pallas_call(
        attention_kernel,
        name="attention",
        out_shape=(jax.ShapeDtypeStruct((2, PART, WIDE), jnp.bfloat16),) * NY,
        in_specs=[smem] + [vmem] * 9,
        out_specs=(vmem,) * NY,
        scratch_shapes=[
            pltpu.VMEM((BOTH, 2, rows, 256), f32),
            pltpu.VMEM((SINGLE, rows, 256), f32),
            pltpu.VMEM((4, rows, HD), jnp.bfloat16),
            pltpu.VMEM((4, rows, HD), f32),
            pltpu.VMEM((4, rows, HD), f32),
            pltpu.VMEM((4, rows, HD), f32),
            pltpu.VMEM((4, ROWS, WIDE), jnp.bfloat16),
        ],
        compiler_params=pltpu.CompilerParams(vmem_limit_bytes=24 << 20),
    )(scalars, q_own, q_far, kva, kvb, k_code, k_pos, wide(q_seg), wide(q_lim), wide(q_pos))

    *heads_out, weight = lax.optimization_barrier((*heads_out, weight))
    weights = [jnp.stack([out_weight, weight], 0)]

    heads_in = [heads_out[0]] + [swap_head(heads_out[k], k) for k in (1, 2, 3)]
    heads_in[3], weights[0] = lax.optimization_barrier((heads_in[3], weights[0]))
    part = [jnp.stack([v[t] for v in heads_in], 0) for t in range(2)]
    weights += [swap_head(weights[0], 2)]
    part_z, late, weights[0] = lax.optimization_barrier((gather_z(part[0]), part[1], weights[0]))
    weights_other = [from_seq(weights[0], flip_core=1)]

    right, left = from_seq(part_z, shift_x=1), from_seq(part_z, shift_x=3)
    late_z = gather_z(late)
    right, left, late_z = lax.optimization_barrier((right, left, late_z))
    early_x = [part_z, right, left, from_seq(right[:2], shift_x=1), from_seq(left[2:], shift_x=3)]
    right, left = from_seq(late_z, shift_x=1), from_seq(late_z, shift_x=3)
    early_x, right, left, weights[1] = lax.optimization_barrier((early_x, right, left, weights[1]))
    part_x = [early_x, [late_z, right, left, from_seq(right[:2], shift_x=1), from_seq(left[2:], shift_x=3)]]
    weights_other += [from_seq(weights[1], flip_core=1)]

    x_of = (my_x + four) & 3
    ends = (x_of & 1) ^ (head // 2)
    where = jnp.where(ends == phase, 0, 2) + x_of // 2
    z_of = my_z ^ four
    place = jnp.concatenate([2 * z_of + my_c, 2 * z_of + (1 - my_c)])
    spots = jnp.where(head < 2, place, 7 - place)
    piece = jax.ShapeDtypeStruct((2, 2 * NZ * PART, 512), jnp.bfloat16)
    pieces = []
    for t in range(2):
        mine, theirs = pl.pallas_call(
            project_kernel,
            name="project",
            out_shape=(piece, piece),
            in_specs=[smem] + [hbm] * 3 + [vmem] * 6,
            out_specs=(vmem, vmem),
            scratch_shapes=[
                pltpu.VMEM((NY, NX, NZ, PART, WIDE), jnp.bfloat16),
                pltpu.SemaphoreType.DMA((5 * NY,)),
            ],
            compiler_params=pltpu.CompilerParams(vmem_limit_bytes=24 << 20),
        )(where, *[off_chip(v) for v in part_x[t][:3]], *[on_chip(v) for v in part_x[t][3:]], *[on_chip(w) for w in weights + weights_other])
        got = lax.ppermute(theirs, "phase", [(0, 1), (1, 0)])
        for_other = (mine[1].astype(f32) + got[1].astype(f32)).astype(jnp.bfloat16)
        pieces += [mine, got, from_seq(for_other, flip_core=1)]
    return pl.pallas_call(
        place_kernel,
        name="place",
        out_shape=jax.ShapeDtypeStruct((8 * SPAN, 512), jnp.bfloat16),
        in_specs=[smem] + [vmem] * 6,
        out_specs=vmem,
        compiler_params=pltpu.CompilerParams(vmem_limit_bytes=16 << 20),
    )(spots, *pieces)


def solution(mesh):
    return jax.shard_map(
        per_device,
        mesh=mesh,
        in_specs=(
            P("seq", None, None, ("head", "phase")),
            P("seq", None, None, ("head", "phase")),
            P("seq", None, None, ("head", "phase")),
            P(("head", "phase"), "seq"),
            P(),
            P(),
        ),
        out_specs=P(("head", "phase"), "seq"),
        check_vma=False,
    )
```

```python
import math

import jax
import jax.numpy as jnp
from jax import lax
from jax.experimental import pallas as pl
from jax.experimental.pallas import tpu as pltpu
from jax.sharding import PartitionSpec as P

HD = 128
SEGS = 10
SPAN = 64
ROWS = 32
PART = 16
NX, NZ, NC = 4, 4, 2
NY = 4
HEADS = 8
WIDE = HEADS * HD
NEG = -1e30
HIDDEN = 1 << 20
BOTH = 8
SINGLE = 18


def places_of_seq(shift_x=0, flip_z=0, flip_core=0):
    pairs = []
    for x in range(NX):
        for z in range(NZ):
            for c in range(NC):
                src = (x * NZ + z) * NC + c
                dst = (((x - shift_x) % NX) * NZ + (z ^ flip_z)) * NC + (c ^ flip_core)
                pairs.append((src, dst))
    return pairs


def from_seq(a, **kw):
    return lax.ppermute(a, "seq", places_of_seq(**kw))


def swap_head(a, k):
    return lax.ppermute(a, "head", [(y, y ^ k) for y in range(NY)])


def gather_z(a, axis=0):
    return jnp.stack([a] + [from_seq(a, flip_z=k) for k in (1, 2, 3)], axis)


def over_x(a):
    return [a] + [from_seq(a, shift_x=k) for k in (1, 2, 3)]


def on_chip(a):
    return pltpu.with_memory_space_constraint(a, pltpu.VMEM)


def off_chip(a):
    return pltpu.with_memory_space_constraint(a, pltpu.HBM)


def attention_kernel(
    sc, q_own, q_far, kva, kvb, kcode, kpos, qseg, qlim, qpos, *rest
):
    outs, (both, single, qs, mx, acc, tot, done) = rest[:NY], rest[NY:]
    tile_lo, tile_hi, my_x, my_zh, half, head = sc[0], sc[1], sc[2], sc[3], sc[4], sc[5]
    rows = HEADS * ROWS
    start = pl.multiple_of(half * ROWS, ROWS)

    for m in range(2):
        near = q_own[m, pl.ds(start, ROWS), :]
        far = q_far[m, pl.ds(start, ROWS), :]
        low = jnp.where(half == 0, near, far)
        high = jnp.where(half == 0, far, near)
        for h in range(HEADS):
            cols = slice(h * HD, (h + 1) * HD)
            qs[3 * m, h * ROWS:(h + 1) * ROWS, :] = low[:, cols]
            qs[1 + m, h * ROWS:(h + 1) * ROWS, :] = high[:, cols]
    mx[...] = jnp.full_like(mx, NEG)
    acc[...] = jnp.zeros_like(acc)
    tot[...] = jnp.zeros_like(tot)

    def tile_of(t):
        pair, u = t // 9, t % 9
        early = u <= (tile_lo if pair == 0 else tile_hi)
        group = jnp.where(early, pair, 3 - pair)
        mk = jnp.where(early, 0, 1)
        g = jnp.where(early, u, u - 1)
        g_rel = (((g >> 1) - my_x) & 3) * 2 + ((g & 1) ^ my_zh)
        return group, mk, g_rel

    def rows_of(kv, mk, g):
        return jnp.concatenate(
            [kva[2 * g, kv, mk], kva[2 * g + 1, kv, mk], kvb[2 * g, kv, mk], kvb[2 * g + 1, kv, mk]], 0
        )

    def masked(s, group, mk, g):
        code = kcode[(group * 2 + mk) * 8 + g]
        ok = ((code == qseg[group]) | (code <= qlim[group])) & (kpos[mk * 8 + g] <= qpos[group])
        return jnp.where(ok[None], s.reshape(HEADS, ROWS, 256), NEG).reshape(rows, 256)

    def dot_keys(q, keys):
        return lax.dot_general(q, keys, (((1,), (1,)), ((), ())), preferred_element_type=jnp.float32)

    for t in range(BOTH):
        s = dot_keys(qs[2:4].reshape(2 * rows, HD), rows_of(0, 0, t))
        for i in range(2):
            part = masked(s[i * rows:(i + 1) * rows], 2 + i, 0, t)
            both[t, i] = part
            mx[2 + i] = jnp.maximum(mx[2 + i], jnp.maximum(part[:, :HD], part[:, HD:]))
    for t in range(SINGLE):
        group, mk, g = tile_of(t)
        s = masked(dot_keys(qs[group], rows_of(0, mk, g)), group, mk, g)
        single[t] = s
        mx[group] = jnp.maximum(mx[group], jnp.maximum(s[:, :HD], s[:, HD:]))
    for i in range(4):
        mx[i] = jnp.broadcast_to(jnp.max(mx[i], axis=1, keepdims=True), (rows, HD))
    factor = math.log2(math.e) / math.sqrt(HD)

    def weigh(s, peak):
        return jnp.exp2((s - jnp.concatenate([peak, peak], 1)) * factor)

    for t in range(BOTH):
        parts = []
        for i in range(2):
            w = weigh(both[t, i], mx[2 + i])
            tot[2 + i] += w[:, :HD] + w[:, HD:]
            parts.append(w.astype(jnp.bfloat16))
        mixed = jnp.dot(jnp.concatenate(parts, 0), rows_of(1, 0, t), preferred_element_type=jnp.float32)
        for i in range(2):
            acc[2 + i] += mixed[i * rows:(i + 1) * rows]
    for t in range(SINGLE):
        group, mk, g = tile_of(t)
        w = weigh(single[t], mx[group])
        tot[group] += w[:, :HD] + w[:, HD:]
        acc[group] += jnp.dot(w.astype(jnp.bfloat16), rows_of(1, mk, g), preferred_element_type=jnp.float32)
    for i in range(4):
        total = jnp.sum(tot[i], axis=1, keepdims=True)
        out = (acc[i] / total).astype(jnp.bfloat16)
        for h in range(HEADS):
            done[i, :, h * HD:(h + 1) * HD] = out[h * ROWS:(h + 1) * ROWS]
    for k in range(NY):
        outs[k][...] = done[head ^ k].reshape(2, PART, WIDE)


def project_kernel(where, *refs):
    a_in, far, w_in, (mine, theirs), (a_all, c_all, sems) = refs[:3], refs[3:5], refs[5:9], refs[9:11], refs[11:]
    copies = []
    for part in range(2):
        heads = pl.ds(2 * part, 2)
        for j in range(3):
            copy = pltpu.make_async_copy(a_in[j].at[heads], a_all.at[j, heads], sems.at[3 * part + j])
            copy.start()
            copies.append(copy)
    count = NZ * PART
    c = [None, None]
    for k in range(NY):
        if k % 2 == 0:
            for copy in copies[3 * (k // 2):3 * (k // 2) + 3]:
                copy.wait()
        lhs = [a_all[j, k].reshape(count, WIDE) for j in range(3)] + [far[k // 2][k % 2].reshape(count, WIDE)]
        lhs = jnp.concatenate(lhs, 0)
        for side in range(2):
            for i in range(2):
                cols = slice(i * WIDE // 2, (i + 1) * WIDE // 2)
                w = w_in[2 * side + k // 2][k % 2, cols]
                part = jnp.dot(lhs[:, cols], w, preferred_element_type=jnp.float32)
                c[side] = part if k + i == 0 else c[side] + part
    for side in range(2):
        out = c[side].astype(jnp.bfloat16)
        for j, slot in enumerate((0, 1, 3, 2)):
            c_all[where[slot], side] = out[j * count:(j + 1) * count]
    for side in range(2):
        mine[side] = c_all[0:2, side].reshape(2 * count, 512)
        theirs[side] = c_all[2:4, side].reshape(2 * count, 512)


def place_kernel(spots, *refs):
    o_ref = refs[-1]
    for t in range(2):
        near, got, other = refs[3 * t:3 * t + 3]
        own = (near[0].astype(jnp.float32) + got[0].astype(jnp.float32)).astype(jnp.bfloat16)
        theirs = other[...]
        for h in range(2):
            for k in range(NZ):
                part = slice((h * NZ + k) * PART, (h * NZ + k + 1) * PART)
                inside = h * ROWS + t * PART
                row = pl.multiple_of(spots[k] * SPAN + inside, PART)
                o_ref[pl.ds(row, PART), :] = own[part]
                row = pl.multiple_of(spots[NZ + k] * SPAN + inside, PART)
                o_ref[pl.ds(row, PART), :] = theirs[part]


def per_device(queries, keys, values, out_weight, block_vis, seg_lengths):
    seq = lax.axis_index("seq")
    phase = lax.axis_index("phase")
    head = lax.axis_index("head")
    my_x, my_z, my_c = seq // 8, (seq // 2) % 4, seq % 2
    f32 = jnp.float32

    q_own = queries.reshape(2, SPAN, WIDE)
    q_far = from_seq(q_own, shift_x=2)
    half = my_x // 2

    kv = jnp.stack([keys.reshape(2, SPAN, HD), values.reshape(2, SPAN, HD)], 0)
    kv_x = over_x(gather_z(kv))
    kv_x, q_far = lax.optimization_barrier((kv_x, q_far))
    kva = jnp.stack(kv_x, 0).reshape(NX * NZ, 2, 2, SPAN, HD)
    kvb = from_seq(kva, flip_core=1)
    kva, kvb, weight = lax.optimization_barrier((kva, kvb, swap_head(out_weight, 1)))

    tri = jnp.arange(SEGS)[None, :] < jnp.arange(SEGS)[:, None]
    starts = jnp.sum(jnp.where(tri, seg_lengths[None, :], 0), axis=1)

    def segment(pos):
        return jnp.sum((starts[1:] <= pos[..., None]).astype(jnp.int32), axis=-1)

    two = jnp.arange(2, dtype=jnp.int32)
    four = jnp.arange(4, dtype=jnp.int32)
    low = seq & 15
    high = low + 16
    q_span = jnp.where(four == 0, low, jnp.where(four == 1, high, jnp.where(four == 2, 63 - high, 63 - low)))
    q_pos = q_span[:, None] * SPAN + half * ROWS + jnp.arange(ROWS, dtype=jnp.int32)
    q_seg = segment(q_pos)
    q_lim = jnp.where(q_seg == SEGS - 1, SEGS - 1, 0)
    g = jnp.arange(8, dtype=jnp.int32)
    key_x = (my_x + g // 2) & 3
    key_z = my_z ^ ((g % 2)[:, None] * 2 + two)
    key_s = key_x[:, None, None] * 8 + key_z[:, None, :] * 2 + (my_c ^ two)[None, :, None]
    key_span = jnp.where(two[:, None, None, None] == 0, key_s[None], 63 - key_s[None])
    key_span = key_span.reshape(2, 8, 4)
    k_pos = (key_span[..., None] * SPAN + jnp.arange(SPAN, dtype=jnp.int32)).reshape(2, 8, 256)
    k_seg = segment(k_pos)
    blocks = jnp.arange(block_vis.shape[0], dtype=jnp.int32)
    vis_rows = jnp.sum(
        jnp.where(((q_span // 2)[:, None] == blocks)[..., None], block_vis[None], 0), axis=1
    )
    seen = jnp.sum(
        jnp.where((key_span // 2)[None, ..., None] == blocks, vis_rows[:, None, None, None, :], 0),
        axis=-1,
    )
    seen = jnp.repeat(seen, SPAN, axis=-1).reshape(4, 2, 8, 256)
    k_code = jnp.where(seen == 1, k_seg[None], HIDDEN).reshape(64, 1, 256)
    k_pos = k_pos.reshape(16, 1, 256)
    wide = lambda v: jnp.broadcast_to(v[..., None], (4, ROWS, 256))
    scalars = jnp.stack([low // 4, high // 4, my_x, my_z // 2, half, head])

    rows = HEADS * ROWS
    smem = pl.BlockSpec(memory_space=pltpu.SMEM)
    vmem = pl.BlockSpec(memory_space=pltpu.VMEM)
    hbm = pl.BlockSpec(memory_space=pltpu.HBM)
    heads_out = pl.pallas_call(
        attention_kernel,
        name="attention",
        out_shape=(jax.ShapeDtypeStruct((2, PART, WIDE), jnp.bfloat16),) * NY,
        in_specs=[smem] + [vmem] * 9,
        out_specs=(vmem,) * NY,
        scratch_shapes=[
            pltpu.VMEM((BOTH, 2, rows, 256), f32),
            pltpu.VMEM((SINGLE, rows, 256), f32),
            pltpu.VMEM((4, rows, HD), jnp.bfloat16),
            pltpu.VMEM((4, rows, HD), f32),
            pltpu.VMEM((4, rows, HD), f32),
            pltpu.VMEM((4, rows, HD), f32),
            pltpu.VMEM((4, ROWS, WIDE), jnp.bfloat16),
        ],
        compiler_params=pltpu.CompilerParams(vmem_limit_bytes=24 << 20),
    )(scalars, q_own, q_far, kva, kvb, k_code, k_pos, wide(q_seg), wide(q_lim), wide(q_pos))

    *heads_out, weight = lax.optimization_barrier((*heads_out, weight))
    weights = [jnp.stack([out_weight, weight], 0)]

    heads_in = [heads_out[0]] + [swap_head(heads_out[k], k) for k in (1, 2, 3)]
    heads_in[3], weights[0] = lax.optimization_barrier((heads_in[3], weights[0]))
    part = [jnp.stack([v[t] for v in heads_in], 0) for t in range(2)]
    weights += [swap_head(weights[0], 2)]
    part_z, late, weights[0] = lax.optimization_barrier((gather_z(part[0], 1), part[1], weights[0]))
    weights_other = [from_seq(weights[0], flip_core=1)]

    right, left = from_seq(part_z, shift_x=1), from_seq(part_z, shift_x=3)
    late_z = gather_z(late, 1)
    right, left, late_z = lax.optimization_barrier((right, left, late_z))
    early_x = [part_z, right, left, from_seq(right[:2], shift_x=1), from_seq(left[2:], shift_x=3)]
    right, left = from_seq(late_z, shift_x=1), from_seq(late_z, shift_x=3)
    early_x, right, left, weights[1] = lax.optimization_barrier((early_x, right, left, weights[1]))
    part_x = [early_x, [late_z, right, left, from_seq(right[:2], shift_x=1), from_seq(left[2:], shift_x=3)]]
    weights_other += [from_seq(weights[1], flip_core=1)]

    x_of = (my_x + four) & 3
    ends = (x_of & 1) ^ (head // 2)
    where = jnp.where(ends == phase, 0, 2) + x_of // 2
    z_of = my_z ^ four
    place = jnp.concatenate([2 * z_of + my_c, 2 * z_of + (1 - my_c)])
    spots = jnp.where(head < 2, place, 7 - place)
    piece = jax.ShapeDtypeStruct((2, 2 * NZ * PART, 512), jnp.bfloat16)
    pieces = []
    for t in range(2):
        mine, theirs = pl.pallas_call(
            project_kernel,
            name="project",
            out_shape=(piece, piece),
            in_specs=[smem] + [hbm] * 3 + [vmem] * 6,
            out_specs=(vmem, vmem),
            scratch_shapes=[
                pltpu.VMEM((3, NY, NZ, PART, WIDE), jnp.bfloat16),
                pltpu.VMEM((NX, 2, NZ * PART, 512), jnp.bfloat16),
                pltpu.SemaphoreType.DMA((6,)),
            ],
            compiler_params=pltpu.CompilerParams(vmem_limit_bytes=24 << 20),
        )(where, *[off_chip(v) for v in part_x[t][:3]], *[on_chip(v) for v in part_x[t][3:]], *[on_chip(w) for w in weights + weights_other])
        got = lax.ppermute(theirs, "phase", [(0, 1), (1, 0)])
        for_other = (mine[1].astype(f32) + got[1].astype(f32)).astype(jnp.bfloat16)
        pieces += [mine, got, from_seq(for_other, flip_core=1)]
    return pl.pallas_call(
        place_kernel,
        name="place",
        out_shape=jax.ShapeDtypeStruct((8 * SPAN, 512), jnp.bfloat16),
        in_specs=[smem] + [vmem] * 6,
        out_specs=vmem,
        compiler_params=pltpu.CompilerParams(vmem_limit_bytes=16 << 20),
    )(spots, *pieces)


def solution(mesh):
    return jax.shard_map(
        per_device,
        mesh=mesh,
        in_specs=(
            P("seq", None, None, ("head", "phase")),
            P("seq", None, None, ("head", "phase")),
            P("seq", None, None, ("head", "phase")),
            P(("head", "phase"), "seq"),
            P(),
            P(),
        ),
        out_specs=P(("head", "phase"), "seq"),
        check_vma=False,
    )
```

```python
import math

import jax
import jax.numpy as jnp
from jax import lax
from jax.experimental import pallas as pl
from jax.experimental.pallas import tpu as pltpu
from jax.sharding import PartitionSpec as P

HD = 128
SEGS = 10
SPAN = 64
ROWS = 32
PART = 16
NX, NZ, NC = 4, 4, 2
NY = 4
HEADS = 8
WIDE = HEADS * HD
NEG = -1e30
HIDDEN = 1 << 20
BOTH = 8
SINGLE = 18


def places_of_seq(shift_x=0, flip_z=0, flip_core=0):
    pairs = []
    for x in range(NX):
        for z in range(NZ):
            for c in range(NC):
                src = (x * NZ + z) * NC + c
                dst = (((x - shift_x) % NX) * NZ + (z ^ flip_z)) * NC + (c ^ flip_core)
                pairs.append((src, dst))
    return pairs


def from_seq(a, **kw):
    return lax.ppermute(a, "seq", places_of_seq(**kw))


def swap_head(a, k):
    return lax.ppermute(a, "head", [(y, y ^ k) for y in range(NY)])


def gather_z(a):
    return jnp.stack([a] + [from_seq(a, flip_z=k) for k in (1, 2, 3)], 0)


def over_x(a):
    return [a] + [from_seq(a, shift_x=k) for k in (1, 2, 3)]


def on_chip(a):
    return pltpu.with_memory_space_constraint(a, pltpu.VMEM)


def off_chip(a):
    return pltpu.with_memory_space_constraint(a, pltpu.HBM)


def attention_kernel(
    sc, q_own, q_far, kva, kvb, kcode, kpos, qseg, qlim, qpos, *rest
):
    outs, (both, single, qs, mx, acc, tot, done) = rest[:NY], rest[NY:]
    tile_lo, tile_hi, my_x, my_zh, half, head = sc[0], sc[1], sc[2], sc[3], sc[4], sc[5]
    rows = HEADS * ROWS
    start = pl.multiple_of(half * ROWS, ROWS)

    for m in range(2):
        near = q_own[m, pl.ds(start, ROWS), :]
        far = q_far[m, pl.ds(start, ROWS), :]
        low = jnp.where(half == 0, near, far)
        high = jnp.where(half == 0, far, near)
        for h in range(HEADS):
            cols = slice(h * HD, (h + 1) * HD)
            qs[3 * m, h * ROWS:(h + 1) * ROWS, :] = low[:, cols]
            qs[1 + m, h * ROWS:(h + 1) * ROWS, :] = high[:, cols]
    mx[...] = jnp.full_like(mx, NEG)
    acc[...] = jnp.zeros_like(acc)
    tot[...] = jnp.zeros_like(tot)

    def tile_of(t):
        pair, u = t // 9, t % 9
        early = u <= (tile_lo if pair == 0 else tile_hi)
        group = jnp.where(early, pair, 3 - pair)
        mk = jnp.where(early, 0, 1)
        g = jnp.where(early, u, u - 1)
        g_rel = (((g >> 1) - my_x) & 3) * 2 + ((g & 1) ^ my_zh)
        return group, mk, g_rel

    def rows_of(kv, mk, g):
        return jnp.concatenate(
            [kva[2 * g, kv, mk], kva[2 * g + 1, kv, mk], kvb[2 * g, kv, mk], kvb[2 * g + 1, kv, mk]], 0
        )

    def masked(s, group, mk, g):
        code = kcode[(group * 2 + mk) * 8 + g]
        ok = ((code == qseg[group]) | (code <= qlim[group])) & (kpos[mk * 8 + g] <= qpos[group])
        return jnp.where(ok[None], s.reshape(HEADS, ROWS, 256), NEG).reshape(rows, 256)

    def dot_keys(q, keys):
        return lax.dot_general(q, keys, (((1,), (1,)), ((), ())), preferred_element_type=jnp.float32)

    for t in range(BOTH):
        s = dot_keys(qs[2:4].reshape(2 * rows, HD), rows_of(0, 0, t))
        for i in range(2):
            part = masked(s[i * rows:(i + 1) * rows], 2 + i, 0, t)
            both[t, i] = part
            mx[2 + i] = jnp.maximum(mx[2 + i], jnp.maximum(part[:, :HD], part[:, HD:]))
    for t in range(SINGLE):
        group, mk, g = tile_of(t)
        s = masked(dot_keys(qs[group], rows_of(0, mk, g)), group, mk, g)
        single[t] = s
        mx[group] = jnp.maximum(mx[group], jnp.maximum(s[:, :HD], s[:, HD:]))
    for i in range(4):
        mx[i] = jnp.broadcast_to(jnp.max(mx[i], axis=1, keepdims=True), (rows, HD))
    factor = math.log2(math.e) / math.sqrt(HD)

    def weigh(s, peak):
        return jnp.exp2((s - jnp.concatenate([peak, peak], 1)) * factor)

    for t in range(BOTH):
        parts = []
        for i in range(2):
            w = weigh(both[t, i], mx[2 + i])
            tot[2 + i] += w[:, :HD] + w[:, HD:]
            parts.append(w.astype(jnp.bfloat16))
        mixed = jnp.dot(jnp.concatenate(parts, 0), rows_of(1, 0, t), preferred_element_type=jnp.float32)
        for i in range(2):
            acc[2 + i] += mixed[i * rows:(i + 1) * rows]
    for t in range(SINGLE):
        group, mk, g = tile_of(t)
        w = weigh(single[t], mx[group])
        tot[group] += w[:, :HD] + w[:, HD:]
        acc[group] += jnp.dot(w.astype(jnp.bfloat16), rows_of(1, mk, g), preferred_element_type=jnp.float32)
    for i in range(4):
        total = jnp.sum(tot[i], axis=1, keepdims=True)
        out = (acc[i] / total).astype(jnp.bfloat16)
        for h in range(HEADS):
            done[i, :, h * HD:(h + 1) * HD] = out[h * ROWS:(h + 1) * ROWS]
    for k in range(NY):
        outs[k][...] = done[head ^ k].reshape(2, PART, WIDE)


def project_kernel(where, *refs):
    a_in, w_in, (mine, theirs), (a_all, sems) = refs[:5], refs[5:9], refs[9:11], refs[11:]
    copies = []
    for k in range(NY):
        for j, slot in enumerate((0, 1, 3, 2)):
            zs = pl.ds(0, NZ)
            src = [(a_in[j], zs)]
            if slot == 2:
                src = [(a_in[3], pl.ds(0, 2)), (a_in[4], pl.ds(2, 2))]
            for ref, zs in src:
                to = a_all.at[where[slot], zs, :, pl.ds(k * WIDE, WIDE)]
                copy = pltpu.make_async_copy(ref.at[:, k], to, sems.at[len(copies)])
                copy.start()
                copies.append(copy)
    count = NZ * PART
    c = [None, None]
    for pair in range(2):
        for copy in copies[10 * pair:10 * pair + 10]:
            copy.wait()
        cols = pl.ds(2 * WIDE * pair, 2 * WIDE)
        lhs = a_all[:, :, :, cols].reshape(NX * count, 2 * WIDE)
        for side in range(2):
            w = w_in[2 * side + pair][...].reshape(2 * WIDE, 512)
            part = jnp.dot(lhs, w, preferred_element_type=jnp.float32)
            c[side] = part if pair == 0 else c[side] + part
    for side in range(2):
        out = c[side].astype(jnp.bfloat16)
        mine[side] = out[:2 * count]
        theirs[side] = out[2 * count:]


def place_kernel(spots, *refs):
    o_ref = refs[-1]
    for t in range(2):
        near, got, other = refs[3 * t:3 * t + 3]
        own = (near[0].astype(jnp.float32) + got[0].astype(jnp.float32)).astype(jnp.bfloat16)
        theirs = other[...]
        for h in range(2):
            for k in range(NZ):
                part = slice((h * NZ + k) * PART, (h * NZ + k + 1) * PART)
                inside = h * ROWS + t * PART
                row = pl.multiple_of(spots[k] * SPAN + inside, PART)
                o_ref[pl.ds(row, PART), :] = own[part]
                row = pl.multiple_of(spots[NZ + k] * SPAN + inside, PART)
                o_ref[pl.ds(row, PART), :] = theirs[part]


def per_device(queries, keys, values, out_weight, block_vis, seg_lengths):
    seq = lax.axis_index("seq")
    phase = lax.axis_index("phase")
    head = lax.axis_index("head")
    my_x, my_z, my_c = seq // 8, (seq // 2) % 4, seq % 2
    f32 = jnp.float32

    q_own = queries.reshape(2, SPAN, WIDE)
    q_far = from_seq(q_own, shift_x=2)
    half = my_x // 2

    kv = jnp.stack([keys.reshape(2, SPAN, HD), values.reshape(2, SPAN, HD)], 0)
    kv_x = over_x(gather_z(kv))
    kv_x, q_far = lax.optimization_barrier((kv_x, q_far))
    kva = jnp.stack(kv_x, 0).reshape(NX * NZ, 2, 2, SPAN, HD)
    kvb = from_seq(kva, flip_core=1)
    kva, kvb, weight = lax.optimization_barrier((kva, kvb, swap_head(out_weight, 1)))

    tri = jnp.arange(SEGS)[None, :] < jnp.arange(SEGS)[:, None]
    starts = jnp.sum(jnp.where(tri, seg_lengths[None, :], 0), axis=1)

    def segment(pos):
        return jnp.sum((starts[1:] <= pos[..., None]).astype(jnp.int32), axis=-1)

    two = jnp.arange(2, dtype=jnp.int32)
    four = jnp.arange(4, dtype=jnp.int32)
    low = seq & 15
    high = low + 16
    q_span = jnp.where(four == 0, low, jnp.where(four == 1, high, jnp.where(four == 2, 63 - high, 63 - low)))
    q_pos = q_span[:, None] * SPAN + half * ROWS + jnp.arange(ROWS, dtype=jnp.int32)
    q_seg = segment(q_pos)
    q_lim = jnp.where(q_seg == SEGS - 1, SEGS - 1, 0)
    g = jnp.arange(8, dtype=jnp.int32)
    key_x = (my_x + g // 2) & 3
    key_z = my_z ^ ((g % 2)[:, None] * 2 + two)
    key_s = key_x[:, None, None] * 8 + key_z[:, None, :] * 2 + (my_c ^ two)[None, :, None]
    key_span = jnp.where(two[:, None, None, None] == 0, key_s[None], 63 - key_s[None])
    key_span = key_span.reshape(2, 8, 4)
    k_pos = (key_span[..., None] * SPAN + jnp.arange(SPAN, dtype=jnp.int32)).reshape(2, 8, 256)
    k_seg = segment(k_pos)
    blocks = jnp.arange(block_vis.shape[0], dtype=jnp.int32)
    vis_rows = jnp.sum(
        jnp.where(((q_span // 2)[:, None] == blocks)[..., None], block_vis[None], 0), axis=1
    )
    seen = jnp.sum(
        jnp.where((key_span // 2)[None, ..., None] == blocks, vis_rows[:, None, None, None, :], 0),
        axis=-1,
    )
    seen = jnp.repeat(seen, SPAN, axis=-1).reshape(4, 2, 8, 256)
    k_code = jnp.where(seen == 1, k_seg[None], HIDDEN).reshape(64, 1, 256)
    k_pos = k_pos.reshape(16, 1, 256)
    wide = lambda v: jnp.broadcast_to(v[..., None], (4, ROWS, 256))
    scalars = jnp.stack([low // 4, high // 4, my_x, my_z // 2, half, head])

    rows = HEADS * ROWS
    smem = pl.BlockSpec(memory_space=pltpu.SMEM)
    vmem = pl.BlockSpec(memory_space=pltpu.VMEM)
    hbm = pl.BlockSpec(memory_space=pltpu.HBM)
    heads_out = pl.pallas_call(
        attention_kernel,
        name="attention",
        out_shape=(jax.ShapeDtypeStruct((2, PART, WIDE), jnp.bfloat16),) * NY,
        in_specs=[smem] + [vmem] * 9,
        out_specs=(vmem,) * NY,
        scratch_shapes=[
            pltpu.VMEM((BOTH, 2, rows, 256), f32),
            pltpu.VMEM((SINGLE, rows, 256), f32),
            pltpu.VMEM((4, rows, HD), jnp.bfloat16),
            pltpu.VMEM((4, rows, HD), f32),
            pltpu.VMEM((4, rows, HD), f32),
            pltpu.VMEM((4, rows, HD), f32),
            pltpu.VMEM((4, ROWS, WIDE), jnp.bfloat16),
        ],
        compiler_params=pltpu.CompilerParams(vmem_limit_bytes=24 << 20),
    )(scalars, q_own, q_far, kva, kvb, k_code, k_pos, wide(q_seg), wide(q_lim), wide(q_pos))

    *heads_out, weight = lax.optimization_barrier((*heads_out, weight))
    weights = [jnp.stack([out_weight, weight], 0)]

    heads_in = [heads_out[0]] + [swap_head(heads_out[k], k) for k in (1, 2, 3)]
    heads_in[3], weights[0] = lax.optimization_barrier((heads_in[3], weights[0]))
    part = [jnp.stack([v[t] for v in heads_in], 0) for t in range(2)]
    weights += [swap_head(weights[0], 2)]
    part_z, late, weights[0] = lax.optimization_barrier((gather_z(part[0]), part[1], weights[0]))
    weights_other = [from_seq(weights[0], flip_core=1)]

    right, left = from_seq(part_z, shift_x=1), from_seq(part_z, shift_x=3)
    late_z = gather_z(late)
    right, left, late_z = lax.optimization_barrier((right, left, late_z))
    early_x = [part_z, right, left, from_seq(right[:2], shift_x=1), from_seq(left[2:], shift_x=3)]
    right, left = from_seq(late_z, shift_x=1), from_seq(late_z, shift_x=3)
    early_x, right, left, weights[1] = lax.optimization_barrier((early_x, right, left, weights[1]))
    part_x = [early_x, [late_z, right, left, from_seq(right[:2], shift_x=1), from_seq(left[2:], shift_x=3)]]
    weights_other += [from_seq(weights[1], flip_core=1)]

    x_of = (my_x + four) & 3
    ends = (x_of & 1) ^ (head // 2)
    where = jnp.where(ends == phase, 0, 2) + x_of // 2
    z_of = my_z ^ four
    place = jnp.concatenate([2 * z_of + my_c, 2 * z_of + (1 - my_c)])
    spots = jnp.where(head < 2, place, 7 - place)
    piece = jax.ShapeDtypeStruct((2, 2 * NZ * PART, 512), jnp.bfloat16)
    pieces = []
    for t in range(2):
        mine, theirs = pl.pallas_call(
            project_kernel,
            name="project",
            out_shape=(piece, piece),
            in_specs=[smem] + [hbm] * 3 + [vmem] * 6,
            out_specs=(vmem, vmem),
            scratch_shapes=[
                pltpu.VMEM((NX, NZ, PART, NY * WIDE), jnp.bfloat16),
                pltpu.SemaphoreType.DMA((5 * NY,)),
            ],
            compiler_params=pltpu.CompilerParams(vmem_limit_bytes=24 << 20),
        )(where, *[off_chip(v) for v in part_x[t][:3]], *[on_chip(v) for v in part_x[t][3:]], *[on_chip(w) for w in weights + weights_other])
        got = lax.ppermute(theirs, "phase", [(0, 1), (1, 0)])
        for_other = (mine[1].astype(f32) + got[1].astype(f32)).astype(jnp.bfloat16)
        pieces += [mine, got, from_seq(for_other, flip_core=1)]
    return pl.pallas_call(
        place_kernel,
        name="place",
        out_shape=jax.ShapeDtypeStruct((8 * SPAN, 512), jnp.bfloat16),
        in_specs=[smem] + [vmem] * 6,
        out_specs=vmem,
        compiler_params=pltpu.CompilerParams(vmem_limit_bytes=16 << 20),
    )(spots, *pieces)


def solution(mesh):
    return jax.shard_map(
        per_device,
        mesh=mesh,
        in_specs=(
            P("seq", None, None, ("head", "phase")),
            P("seq", None, None, ("head", "phase")),
            P("seq", None, None, ("head", "phase")),
            P(("head", "phase"), "seq"),
            P(),
            P(),
        ),
        out_specs=P(("head", "phase"), "seq"),
        check_vma=False,
    )
```

```python
import math

import jax
import jax.numpy as jnp
from jax import lax
from jax.experimental import pallas as pl
from jax.experimental.pallas import tpu as pltpu
from jax.sharding import PartitionSpec as P

HD = 128
SEGS = 10
SPAN = 64
ROWS = 32
PART = 16
NX, NZ, NC = 4, 4, 2
NY = 4
HEADS = 8
WIDE = HEADS * HD
NEG = -1e30
HIDDEN = 1 << 20
BOTH = 8
SINGLE = 18


def places_of_seq(shift_x=0, flip_z=0, flip_core=0):
    pairs = []
    for x in range(NX):
        for z in range(NZ):
            for c in range(NC):
                src = (x * NZ + z) * NC + c
                dst = (((x - shift_x) % NX) * NZ + (z ^ flip_z)) * NC + (c ^ flip_core)
                pairs.append((src, dst))
    return pairs


def from_seq(a, **kw):
    return lax.ppermute(a, "seq", places_of_seq(**kw))


def swap_head(a, k):
    return lax.ppermute(a, "head", [(y, y ^ k) for y in range(NY)])


def gather_z(a):
    return jnp.stack([a] + [from_seq(a, flip_z=k) for k in (1, 2, 3)], 0)


def over_x(a):
    return [a] + [from_seq(a, shift_x=k) for k in (1, 2, 3)]


def on_chip(a):
    return pltpu.with_memory_space_constraint(a, pltpu.VMEM)


def off_chip(a):
    return pltpu.with_memory_space_constraint(a, pltpu.HBM)


def attention_kernel(
    sc, q_own, q_far, kva, kvb, kcode, kpos, qseg, qlim, qpos, *rest
):
    outs, (both, single, qs, mx, acc, tot, done) = rest[:NY], rest[NY:]
    tile_lo, tile_hi, my_x, my_zh, half, head = sc[0], sc[1], sc[2], sc[3], sc[4], sc[5]
    rows = HEADS * ROWS
    start = pl.multiple_of(half * ROWS, ROWS)

    for m in range(2):
        near = q_own[m, pl.ds(start, ROWS), :]
        far = q_far[m, pl.ds(start, ROWS), :]
        low = jnp.where(half == 0, near, far)
        high = jnp.where(half == 0, far, near)
        for h in range(HEADS):
            cols = slice(h * HD, (h + 1) * HD)
            qs[3 * m, h * ROWS:(h + 1) * ROWS, :] = low[:, cols]
            qs[1 + m, h * ROWS:(h + 1) * ROWS, :] = high[:, cols]
    mx[...] = jnp.full_like(mx, NEG)
    acc[...] = jnp.zeros_like(acc)
    tot[...] = jnp.zeros_like(tot)

    def tile_of(t):
        pair, u = t // 9, t % 9
        early = u <= (tile_lo if pair == 0 else tile_hi)
        group = jnp.where(early, pair, 3 - pair)
        mk = jnp.where(early, 0, 1)
        g = jnp.where(early, u, u - 1)
        g_rel = (((g >> 1) - my_x) & 3) * 2 + ((g & 1) ^ my_zh)
        return group, mk, g_rel

    def rows_of(kv, mk, g):
        return jnp.concatenate(
            [kva[2 * g, kv, mk], kva[2 * g + 1, kv, mk], kvb[2 * g, kv, mk], kvb[2 * g + 1, kv, mk]], 0
        )

    def masked(s, group, mk, g):
        code = kcode[(group * 2 + mk) * 8 + g]
        ok = ((code == qseg[group]) | (code <= qlim[group])) & (kpos[mk * 8 + g] <= qpos[group])
        return jnp.where(ok[None], s.reshape(HEADS, ROWS, 256), NEG).reshape(rows, 256)

    def dot_keys(q, keys):
        return lax.dot_general(q, keys, (((1,), (1,)), ((), ())), preferred_element_type=jnp.float32)

    for t in range(BOTH):
        s = dot_keys(qs[2:4].reshape(2 * rows, HD), rows_of(0, 0, t))
        for i in range(2):
            part = masked(s[i * rows:(i + 1) * rows], 2 + i, 0, t)
            both[t, i] = part
            mx[2 + i] = jnp.maximum(mx[2 + i], jnp.maximum(part[:, :HD], part[:, HD:]))
    for t in range(SINGLE):
        group, mk, g = tile_of(t)
        s = masked(dot_keys(qs[group], rows_of(0, mk, g)), group, mk, g)
        single[t] = s
        mx[group] = jnp.maximum(mx[group], jnp.maximum(s[:, :HD], s[:, HD:]))
    for i in range(4):
        mx[i] = jnp.broadcast_to(jnp.max(mx[i], axis=1, keepdims=True), (rows, HD))
    factor = math.log2(math.e) / math.sqrt(HD)

    def weigh(s, peak):
        return jnp.exp2((s - jnp.concatenate([peak, peak], 1)) * factor)

    for t in range(BOTH):
        parts = []
        for i in range(2):
            w = weigh(both[t, i], mx[2 + i])
            tot[2 + i] += w[:, :HD] + w[:, HD:]
            parts.append(w.astype(jnp.bfloat16))
        mixed = jnp.dot(jnp.concatenate(parts, 0), rows_of(1, 0, t), preferred_element_type=jnp.float32)
        for i in range(2):
            acc[2 + i] += mixed[i * rows:(i + 1) * rows]
    for t in range(SINGLE):
        group, mk, g = tile_of(t)
        w = weigh(single[t], mx[group])
        tot[group] += w[:, :HD] + w[:, HD:]
        acc[group] += jnp.dot(w.astype(jnp.bfloat16), rows_of(1, mk, g), preferred_element_type=jnp.float32)
    for i in range(4):
        total = jnp.sum(tot[i], axis=1, keepdims=True)
        out = (acc[i] / total).astype(jnp.bfloat16)
        for h in range(HEADS):
            done[i, :, h * HD:(h + 1) * HD] = out[h * ROWS:(h + 1) * ROWS]
    for k in range(NY):
        outs[k][...] = done[head ^ k].reshape(2, PART, WIDE)


def project_kernel(where, *refs):
    a_in, w_in, (mine, theirs), (a_all, w_all, sems, w_sems) = refs[:5], refs[5:9], refs[9:11], refs[11:]
    rows, weights = [], {}
    for k in range(NY):
        for j, slot in enumerate((0, 1, 3, 2, 2)):
            to = a_all.at[k, where[slot]]
            if slot == 2:
                to = to.at[pl.ds(2 * (j - 3), 2)]
            copy = pltpu.make_async_copy(a_in[j].at[:, k], to, sems.at[5 * k + j])
            copy.start()
            rows.append(copy)
        if k > 0:
            i = (2, 1, 3)[k - 1]
            weights[i] = pltpu.make_async_copy(w_in[i], w_all.at[i - 1], w_sems.at[i - 1])
            weights[i].start()
    count = NZ * PART
    c = [None, None]
    for pair in range(2):
        for side in range(2):
            i = 2 * side + pair
            if i:
                weights[i].wait()
            for k in (2 * pair, 2 * pair + 1):
                if side == 0:
                    for copy in rows[5 * k:5 * k + 5]:
                        copy.wait()
                w = w_all[i - 1, k % 2] if i else w_in[0][k % 2]
                part = jnp.dot(a_all[k].reshape(NX * count, WIDE), w, preferred_element_type=jnp.float32)
                c[side] = part if c[side] is None else c[side] + part
    for side in range(2):
        out = c[side].astype(jnp.bfloat16)
        mine[side] = out[:2 * count]
        theirs[side] = out[2 * count:]


def place_kernel(spots, *refs):
    o_ref = refs[-1]
    for t in range(2):
        near, got, other = refs[3 * t:3 * t + 3]
        own = (near[0].astype(jnp.float32) + got[0].astype(jnp.float32)).astype(jnp.bfloat16)
        theirs = other[...]
        for h in range(2):
            for k in range(NZ):
                part = slice((h * NZ + k) * PART, (h * NZ + k + 1) * PART)
                inside = h * ROWS + t * PART
                row = pl.multiple_of(spots[k] * SPAN + inside, PART)
                o_ref[pl.ds(row, PART), :] = own[part]
                row = pl.multiple_of(spots[NZ + k] * SPAN + inside, PART)
                o_ref[pl.ds(row, PART), :] = theirs[part]


def per_device(queries, keys, values, out_weight, block_vis, seg_lengths):
    seq = lax.axis_index("seq")
    phase = lax.axis_index("phase")
    head = lax.axis_index("head")
    my_x, my_z, my_c = seq // 8, (seq // 2) % 4, seq % 2
    f32 = jnp.float32

    q_own = queries.reshape(2, SPAN, WIDE)
    q_far = from_seq(q_own, shift_x=2)
    half = my_x // 2

    kv = jnp.stack([keys.reshape(2, SPAN, HD), values.reshape(2, SPAN, HD)], 0)
    kv_x = over_x(gather_z(kv))
    kv_x, q_far = lax.optimization_barrier((kv_x, q_far))
    kva = jnp.stack(kv_x, 0).reshape(NX * NZ, 2, 2, SPAN, HD)
    kvb = from_seq(kva, flip_core=1)
    kva, kvb, weight = lax.optimization_barrier((kva, kvb, swap_head(out_weight, 1)))

    tri = jnp.arange(SEGS)[None, :] < jnp.arange(SEGS)[:, None]
    starts = jnp.sum(jnp.where(tri, seg_lengths[None, :], 0), axis=1)

    def segment(pos):
        return jnp.sum((starts[1:] <= pos[..., None]).astype(jnp.int32), axis=-1)

    two = jnp.arange(2, dtype=jnp.int32)
    four = jnp.arange(4, dtype=jnp.int32)
    low = seq & 15
    high = low + 16
    q_span = jnp.where(four == 0, low, jnp.where(four == 1, high, jnp.where(four == 2, 63 - high, 63 - low)))
    q_pos = q_span[:, None] * SPAN + half * ROWS + jnp.arange(ROWS, dtype=jnp.int32)
    q_seg = segment(q_pos)
    q_lim = jnp.where(q_seg == SEGS - 1, SEGS - 1, 0)
    g = jnp.arange(8, dtype=jnp.int32)
    key_x = (my_x + g // 2) & 3
    key_z = my_z ^ ((g % 2)[:, None] * 2 + two)
    key_s = key_x[:, None, None] * 8 + key_z[:, None, :] * 2 + (my_c ^ two)[None, :, None]
    key_span = jnp.where(two[:, None, None, None] == 0, key_s[None], 63 - key_s[None])
    key_span = key_span.reshape(2, 8, 4)
    k_pos = (key_span[..., None] * SPAN + jnp.arange(SPAN, dtype=jnp.int32)).reshape(2, 8, 256)
    k_seg = segment(k_pos)
    blocks = jnp.arange(block_vis.shape[0], dtype=jnp.int32)
    vis_rows = jnp.sum(
        jnp.where(((q_span // 2)[:, None] == blocks)[..., None], block_vis[None], 0), axis=1
    )
    seen = jnp.sum(
        jnp.where((key_span // 2)[None, ..., None] == blocks, vis_rows[:, None, None, None, :], 0),
        axis=-1,
    )
    seen = jnp.repeat(seen, SPAN, axis=-1).reshape(4, 2, 8, 256)
    k_code = jnp.where(seen == 1, k_seg[None], HIDDEN).reshape(64, 1, 256)
    k_pos = k_pos.reshape(16, 1, 256)
    wide = lambda v: jnp.broadcast_to(v[..., None], (4, ROWS, 256))
    scalars = jnp.stack([low // 4, high // 4, my_x, my_z // 2, half, head])

    rows = HEADS * ROWS
    smem = pl.BlockSpec(memory_space=pltpu.SMEM)
    vmem = pl.BlockSpec(memory_space=pltpu.VMEM)
    hbm = pl.BlockSpec(memory_space=pltpu.HBM)
    heads_out = pl.pallas_call(
        attention_kernel,
        name="attention",
        out_shape=(jax.ShapeDtypeStruct((2, PART, WIDE), jnp.bfloat16),) * NY,
        in_specs=[smem] + [vmem] * 9,
        out_specs=(vmem,) * NY,
        scratch_shapes=[
            pltpu.VMEM((BOTH, 2, rows, 256), f32),
            pltpu.VMEM((SINGLE, rows, 256), f32),
            pltpu.VMEM((4, rows, HD), jnp.bfloat16),
            pltpu.VMEM((4, rows, HD), f32),
            pltpu.VMEM((4, rows, HD), f32),
            pltpu.VMEM((4, rows, HD), f32),
            pltpu.VMEM((4, ROWS, WIDE), jnp.bfloat16),
        ],
        compiler_params=pltpu.CompilerParams(vmem_limit_bytes=24 << 20),
    )(scalars, q_own, q_far, kva, kvb, k_code, k_pos, wide(q_seg), wide(q_lim), wide(q_pos))

    *heads_out, weight = lax.optimization_barrier((*heads_out, weight))
    weights = [jnp.stack([out_weight, weight], 0)]

    heads_in = [heads_out[0]] + [swap_head(heads_out[k], k) for k in (1, 2, 3)]
    heads_in[3], weights[0] = lax.optimization_barrier((heads_in[3], weights[0]))
    part = [jnp.stack([v[t] for v in heads_in], 0) for t in range(2)]
    weights += [swap_head(weights[0], 2)]
    part_z, late, weights[0] = lax.optimization_barrier((gather_z(part[0]), part[1], weights[0]))
    weights_other = [from_seq(weights[0], flip_core=1)]

    right, left = from_seq(part_z, shift_x=1), from_seq(part_z, shift_x=3)
    late_z = gather_z(late)
    right, left, late_z = lax.optimization_barrier((right, left, late_z))
    early_x = [part_z, right, left, from_seq(right[:2], shift_x=1), from_seq(left[2:], shift_x=3)]
    right, left = from_seq(late_z, shift_x=1), from_seq(late_z, shift_x=3)
    early_x, right, left, weights[1] = lax.optimization_barrier((early_x, right, left, weights[1]))
    part_x = [early_x, [late_z, right, left, from_seq(right[:2], shift_x=1), from_seq(left[2:], shift_x=3)]]
    weights_other += [from_seq(weights[1], flip_core=1)]

    x_of = (my_x + four) & 3
    ends = (x_of & 1) ^ (head // 2)
    where = jnp.where(ends == phase, 0, 2) + x_of // 2
    z_of = my_z ^ four
    place = jnp.concatenate([2 * z_of + my_c, 2 * z_of + (1 - my_c)])
    spots = jnp.where(head < 2, place, 7 - place)
    piece = jax.ShapeDtypeStruct((2, 2 * NZ * PART, 512), jnp.bfloat16)
    pieces = []
    for t in range(2):
        mine, theirs = pl.pallas_call(
            project_kernel,
            name="project",
            out_shape=(piece, piece),
            in_specs=[smem] + [hbm] * 3 + [vmem] * 3 + [hbm] * 3,
            out_specs=(vmem, vmem),
            scratch_shapes=[
                pltpu.VMEM((NY, NX, NZ, PART, WIDE), jnp.bfloat16),
                pltpu.VMEM((3, 2, WIDE, 512), jnp.bfloat16),
                pltpu.SemaphoreType.DMA((5 * NY,)),
                pltpu.SemaphoreType.DMA((3,)),
            ],
            compiler_params=pltpu.CompilerParams(vmem_limit_bytes=24 << 20),
        )(where, *[off_chip(v) for v in part_x[t][:3]], *[on_chip(v) for v in part_x[t][3:]], on_chip(weights[0]), *[off_chip(w) for w in (weights[1], *weights_other)])
        got = lax.ppermute(theirs, "phase", [(0, 1), (1, 0)])
        for_other = (mine[1].astype(f32) + got[1].astype(f32)).astype(jnp.bfloat16)
        pieces += [mine, got, from_seq(for_other, flip_core=1)]
    return pl.pallas_call(
        place_kernel,
        name="place",
        out_shape=jax.ShapeDtypeStruct((8 * SPAN, 512), jnp.bfloat16),
        in_specs=[smem] + [vmem] * 6,
        out_specs=vmem,
        compiler_params=pltpu.CompilerParams(vmem_limit_bytes=16 << 20),
    )(spots, *pieces)


def solution(mesh):
    return jax.shard_map(
        per_device,
        mesh=mesh,
        in_specs=(
            P("seq", None, None, ("head", "phase")),
            P("seq", None, None, ("head", "phase")),
            P("seq", None, None, ("head", "phase")),
            P(("head", "phase"), "seq"),
            P(),
            P(),
        ),
        out_specs=P(("head", "phase"), "seq"),
        check_vma=False,
    )
```

```python
import math

import jax
import jax.numpy as jnp
from jax import lax
from jax.experimental import pallas as pl
from jax.experimental.pallas import tpu as pltpu
from jax.sharding import PartitionSpec as P

HD = 128
SEGS = 10
SPAN = 64
ROWS = 32
PART = 16
NX, NZ, NC = 4, 4, 2
NY = 4
HEADS = 8
WIDE = HEADS * HD
NEG = -1e30
HIDDEN = 1 << 20
BOTH = 8
SINGLE = 18


def places_of_seq(shift_x=0, flip_z=0, flip_core=0):
    pairs = []
    for x in range(NX):
        for z in range(NZ):
            for c in range(NC):
                src = (x * NZ + z) * NC + c
                dst = (((x - shift_x) % NX) * NZ + (z ^ flip_z)) * NC + (c ^ flip_core)
                pairs.append((src, dst))
    return pairs


def from_seq(a, **kw):
    return lax.ppermute(a, "seq", places_of_seq(**kw))


def swap_head(a, k):
    return lax.ppermute(a, "head", [(y, y ^ k) for y in range(NY)])


def gather_z(a):
    return jnp.stack([a] + [from_seq(a, flip_z=k) for k in (1, 2, 3)], 0)


def over_x(a):
    return [a] + [from_seq(a, shift_x=k) for k in (1, 2, 3)]


def on_chip(a):
    return pltpu.with_memory_space_constraint(a, pltpu.VMEM)


def off_chip(a):
    return pltpu.with_memory_space_constraint(a, pltpu.HBM)


def attention_kernel(
    sc, q_own, q_far, kva, kvb, kcode, kpos, qseg, qlim, qpos, *rest
):
    outs, (both, single, qs, mx, acc, tot, done) = rest[:NY], rest[NY:]
    tile_lo, tile_hi, my_x, my_zh, half, head = sc[0], sc[1], sc[2], sc[3], sc[4], sc[5]
    rows = HEADS * ROWS
    start = pl.multiple_of(half * ROWS, ROWS)

    for m in range(2):
        near = q_own[m, pl.ds(start, ROWS), :]
        far = q_far[m, pl.ds(start, ROWS), :]
        low = jnp.where(half == 0, near, far)
        high = jnp.where(half == 0, far, near)
        for h in range(HEADS):
            cols = slice(h * HD, (h + 1) * HD)
            qs[3 * m, h * ROWS:(h + 1) * ROWS, :] = low[:, cols]
            qs[1 + m, h * ROWS:(h + 1) * ROWS, :] = high[:, cols]
    mx[...] = jnp.full_like(mx, NEG)
    acc[...] = jnp.zeros_like(acc)
    tot[...] = jnp.zeros_like(tot)

    def tile_of(t):
        pair, u = t // 9, t % 9
        early = u <= (tile_lo if pair == 0 else tile_hi)
        group = jnp.where(early, pair, 3 - pair)
        mk = jnp.where(early, 0, 1)
        g = jnp.where(early, u, u - 1)
        g_rel = (((g >> 1) - my_x) & 3) * 2 + ((g & 1) ^ my_zh)
        return group, mk, g_rel

    def rows_of(kv, mk, g):
        return jnp.concatenate(
            [kva[2 * g, kv, mk], kva[2 * g + 1, kv, mk], kvb[2 * g, kv, mk], kvb[2 * g + 1, kv, mk]], 0
        )

    def masked(s, group, mk, g):
        code = kcode[(group * 2 + mk) * 8 + g]
        ok = ((code == qseg[group]) | (code <= qlim[group])) & (kpos[mk * 8 + g] <= qpos[group])
        return jnp.where(ok[None], s.reshape(HEADS, ROWS, 256), NEG).reshape(rows, 256)

    def dot_keys(q, keys):
        return lax.dot_general(q, keys, (((1,), (1,)), ((), ())), preferred_element_type=jnp.float32)

    for t in range(BOTH):
        s = dot_keys(qs[2:4].reshape(2 * rows, HD), rows_of(0, 0, t))
        for i in range(2):
            part = masked(s[i * rows:(i + 1) * rows], 2 + i, 0, t)
            both[t, i] = part
            mx[2 + i] = jnp.maximum(mx[2 + i], jnp.maximum(part[:, :HD], part[:, HD:]))
    for t in range(SINGLE):
        group, mk, g = tile_of(t)
        s = masked(dot_keys(qs[group], rows_of(0, mk, g)), group, mk, g)
        single[t] = s
        mx[group] = jnp.maximum(mx[group], jnp.maximum(s[:, :HD], s[:, HD:]))
    for i in range(4):
        mx[i] = jnp.broadcast_to(jnp.max(mx[i], axis=1, keepdims=True), (rows, HD))
    factor = math.log2(math.e) / math.sqrt(HD)

    def weigh(s, peak):
        return jnp.exp2((s - jnp.concatenate([peak, peak], 1)) * factor)

    for t in range(BOTH):
        parts = []
        for i in range(2):
            w = weigh(both[t, i], mx[2 + i])
            tot[2 + i] += w[:, :HD] + w[:, HD:]
            parts.append(w.astype(jnp.bfloat16))
        mixed = jnp.dot(jnp.concatenate(parts, 0), rows_of(1, 0, t), preferred_element_type=jnp.float32)
        for i in range(2):
            acc[2 + i] += mixed[i * rows:(i + 1) * rows]
    for t in range(SINGLE):
        group, mk, g = tile_of(t)
        w = weigh(single[t], mx[group])
        tot[group] += w[:, :HD] + w[:, HD:]
        acc[group] += jnp.dot(w.astype(jnp.bfloat16), rows_of(1, mk, g), preferred_element_type=jnp.float32)
    for i in range(4):
        total = jnp.sum(tot[i], axis=1, keepdims=True)
        out = (acc[i] / total).astype(jnp.bfloat16)
        for h in range(HEADS):
            done[i, :, h * HD:(h + 1) * HD] = out[h * ROWS:(h + 1) * ROWS]
    for k in range(NY):
        outs[k][...] = done[head ^ k].reshape(2, PART, WIDE)


def project_kernel(where, *refs):
    a_in, w_in, (mine, theirs), (a_all, w_all, sems, w_sems) = refs[:5], refs[5:9], refs[9:11], refs[11:]
    rows, weights = [], {}
    for k in range(NY):
        for j, slot in enumerate((0, 1, 3, 2, 2)):
            to = a_all.at[k, where[slot]]
            if slot == 2:
                to = to.at[pl.ds(2 * (j - 3), 2)]
            copy = pltpu.make_async_copy(a_in[j].at[:, k], to, sems.at[5 * k + j])
            copy.start()
            rows.append(copy)
        if k > 0:
            i = (2, 1, 3)[k - 1]
            weights[i] = pltpu.make_async_copy(w_in[i], w_all.at[i - 1], w_sems.at[i - 1])
            weights[i].start()
    count = NZ * PART
    c = [None, None]
    for pair in range(2):
        for side in range(2):
            i = 2 * side + pair
            if i:
                weights[i].wait()
            for k in (2 * pair, 2 * pair + 1):
                if side == 0:
                    for copy in rows[5 * k:5 * k + 5]:
                        copy.wait()
                w = w_all[i - 1, k % 2] if i else w_in[0][k % 2]
                part = jnp.dot(a_all[k].reshape(NX * count, WIDE), w, preferred_element_type=jnp.float32)
                c[side] = part if c[side] is None else c[side] + part
    for side in range(2):
        out = c[side].astype(jnp.bfloat16)
        mine[side] = out[:2 * count]
        theirs[side] = out[2 * count:]


def place_kernel(spots, *refs):
    o_ref = refs[-1]
    for t in range(2):
        near, got, other = refs[3 * t:3 * t + 3]
        own = (near[0].astype(jnp.float32) + got[0].astype(jnp.float32)).astype(jnp.bfloat16)
        theirs = other[...]
        for h in range(2):
            for k in range(NZ):
                part = slice((h * NZ + k) * PART, (h * NZ + k + 1) * PART)
                inside = h * ROWS + t * PART
                row = pl.multiple_of(spots[k] * SPAN + inside, PART)
                o_ref[pl.ds(row, PART), :] = own[part]
                row = pl.multiple_of(spots[NZ + k] * SPAN + inside, PART)
                o_ref[pl.ds(row, PART), :] = theirs[part]


def per_device(queries, keys, values, out_weight, block_vis, seg_lengths):
    seq = lax.axis_index("seq")
    phase = lax.axis_index("phase")
    head = lax.axis_index("head")
    my_x, my_z, my_c = seq // 8, (seq // 2) % 4, seq % 2
    f32 = jnp.float32

    q_own = queries.reshape(2, SPAN, WIDE)
    q_far = from_seq(q_own, shift_x=2)
    half = my_x // 2

    kv = jnp.stack([keys.reshape(2, SPAN, HD), values.reshape(2, SPAN, HD)], 0)
    kv_x = over_x(gather_z(kv))
    kv_x, q_far = lax.optimization_barrier((kv_x, q_far))
    kva = jnp.stack(kv_x, 0).reshape(NX * NZ, 2, 2, SPAN, HD)
    kvb = from_seq(kva, flip_core=1)
    kva, kvb, weight = lax.optimization_barrier((kva, kvb, swap_head(out_weight, 1)))

    tri = jnp.arange(SEGS)[None, :] < jnp.arange(SEGS)[:, None]
    starts = jnp.sum(jnp.where(tri, seg_lengths[None, :], 0), axis=1)

    def segment(pos):
        return jnp.sum((starts[1:] <= pos[..., None]).astype(jnp.int32), axis=-1)

    two = jnp.arange(2, dtype=jnp.int32)
    four = jnp.arange(4, dtype=jnp.int32)
    low = seq & 15
    high = low + 16
    q_span = jnp.where(four == 0, low, jnp.where(four == 1, high, jnp.where(four == 2, 63 - high, 63 - low)))
    q_pos = q_span[:, None] * SPAN + half * ROWS + jnp.arange(ROWS, dtype=jnp.int32)
    q_seg = segment(q_pos)
    q_lim = jnp.where(q_seg == SEGS - 1, SEGS - 1, 0)
    g = jnp.arange(8, dtype=jnp.int32)
    key_x = (my_x + g // 2) & 3
    key_z = my_z ^ ((g % 2)[:, None] * 2 + two)
    key_s = key_x[:, None, None] * 8 + key_z[:, None, :] * 2 + (my_c ^ two)[None, :, None]
    key_span = jnp.where(two[:, None, None, None] == 0, key_s[None], 63 - key_s[None])
    key_span = key_span.reshape(2, 8, 4)
    k_pos = (key_span[..., None] * SPAN + jnp.arange(SPAN, dtype=jnp.int32)).reshape(2, 8, 256)
    k_seg = segment(k_pos)
    blocks = jnp.arange(block_vis.shape[0], dtype=jnp.int32)
    vis_rows = jnp.sum(
        jnp.where(((q_span // 2)[:, None] == blocks)[..., None], block_vis[None], 0), axis=1
    )
    seen = jnp.sum(
        jnp.where((key_span // 2)[None, ..., None] == blocks, vis_rows[:, None, None, None, :], 0),
        axis=-1,
    )
    seen = jnp.repeat(seen, SPAN, axis=-1).reshape(4, 2, 8, 256)
    k_code = jnp.where(seen == 1, k_seg[None], HIDDEN).reshape(64, 1, 256)
    k_pos = k_pos.reshape(16, 1, 256)
    wide = lambda v: jnp.broadcast_to(v[..., None], (4, ROWS, 256))
    scalars = jnp.stack([low // 4, high // 4, my_x, my_z // 2, half, head])

    rows = HEADS * ROWS
    smem = pl.BlockSpec(memory_space=pltpu.SMEM)
    vmem = pl.BlockSpec(memory_space=pltpu.VMEM)
    hbm = pl.BlockSpec(memory_space=pltpu.HBM)
    heads_out = pl.pallas_call(
        attention_kernel,
        name="attention",
        out_shape=(jax.ShapeDtypeStruct((2, PART, WIDE), jnp.bfloat16),) * NY,
        in_specs=[smem] + [vmem] * 9,
        out_specs=(vmem,) * NY,
        scratch_shapes=[
            pltpu.VMEM((BOTH, 2, rows, 256), f32),
            pltpu.VMEM((SINGLE, rows, 256), f32),
            pltpu.VMEM((4, rows, HD), jnp.bfloat16),
            pltpu.VMEM((4, rows, HD), f32),
            pltpu.VMEM((4, rows, HD), f32),
            pltpu.VMEM((4, rows, HD), f32),
            pltpu.VMEM((4, ROWS, WIDE), jnp.bfloat16),
        ],
        compiler_params=pltpu.CompilerParams(vmem_limit_bytes=24 << 20),
    )(scalars, q_own, q_far, kva, kvb, k_code, k_pos, wide(q_seg), wide(q_lim), wide(q_pos))

    *heads_out, weight = lax.optimization_barrier((*heads_out, weight))
    weights = [jnp.stack([out_weight, weight], 0)]

    heads_in = [heads_out[0]] + [swap_head(heads_out[k], k) for k in (1, 2, 3)]
    heads_in[3], weights[0] = lax.optimization_barrier((heads_in[3], weights[0]))
    part = [jnp.stack([v[t] for v in heads_in], 0) for t in range(2)]
    weights += [swap_head(weights[0], 2)]
    part[0], weights[0] = lax.optimization_barrier((part[0], weights[0]))
    weights_other = [from_seq(weights[0], flip_core=1)]
    part_z, late, weights_other[0] = lax.optimization_barrier((gather_z(part[0]), part[1], weights_other[0]))

    right, left = from_seq(part_z, shift_x=1), from_seq(part_z, shift_x=3)
    late_z = gather_z(late)
    right, left, late_z = lax.optimization_barrier((right, left, late_z))
    early_x = [part_z, right, left, from_seq(right[:2], shift_x=1), from_seq(left[2:], shift_x=3)]
    right, left = from_seq(late_z, shift_x=1), from_seq(late_z, shift_x=3)
    early_x, right, left, weights[1] = lax.optimization_barrier((early_x, right, left, weights[1]))
    part_x = [early_x, [late_z, right, left, from_seq(right[:2], shift_x=1), from_seq(left[2:], shift_x=3)]]
    weights_other += [from_seq(weights[1], flip_core=1)]

    x_of = (my_x + four) & 3
    ends = (x_of & 1) ^ (head // 2)
    where = jnp.where(ends == phase, 0, 2) + x_of // 2
    z_of = my_z ^ four
    place = jnp.concatenate([2 * z_of + my_c, 2 * z_of + (1 - my_c)])
    spots = jnp.where(head < 2, place, 7 - place)
    piece = jax.ShapeDtypeStruct((2, 2 * NZ * PART, 512), jnp.bfloat16)
    pieces = []
    for t in range(2):
        mine, theirs = pl.pallas_call(
            project_kernel,
            name="project",
            out_shape=(piece, piece),
            in_specs=[smem] + [hbm] * 3 + [vmem] * 3 + [hbm] * 3,
            out_specs=(vmem, vmem),
            scratch_shapes=[
                pltpu.VMEM((NY, NX, NZ, PART, WIDE), jnp.bfloat16),
                pltpu.VMEM((3, 2, WIDE, 512), jnp.bfloat16),
                pltpu.SemaphoreType.DMA((5 * NY,)),
                pltpu.SemaphoreType.DMA((3,)),
            ],
            compiler_params=pltpu.CompilerParams(vmem_limit_bytes=24 << 20),
        )(where, *[off_chip(v) for v in part_x[t][:3]], *[on_chip(v) for v in part_x[t][3:]], on_chip(weights[0]), *[off_chip(w) for w in (weights[1], *weights_other)])
        got = lax.ppermute(theirs, "phase", [(0, 1), (1, 0)])
        for_other = (mine[1].astype(f32) + got[1].astype(f32)).astype(jnp.bfloat16)
        pieces += [mine, got, from_seq(for_other, flip_core=1)]
    return pl.pallas_call(
        place_kernel,
        name="place",
        out_shape=jax.ShapeDtypeStruct((8 * SPAN, 512), jnp.bfloat16),
        in_specs=[smem] + [vmem] * 6,
        out_specs=vmem,
        compiler_params=pltpu.CompilerParams(vmem_limit_bytes=16 << 20),
    )(spots, *pieces)


def solution(mesh):
    return jax.shard_map(
        per_device,
        mesh=mesh,
        in_specs=(
            P("seq", None, None, ("head", "phase")),
            P("seq", None, None, ("head", "phase")),
            P("seq", None, None, ("head", "phase")),
            P(("head", "phase"), "seq"),
            P(),
            P(),
        ),
        out_specs=P(("head", "phase"), "seq"),
        check_vma=False,
    )
```
